256 devices in a mesh: gx: 16 (over z, core), gy: 16 (over y, x).
Axes of the slice: x: 4, y: 4, z: 8, core: 2. Of those that a mesh axis runs over, the one named last changes fastest.
Arguments:
- adjoint_field: float32 [3, 16, 16, 64, 512], P(None, 'gx', 'gy'), may hold values from -12 to 27
- velocity: bfloat16 [3, 16, 16, 64, 512], P(None, 'gx', 'gy'), may hold values from -1.1953125 to 1.1953125
- diffusivity: float32 [3, 16, 16, 64, 512], P(None, 'gx', 'gy'), may hold values from 0.3 to 3
- jacobian: float32 [16, 16, 64, 512], P('gx', 'gy'), may hold values from 0.5 to 2
- element_slot: int32 [16, 16, 64], P('gx', 'gy'), may hold values from 0 to 63, each once within a row
Outputs:
- adjoint_prev: float32 [3, 16, 16, 64, 512], P(None, 'gx', 'gy')
The draws below stay inside these ranges and needn't reach their ends.
Inputs may be any that keep to these rules, and one draw needn't show every extreme that they name: Each partition's row of element_slot is a permutation of 0 to 63.
All inputs are finite; a program needn't handle non-finite values.
Results may differ from the reference program's by a relative error of at most 0.0003.
Values sent between devices are 32-bit elements; how exact they have to be, the bound alone decides.
No kernel may reach another device: no remote copies, remote signals or barrier semaphores. Data moves between devices by JAX's collectives and lax.ppermute only.
A program may use at most 64 MiB of HBM per device.

```python
import math
import jax
import jax.numpy as jnp
import numpy as np
from jax import lax

EX = 2
EY = 2
EZ = 16
ITERS = 4
E_DEV = 64
PARTS_X = 16
PARTS_Y = 16


def draw_adjoint_field(key, part):
    shape = (3, PARTS_X, PARTS_Y, E_DEV, 512)
    rough = jax.random.truncated_normal(key, -4.0, 4.0, shape, jnp.float32)
    along_x = jnp.exp(jnp.linspace(0.0, math.log(3.0), PARTS_X))
    scaling = jnp.broadcast_to(along_x[None, :, None, None, None], shape)
    return rough * scaling


def block_levels(key, extent, shards, least, top_value):
    gain = 1.0
    for axis_at, shards_of in shards:
        steps = jax.random.uniform(jax.random.fold_in(jax.random.fold_in(key, 6), axis_at), (shards_of,), jnp.float32, least / len(shards), top_value / len(shards))
        gain = gain * jnp.repeat(jnp.exp(steps), extent[axis_at] // shards_of).reshape((-1,) + (1,) * (len(extent) - 1 - axis_at))
    return gain


def scatter_about(rng, shape, scale, most, split=(), held_as=jnp.bfloat16):
    entries = scale * jax.random.normal(rng, shape, jnp.float32)
    if split:
        entries = entries * block_levels(rng, shape, split, -0.22, 0.18)
    return jnp.clip(entries, -most, most).astype(held_as)


def setup_inputs(seed: int = 0) -> dict:
    streams_of = jax.random.split(jax.random.key(seed), 6)
    adjoint_field = draw_adjoint_field(jax.random.fold_in(streams_of[5], 71), 0)
    velocity = scatter_about(streams_of[1], (3, PARTS_X, PARTS_Y, E_DEV, 512), 0.2, 1.1953125, ((1, 16), (2, 16)))
    diffusivity = jnp.clip(jnp.exp(math.log(3.0) - 2.3025851 * jax.random.uniform(streams_of[2], (3, PARTS_X, PARTS_Y, E_DEV, 512), jnp.float32) ** block_levels(streams_of[2], (3, PARTS_X, PARTS_Y, E_DEV, 512), ((1, 16), (2, 16)), -0.2, 0.2)), 0.3, 3.0)
    jacobian = jnp.clip(jnp.exp(math.log(2.0) - 1.3862944 * jax.random.uniform(streams_of[3], (PARTS_X, PARTS_Y, E_DEV, 512), jnp.float32) ** block_levels(streams_of[3], (PARTS_X, PARTS_Y, E_DEV, 512), ((0, 16), (1, 16)), -0.2, 0.2)), 0.5, 2.0)
    element_slot = jax.vmap(lambda own: jax.random.permutation(own, E_DEV))(jax.random.split(streams_of[4], PARTS_X * PARTS_Y)).reshape((PARTS_X, PARTS_Y, E_DEV)).astype(jnp.int32)
    return dict(adjoint_field=adjoint_field, velocity=velocity, diffusivity=diffusivity, jacobian=jacobian, element_slot=element_slot)


time_step = 0.25


def legendre_seven(points):
    previous = points * 0.0 + 1.0
    current = points
    for degree in range(1, 7):
        following = ((2 * degree + 1) * points * current - degree * previous) / (degree + 1)
        previous = current
        current = following
    return current


def gll_tables():
    poly_order = 7
    points = np.array([-1.0, -0.8717401485096066, -0.5917001814331423, -0.2092992179024789,
                       0.2092992179024789, 0.5917001814331423, 0.8717401485096066, 1.0])
    end_values = legendre_seven(points)
    weights = 2.0 / (poly_order * (poly_order + 1) * end_values ** 2)
    spread = points[:, None] - points[None, :]
    identity = np.eye(poly_order + 1)
    diff_table = end_values[:, None] / (end_values[None, :] * (spread + identity))
    diff_table = diff_table * (1.0 - identity)
    corners = np.zeros(poly_order + 1)
    corners[0] = -poly_order * (poly_order + 1) / 4.0
    corners[-1] = poly_order * (poly_order + 1) / 4.0
    diff_table = diff_table + identity * corners[None, :]
    return weights.astype(np.float32), diff_table.astype(np.float32)


def weight_outer(weights):
    return weights[:, None, None] * weights[None, :, None] * weights[None, None, :]


def fold_pair(values_in, position):
    moved = jnp.moveaxis(values_in, (position, position + 1), (-2, -1))
    leading = moved.shape[:-2]
    number = moved.shape[-2]
    body_part = moved[..., :7].reshape(leading + (7 * number,))
    body_part = jnp.concatenate([body_part, jnp.zeros(leading + (1,), moved.dtype)], axis=-1)
    padding = [(0, 0)] * len(leading) + [(1, 0), (0, 6)]
    trailing = jnp.pad(moved[..., 7:8], padding).reshape(leading + (7 * number + 7,))[..., : 7 * number + 1]
    return jnp.moveaxis(body_part + trailing, -1, position)


def unfold_pair(values_in, position):
    moved = jnp.moveaxis(values_in, position, -1)
    leading = moved.shape[:-1]
    number = (moved.shape[-1] - 1) // 7
    body_part = moved[..., : 7 * number].reshape(leading + (number, 7))
    trailing = moved[..., 7::7][..., None]
    joined = jnp.concatenate([body_part, trailing], axis=-1)
    return jnp.moveaxis(joined, (-2, -1), (position, position + 1))


def assemble(element_vals):
    sectioned = jnp.transpose(element_vals, (0, 1, 4, 2, 5, 3, 6))
    sectioned = fold_pair(sectioned, 5)
    sectioned = fold_pair(sectioned, 3)
    return fold_pair(sectioned, 1)


def spread_out(unique_grid):
    sectioned = unfold_pair(unique_grid, 1)
    sectioned = unfold_pair(sectioned, 3)
    sectioned = unfold_pair(sectioned, 5)
    return jnp.transpose(sectioned, (0, 1, 3, 5, 2, 4, 6))


def grid_form(values_in, slot_list):
    comps = values_in.shape[0]
    inverse = jnp.argsort(slot_list, axis=-1).astype(jnp.int32)
    picker = jnp.broadcast_to(inverse[None, :, :, :, None], values_in.shape)
    ordered = jnp.take_along_axis(values_in, picker, axis=3)
    shaped = ordered.reshape(comps, PARTS_X, PARTS_Y, EX, EY, EZ, 8, 8, 8)
    shaped = jnp.transpose(shaped, (0, 1, 3, 2, 4, 5, 6, 7, 8))
    return shaped.reshape(comps, PARTS_X * EX, PARTS_Y * EY, EZ, 8, 8, 8)


def stored_form(values_in, slot_list):
    comps = values_in.shape[0]
    shaped = values_in.reshape(comps, PARTS_X, EX, PARTS_Y, EY, EZ, 512)
    shaped = jnp.transpose(shaped, (0, 1, 3, 2, 4, 5, 6)).reshape(comps, PARTS_X, PARTS_Y, E_DEV, 512)
    picker = jnp.broadcast_to(slot_list[None, :, :, :, None].astype(jnp.int32), shaped.shape)
    return jnp.take_along_axis(shaped, picker, axis=3)


def derive(values_in, diff_table, direction, flip):
    matrix = diff_table.T if flip else diff_table
    forms = ("ai,...ijk->...ajk", "aj,...ijk->...iak", "ak,...ijk->...ija")
    return jnp.einsum(forms[direction], matrix, values_in, precision=lax.Precision.HIGHEST)


def reference(adjoint_field, velocity, diffusivity, jacobian, element_slot):
    weights, table_np = gll_tables()
    diff_table = jnp.asarray(table_np)
    weight_cube = jnp.asarray(weight_outer(weights))
    adjoint = grid_form(adjoint_field, element_slot)
    flow = grid_form(velocity.astype(jnp.float32), element_slot)
    conduct = grid_form(diffusivity, element_slot)
    mass_term = grid_form(jacobian[None], element_slot)[0] * weight_cube

    def deriv(values_in, direction):
        return derive(values_in, diff_table, direction, False)

    rotation = jnp.stack([
        deriv(adjoint[2], 1) - deriv(adjoint[1], 2),
        deriv(adjoint[0], 2) - deriv(adjoint[2], 0),
        deriv(adjoint[1], 0) - deriv(adjoint[0], 1)])
    induced = jnp.stack([
        flow[1] * rotation[2] - flow[2] * rotation[1],
        flow[2] * rotation[0] - flow[0] * rotation[2],
        flow[0] * rotation[1] - flow[1] * rotation[0]])
    source = mass_term * (adjoint + time_step * induced)
    right_side = assemble(source)

    def operate(vector):
        element_vals = spread_out(vector)
        stiffness = jnp.zeros_like(element_vals)
        for direction in range(3):
            fluxes = weight_cube * conduct[direction] * derive(element_vals, diff_table, direction, False)
            stiffness = stiffness + derive(fluxes, diff_table, direction, True)
        return assemble(mass_term * element_vals + time_step * stiffness)

    solution = jnp.zeros_like(right_side)
    residual = right_side
    direction_vec = right_side
    norm_now = jnp.sum(residual * residual)
    for step_index in range(ITERS):
        applied = operate(direction_vec)
        step_len = norm_now / jnp.sum(direction_vec * applied)
        solution = solution + step_len * direction_vec
        residual = residual - step_len * applied
        norm_next = jnp.sum(residual * residual)
        direction_vec = residual + (norm_next / norm_now) * direction_vec
        norm_now = norm_next
    return stored_form(spread_out(solution), element_slot)
```

```python
import jax
import jax.numpy as jnp
import numpy as np
from jax import lax
from jax.experimental import pallas as pl
from jax.experimental.pallas import tpu as pltpu
from jax.sharding import PartitionSpec as P


STEPS = 4
DT = 0.25
SCALE = 0.5
f32 = jnp.float32
highest = lax.Precision.HIGHEST


def legendre_seven(points):
    previous = points * 0.0 + 1.0
    current = points
    for degree in range(1, 7):
        following = ((2 * degree + 1) * points * current - degree * previous) / (degree + 1)
        previous = current
        current = following
    return current


def gll_tables():
    poly_order = 7
    points = np.array(
        [
            -1.0,
            -0.8717401485096066,
            -0.5917001814331423,
            -0.2092992179024789,
            0.2092992179024789,
            0.5917001814331423,
            0.8717401485096066,
            1.0,
        ]
    )
    end_values = legendre_seven(points)
    weights = 2.0 / (poly_order * (poly_order + 1) * end_values**2)
    spread = points[:, None] - points[None, :]
    identity = np.eye(poly_order + 1)
    diff_table = end_values[:, None] / (end_values[None, :] * (spread + identity))
    diff_table = diff_table * (1.0 - identity)
    corners = np.zeros(poly_order + 1)
    corners[0] = -poly_order * (poly_order + 1) / 4.0
    corners[-1] = poly_order * (poly_order + 1) / 4.0
    diff_table = diff_table + identity * corners[None, :]
    return (weights.astype(np.float32), diff_table.astype(np.float32))


WEIGHTS, DMAT = gll_tables()
WMAX = [float(w) for w in WEIGHTS]


def halves(mat):
    mat = mat.astype(np.float64)
    assert np.array_equal(mat[::-1, ::-1], -mat)
    odd = 0.5 * (mat[:4, :4] - mat[:4, 7:3:-1])
    even = 0.5 * (mat[:4, :4] + mat[:4, 7:3:-1])
    return odd, even


FWD = halves(DMAT)
BWD = halves(DMAT.T)


def roll_table(mat):
    out = np.zeros((8, 8, 128), np.float32)
    for r in range(8):
        for k in range(8):
            out[r, k, :] = mat[k, (k - r) % 8]
    return out


ROLLS = np.concatenate([roll_table(DMAT), roll_table(DMAT.T)], axis=0)


def along(xs, tables):
    odd, even = tables
    diff = [xs[b] - xs[7 - b] for b in range(4)]
    both = [xs[b] + xs[7 - b] for b in range(4)]
    out = [None] * 8
    for a in range(4):
        s = float(odd[a, 0]) * diff[0]
        t = float(even[a, 0]) * both[0]
        for b in range(1, 4):
            s = s + float(odd[a, b]) * diff[b]
            t = t + float(even[a, b]) * both[b]
        out[a] = s + t
        out[7 - a] = s - t
    return out


def along_k(x, coef):
    out = coef[0] * x
    for r in range(1, 8):
        out = out + coef[r] * pltpu.roll(x, r, 0)
    return out


def lanes():
    lane = lax.broadcasted_iota(jnp.int32, (8, 128), 1)
    return (lane // 32) % 2, (lane // 16) % 2, lane % 16, lane


def is_set(flags, index):
    return jnp.full((8, 128), flags[index], jnp.int32) != 0


def rows(j):
    return pl.ds(pl.multiple_of(8 * j, 8), 8)


def pack_low(face0, face1, first, shift):
    return jnp.where(first, face0, pltpu.roll(face1, shift, 1))


def pack_high(face0, face1, first, shift):
    return jnp.where(first, pltpu.roll(face1, 128 - shift, 1), face0)


def unpack_high(got, first, shift):
    zero = jnp.zeros_like(got)
    return jnp.where(first, zero, pltpu.roll(got, shift, 1)), jnp.where(first, zero, got)


def unpack_low(got, first, shift):
    zero = jnp.zeros_like(got)
    return jnp.where(first, pltpu.roll(got, 128 - shift, 1), zero), jnp.where(first, got, zero)


def received(even, odd, parity, has_low, has_high):
    zero = jnp.zeros_like(even)
    low = jnp.where(has_low, jnp.where(parity, even, odd), zero)
    high = jnp.where(has_high, jnp.where(parity, odd, even), zero)
    return low, high


def assemble_local(u, flags, send_e, send_o, y_low, y_high):
    X, Y, Z, _ = lanes()
    x0, y0 = X == 0, Y == 0
    for t in range(2):
        for i in range(8):
            low = u[t, i, pl.ds(0, 8, 8), :]
            high = u[t, i, pl.ds(7, 8, 8), :]
            u[t, i, pl.ds(0, 8, 8), :] = low + jnp.where(Z > 0, pltpu.roll(high, 1, 1), 0.0)
            u[t, i, pl.ds(7, 8, 8), :] = high + jnp.where(Z < 15, pltpu.roll(low, 127, 1), 0.0)
    for t in range(2):
        for i in range(8):
            low = u[t, i, 0:8, :]
            high = u[t, i, 56:64, :]
            u[t, i, 0:8, :] = low + jnp.where(y0, 0.0, pltpu.roll(high, 16, 1))
            u[t, i, 56:64, :] = high + jnp.where(y0, pltpu.roll(low, 112, 1), 0.0)
    parity = is_set(flags, 0)
    for j in range(8):
        at = slice(8 * j, 8 * j + 8)
        lows, highs = [], []
        for t in range(2):
            low = u[t, 0, at, :]
            high = u[t, 7, at, :]
            lows.append(low + jnp.where(x0, 0.0, pltpu.roll(high, 32, 1)))
            highs.append(high + jnp.where(x0, pltpu.roll(low, 96, 1), 0.0))
            u[t, 0, at, :] = lows[t]
            u[t, 7, at, :] = highs[t]
        to_low = pack_low(lows[0], lows[1], x0, 32)
        to_high = pack_high(highs[0], highs[1], x0, 32)
        send_e[at, :] = jnp.where(parity, to_low, to_high)
        send_o[at, :] = jnp.where(parity, to_high, to_low)
    for i in range(8):
        at = slice(8 * i, 8 * i + 8)
        y_low[at, :] = pack_low(u[0, i, 0:8, :], u[1, i, 0:8, :], y0, 16)
        y_high[at, :] = pack_high(u[0, i, 56:64, :], u[1, i, 56:64, :], y0, 16)


def setup_kernel(flags, slot, adj, vel, dif, jac, roll_ref, mass, coef, u, send_e, send_o, y_low, y_high, a, v, di, dj, dk):
    _, _, _, lane = lanes()
    where_to = jnp.concatenate([slot[...], slot[...] + 64], axis=1)
    pick = (lax.broadcasted_iota(jnp.int32, (128, 128), 0) == where_to).astype(f32).T
    over = pick[0:64, :] + pick[64:128, :]

    def place(rows_in, table):
        return lax.dot_general(rows_in, table, (((0,), (0,)), ((), ())), precision=highest, preferred_element_type=f32)

    for src, dst in ((adj, a), (vel, v)):
        both = jnp.concatenate([src[0].astype(f32), src[1].astype(f32)], axis=0)
        dst[0] = place(both, pick).reshape(8, 64, 128)
        dst[1] = place(src[2].astype(f32), over).reshape(8, 64, 128)
    for m in range(3):
        coef[m] = place(dif[m], over).reshape(8, 64, 128)
    mass[...] = place(jac[...], over).reshape(8, 64, 128)
    sub = lax.broadcasted_iota(jnp.int32, (8, 128), 0)
    wk = jnp.zeros((8, 128), f32)
    for k in range(8):
        wk = jnp.where(sub == k, WMAX[k], wk)
    for i in range(8):
        for j in range(8):
            at = slice(8 * j, 8 * j + 8)
            w = wk * (WMAX[i] * WMAX[j])
            mass[i, at, :] = mass[i, at, :] * w
            for m in range(3):
                coef[m, i, at, :] = coef[m, i, at, :] * (w * DT)
    kf = [roll_ref[r] for r in range(8)]

    def planes(n, carry):
        t, j = n // 8, n % 8
        xs = [a[t, i, rows(j), :] for i in range(8)]
        out = along(xs, FWD)
        for i in range(8):
            di[t, i, rows(j), :] = out[i]
            dk[t, i, rows(j), :] = along_k(xs[i], kf)
        return carry

    lax.fori_loop(0, 16, planes, 0)

    def columns(n, carry):
        t, i = n // 8, n % 8
        out = along([a[t, i, 8 * j : 8 * j + 8, :] for j in range(8)], FWD)
        for j in range(8):
            dj[t, i, 8 * j : 8 * j + 8, :] = out[j]
        return carry

    lax.fori_loop(0, 16, columns, 0)
    left = lane < 64
    sign = jnp.where(left, 1.0, -1.0)

    def other(x):
        return pltpu.roll(x, 64, 1)

    def cross(i, carry):
        for j in range(8):
            at = slice(8 * j, 8 * j + 8)
            swapped = other(dk[0, i, at, :])
            r_a = jnp.where(left, dj[1, i, at, :] - swapped, swapped - di[1, i, at, :])
            mixed = jnp.where(left, dj[0, i, at, :], di[0, i, at, :])
            r_b = sign * (other(mixed) - mixed)
            v_a, v_b = v[0, i, at, :], v[1, i, at, :]
            s_a = sign * (other(v_a) * r_b - v_b * other(r_a))
            prod = v_a * other(r_a)
            s_b = sign * (prod - other(prod))
            m = mass[i, at, :]
            u[0, i, at, :] = m * (a[0, i, at, :] + DT * s_a)
            u[1, i, at, :] = m * (a[1, i, at, :] + DT * s_b)
        return carry

    lax.fori_loop(0, 8, cross, 0)
    assemble_local(u, flags, send_e, send_o, y_low, y_high)


def mid_kernel(flags, got_e, got_o, y_low, y_high, send_e, send_o):
    X, Y, _, _ = lanes()
    x0, y0 = X == 0, Y == 0
    lows, highs = [], []
    for i in range(8):
        lows.append(y_low[8 * i : 8 * i + 8, :])
        highs.append(y_high[8 * i : 8 * i + 8, :])
    for j, into, pack in ((0, lows, pack_low), (7, highs, pack_high)):
        at = slice(8 * j, 8 * j + 8)
        low, high = received(got_e[at, :], got_o[at, :], is_set(flags, 0), is_set(flags, 2), is_set(flags, 3))
        into[0] = into[0] + pack(*unpack_low(low, x0, 32), y0, 16)
        into[7] = into[7] + pack(*unpack_high(high, x0, 32), y0, 16)
    parity = is_set(flags, 1)
    for i in range(8):
        send_e[8 * i : 8 * i + 8, :] = jnp.where(parity, lows[i], highs[i])
        send_o[8 * i : 8 * i + 8, :] = jnp.where(parity, highs[i], lows[i])


def make_apply(step):
    last = step == STEPS - 1
    n_dots = step + 1 + (step == 0)

    def kernel(flags, u, xe, xo, ye, yo, mass, coef, roll_ref, *refs):
        older = refs[:step]
        if last:
            parts, v, message, y = refs[step:]
        else:
            v, y, send_e, send_o, y_low, y_high, dots = refs[step:]
        X, Y, Z, lane = lanes()
        x0, y0 = X == 0, Y == 0
        scale = 1.0 if step == 0 else SCALE

        def shift(n, carry):
            t, i = n // 8, n % 8
            for j in range(8):
                at = slice(8 * j, 8 * j + 8)
                if step == 0:
                    v[t, i, at, :] = u[t, i, at, :]
                else:
                    v[t, i, at, :] = scale * u[t, i, at, :] - older[-1][t, i, at, :]
            return carry

        lax.fori_loop(0, 16, shift, 0)
        for j in range(8):
            at = slice(8 * j, 8 * j + 8)
            low, high = received(xe[at, :], xo[at, :], is_set(flags, 0), is_set(flags, 2), is_set(flags, 3))
            for i, pair in ((0, unpack_low(low, x0, 32)), (7, unpack_high(high, x0, 32))):
                for t in range(2):
                    v[t, i, at, :] = v[t, i, at, :] + scale * pair[t]
        for i in range(8):
            at = slice(8 * i, 8 * i + 8)
            low, high = received(ye[at, :], yo[at, :], is_set(flags, 1), is_set(flags, 4), is_set(flags, 5))
            for j, pair in ((0, unpack_low(low, y0, 16)), (7, unpack_high(high, y0, 16))):
                for t in range(2):
                    v[t, i, 8 * j : 8 * j + 8, :] = v[t, i, 8 * j : 8 * j + 8, :] + scale * pair[t]

        def planes(n, carry):
            t, j = n // 8, n % 8
            xs = [v[t, i, rows(j), :] for i in range(8)]
            flux = along(xs, FWD)
            out = along([coef[0, i, rows(j), :] * flux[i] for i in range(8)], BWD)
            for i in range(8):
                part = coef[2, i, rows(j), :] * along_k(xs[i], [roll_ref[r] for r in range(8)])
                part = along_k(part, [roll_ref[8 + r] for r in range(8)])
                y[t, i, rows(j), :] = mass[i, rows(j), :] * xs[i] + out[i] + part
            return carry

        lax.fori_loop(0, 16, planes, 0)
        if step == 0:
            wz = jnp.where(((Z > 0) & (lax.broadcasted_iota(jnp.int32, (8, 128), 0) == 0)) | ((Z < 15) & (lax.broadcasted_iota(jnp.int32, (8, 128), 0) == 7)), 0.5, 1.0)
            wy_low = jnp.where((Y == 1) | is_set(flags, 4), 0.5, 1.0)
            wy_high = jnp.where((Y == 0) | is_set(flags, 5), 0.5, 1.0)
            wx_low = jnp.where((X == 1) | is_set(flags, 2), 0.5, 1.0)
            wx_high = jnp.where((X == 0) | is_set(flags, 3), 0.5, 1.0)

        def columns(t):
            def body(i, sums):
                xs = [v[t, i, 8 * j : 8 * j + 8, :] for j in range(8)]
                flux = along(xs, FWD)
                out = along([coef[1, i, 8 * j : 8 * j + 8, :] * flux[j] for j in range(8)], BWD)
                sums = list(sums)
                for j in range(8):
                    at = slice(8 * j, 8 * j + 8)
                    total = y[t, i, at, :] + out[j]
                    if not last:
                        y[t, i, at, :] = total
                    for m in range(step):
                        sums[m] = sums[m] + older[m][t, i, at, :] * total
                    sums[step] = sums[step] + xs[j] * total
                if step == 0:
                    index = jnp.full((8, 128), i, jnp.int32)
                    wx = wz * jnp.where(index == 0, wx_low, jnp.where(index == 7, wx_high, 1.0))
                    square = xs[1] * xs[1]
                    for j in range(2, 7):
                        square = square + xs[j] * xs[j]
                    square = square + wy_low * (xs[0] * xs[0]) + wy_high * (xs[7] * xs[7])
                    sums[1] = sums[1] + wx * square
                return tuple(sums)

            return lax.fori_loop(0, 8, body, tuple(jnp.zeros((8, 128), f32) for _ in range(n_dots)))

        first = columns(0)
        second = columns(1)
        sums = [p + 0.5 * q for p, q in zip(first, second)]
        if not last:
            for m in range(n_dots):
                dots[8 * m : 8 * m + 8, :] = sums[m]
            assemble_local(y, flags, send_e, send_o, y_low, y_high)
            return
        row_of = lax.broadcasted_iota(jnp.int32, (16, 128), 0)
        lane_of = lax.broadcasted_iota(jnp.int32, (16, 128), 1)
        table = jnp.zeros((16, 128), f32)
        every = [parts[8 * m : 8 * m + 8, :] for m in range(7)] + sums
        for m, value in enumerate(every):
            table = jnp.where(row_of == m, jnp.sum(value, axis=0, keepdims=True), table)
        column = jnp.sum(table, axis=1, keepdims=True)
        line = jnp.sum(jnp.where(row_of == lane_of, column, 0.0), axis=0, keepdims=True)
        message[...] = jnp.broadcast_to(line, message.shape)

    return kernel


def finish_kernel(slot, got, v0, v1, v2, v3, out):
    total = jnp.sum(got[...], axis=0, keepdims=True)
    lane = lax.broadcasted_iota(jnp.int32, (1, 128), 1)

    def entry(m):
        return jnp.sum(jnp.where(lane == m, total, 0.0), axis=1, keepdims=True)

    gram = {}
    order = [(0, 0), None, (0, 1), (1, 1), (0, 2), (1, 2), (2, 2), (0, 3), (1, 3), (2, 3), (3, 3)]
    for m, pair in enumerate(order):
        if pair is None:
            square = entry(m)
        else:
            gram[pair] = entry(m)
    right = [square]
    for j in range(3):
        right.append(SCALE * gram[(0, j)] - right[j])
    lower, inverse, reduced = {}, [], []
    for c in range(4):
        pivot = gram[(c, c)]
        value = right[c]
        for m in range(c):
            pivot = pivot - lower[(c, m)] * lower[(c, m)] * inverse[m]
            value = value - lower[(c, m)] * reduced[m] * inverse[m]
        good = pivot > 1e-6 * gram[(c, c)]
        inverse.append(jnp.where(good, 1.0 / jnp.where(good, pivot, 1.0), 0.0))
        reduced.append(value)
        for r in range(c + 1, 4):
            acc = gram[(c, r)]
            for m in range(c):
                acc = acc - lower[(r, m)] * lower[(c, m)] * inverse[m]
            lower[(r, c)] = acc
    weight = [None] * 4
    for c in reversed(range(4)):
        acc = reduced[c]
        for r in range(c + 1, 4):
            acc = acc - lower[(r, c)] * weight[r]
        weight[c] = acc * inverse[c]
    where_to = jnp.concatenate([slot[...], slot[...] + 64], axis=1)
    pick = (lax.broadcasted_iota(jnp.int32, (128, 128), 0) == where_to).astype(f32).T
    for t in range(2):
        x = weight[0].reshape(1, 1, 1) * v0[t]
        for c, v in ((1, v1), (2, v2), (3, v3)):
            x = x + weight[c].reshape(1, 1, 1) * v[t]
        table = pick if t == 0 else pick[0:64, :]
        res = lax.dot_general(table, x.reshape(512, 128), (((1,), (1,)), ((), ())), precision=highest, preferred_element_type=f32)
        if t == 0:
            out[0] = res[0:64, :]
            out[1] = res[64:128, :]
        else:
            out[2] = res


def swaps(count, odd):
    pairs = []
    for i in range(odd, count, 2):
        pairs += [(i, (i + 1) % count), ((i + 1) % count, i)]
    return pairs


def solution(mesh):
    vmem = pl.BlockSpec(memory_space=pltpu.VMEM)
    smem = pl.BlockSpec(memory_space=pltpu.SMEM)
    params = pltpu.CompilerParams(vmem_limit_bytes=40 * 1024 * 1024)
    sx, sy = mesh.shape["gx"], mesh.shape["gy"]

    def shape(*dims):
        return jax.ShapeDtypeStruct(dims, f32)

    field, face = shape(2, 8, 64, 128), shape(64, 128)

    def call(kernel, outs, n_in, scratch=(), name=None):
        return pl.pallas_call(
            kernel,
            out_shape=outs,
            in_specs=[smem] + [vmem] * (n_in - 1),
            out_specs=[vmem] * len(outs),
            scratch_shapes=scratch,
            compiler_params=params,
            name=name,
        )

    def local(adjoint_field, velocity, diffusivity, jacobian, element_slot):
        gx, gy = lax.axis_index("gx"), lax.axis_index("gy")
        flags = jnp.stack([gx % 2, gy % 2, gx > 0, gx < sx - 1, gy > 0, gy < sy - 1]).astype(jnp.int32)
        slot = element_slot.reshape(1, 64)
        table = jnp.asarray(ROLLS)
        big = pltpu.VMEM((2, 8, 64, 128), f32)
        mass, coef, u, xe, xo, yl, yh = call(
            setup_kernel, [shape(8, 64, 128), shape(3, 8, 64, 128), field, face, face, face, face], 7, [big] * 5, "setup"
        )(flags, slot, adjoint_field.reshape(3, 64, 512), velocity.reshape(3, 64, 512), diffusivity.reshape(3, 64, 512), jacobian.reshape(64, 512), table)
        vs, parts = [], []
        for step in range(STEPS):
            xe = lax.ppermute(xe, "gx", swaps(sx, 0))
            xo = lax.ppermute(xo, "gx", swaps(sx, 1))
            ye, yo = call(mid_kernel, [face, face], 5, name="mid")(flags, xe, xo, yl, yh)
            ye = lax.ppermute(ye, "gy", swaps(sy, 0))
            yo = lax.ppermute(yo, "gy", swaps(sy, 1))
            args = [flags, u, xe, xo, ye, yo, mass, coef, table] + vs
            if step < STEPS - 1:
                n_dots = step + 1 + (step == 0)
                v, u, xe, xo, yl, yh, dots = call(
                    make_apply(step), [field, field, face, face, face, face, shape(8 * n_dots, 128)], len(args), name=f"apply{step}"
                )(*args)
                vs.append(v)
                parts.append(dots)
            else:
                parts = jnp.concatenate(parts, axis=0)
                v, message = call(make_apply(step), [field, shape(sx * sy, 128)], len(args) + 1, [big], "apply3")(*args, parts)
                vs.append(v)
        got = lax.all_to_all(message.reshape(sx * sy, 1, 128), ("gx", "gy"), 0, 0).reshape(sx * sy, 128)
        (out,) = pl.pallas_call(
            finish_kernel,
            out_shape=[shape(3, 64, 512)],
            in_specs=[vmem] * 6,
            out_specs=[vmem],
            compiler_params=params,
            name="finish",
        )(slot, got, *vs)
        return out.reshape(3, 1, 1, 64, 512)

    in_specs = (
        P(None, "gx", "gy", None, None),
        P(None, "gx", "gy", None, None),
        P(None, "gx", "gy", None, None),
        P("gx", "gy", None, None),
        P("gx", "gy", None),
    )
    return jax.shard_map(local, mesh=mesh, in_specs=in_specs, out_specs=P(None, "gx", "gy", None, None), check_vma=False)
```

```python
import jax
import jax.numpy as jnp
import numpy as np
from jax import lax
from jax.experimental import pallas as pl
from jax.experimental.pallas import tpu as pltpu
from jax.sharding import PartitionSpec as P


STEPS = 4
DT = 0.25
SCALE = 0.5
f32 = jnp.float32


def legendre_seven(points):
    previous = points * 0.0 + 1.0
    current = points
    for degree in range(1, 7):
        following = ((2 * degree + 1) * points * current - degree * previous) / (degree + 1)
        previous = current
        current = following
    return current


def gll_tables():
    poly_order = 7
    points = np.array(
        [
            -1.0,
            -0.8717401485096066,
            -0.5917001814331423,
            -0.2092992179024789,
            0.2092992179024789,
            0.5917001814331423,
            0.8717401485096066,
            1.0,
        ]
    )
    end_values = legendre_seven(points)
    weights = 2.0 / (poly_order * (poly_order + 1) * end_values**2)
    spread = points[:, None] - points[None, :]
    identity = np.eye(poly_order + 1)
    diff_table = end_values[:, None] / (end_values[None, :] * (spread + identity))
    diff_table = diff_table * (1.0 - identity)
    corners = np.zeros(poly_order + 1)
    corners[0] = -poly_order * (poly_order + 1) / 4.0
    corners[-1] = poly_order * (poly_order + 1) / 4.0
    diff_table = diff_table + identity * corners[None, :]
    return (weights.astype(np.float32), diff_table.astype(np.float32))


WEIGHTS, DMAT = gll_tables()
WMAX = [float(w) for w in WEIGHTS]


def halves(mat):
    mat = mat.astype(np.float64)
    assert np.array_equal(mat[::-1, ::-1], -mat)
    odd = 0.5 * (mat[:4, :4] - mat[:4, 7:3:-1])
    even = 0.5 * (mat[:4, :4] + mat[:4, 7:3:-1])
    return odd, even


FWD = halves(DMAT)
BWD = halves(DMAT.T)


def roll_factors(mat):
    sub = lax.broadcasted_iota(jnp.int32, (8, 128), 0)
    out = []
    for r in range(8):
        factor = jnp.full((8, 128), float(mat[0, -r % 8]), f32)
        for k in range(1, 8):
            factor = jnp.where(sub == k, float(mat[k, (k - r) % 8]), factor)
        out.append(factor)
    return out


def along(xs, tables):
    odd, even = tables
    diff = [xs[b] - xs[7 - b] for b in range(4)]
    both = [xs[b] + xs[7 - b] for b in range(4)]
    out = [None] * 8
    for a in range(4):
        s = float(odd[a, 0]) * diff[0]
        t = float(even[a, 0]) * both[0]
        for b in range(1, 4):
            s = s + float(odd[a, b]) * diff[b]
            t = t + float(even[a, b]) * both[b]
        out[a] = s + t
        out[7 - a] = s - t
    return out


def along_k(x, coef):
    out = coef[0] * x
    for r in range(1, 8):
        out = out + coef[r] * pltpu.roll(x, r, 0)
    return out


def lanes():
    lane = lax.broadcasted_iota(jnp.int32, (8, 128), 1)
    return (lane // 32) % 2, (lane // 16) % 2, lane % 16, lane


def is_set(flags, index):
    return jnp.broadcast_to(flags[index : index + 1, :], (8, 128)) != 0


def rows(j):
    return pl.ds(pl.multiple_of(8 * j, 8), 8)


def pack_low(face0, face1, first, shift):
    return jnp.where(first, face0, pltpu.roll(face1, shift, 1))


def pack_high(face0, face1, first, shift):
    return jnp.where(first, pltpu.roll(face1, 128 - shift, 1), face0)


def unpack_high(got, first, shift):
    zero = jnp.zeros_like(got)
    return jnp.where(first, zero, pltpu.roll(got, shift, 1)), jnp.where(first, zero, got)


def unpack_low(got, first, shift):
    zero = jnp.zeros_like(got)
    return jnp.where(first, pltpu.roll(got, 128 - shift, 1), zero), jnp.where(first, got, zero)


def received(even, odd, parity, has_low, has_high):
    zero = jnp.zeros_like(even)
    low = jnp.where(has_low, jnp.where(parity, even, odd), zero)
    high = jnp.where(has_high, jnp.where(parity, odd, even), zero)
    return low, high


def assemble_local(u, flags, send_e, send_o, y_low, y_high):
    X, Y, Z, _ = lanes()
    x0, y0 = X == 0, Y == 0
    for t in range(2):
        for i in range(8):
            low = u[t, i, pl.ds(0, 8, 8), :]
            high = u[t, i, pl.ds(7, 8, 8), :]
            u[t, i, pl.ds(0, 8, 8), :] = low + jnp.where(Z > 0, pltpu.roll(high, 1, 1), 0.0)
            u[t, i, pl.ds(7, 8, 8), :] = high + jnp.where(Z < 15, pltpu.roll(low, 127, 1), 0.0)
    for t in range(2):
        for i in range(8):
            low = u[t, i, 0:8, :]
            high = u[t, i, 56:64, :]
            u[t, i, 0:8, :] = low + jnp.where(y0, 0.0, pltpu.roll(high, 16, 1))
            u[t, i, 56:64, :] = high + jnp.where(y0, pltpu.roll(low, 112, 1), 0.0)
    parity = is_set(flags, 0)
    for j in range(8):
        at = slice(8 * j, 8 * j + 8)
        lows, highs = [], []
        for t in range(2):
            low = u[t, 0, at, :]
            high = u[t, 7, at, :]
            lows.append(low + jnp.where(x0, 0.0, pltpu.roll(high, 32, 1)))
            highs.append(high + jnp.where(x0, pltpu.roll(low, 96, 1), 0.0))
            u[t, 0, at, :] = lows[t]
            u[t, 7, at, :] = highs[t]
        to_low = pack_low(lows[0], lows[1], x0, 32)
        to_high = pack_high(highs[0], highs[1], x0, 32)
        send_e[at, :] = jnp.where(parity, to_low, to_high)
        send_o[at, :] = jnp.where(parity, to_high, to_low)
    for i in range(8):
        at = slice(8 * i, 8 * i + 8)
        y_low[at, :] = pack_low(u[0, i, 0:8, :], u[1, i, 0:8, :], y0, 16)
        y_high[at, :] = pack_high(u[0, i, 56:64, :], u[1, i, 56:64, :], y0, 16)


def thirds(x):
    high = x.astype(jnp.bfloat16)
    rest = x - high.astype(f32)
    mid = rest.astype(jnp.bfloat16)
    low = (rest - mid.astype(f32)).astype(jnp.bfloat16)
    return [high, mid, low]


def pick_table(flags):
    return (lax.broadcasted_iota(jnp.int32, (128, 128), 0) == flags[8:9, :]).astype(f32).T


def place(parts, table):
    rows_in = jnp.concatenate(parts, axis=0)
    tables = jnp.concatenate([table.astype(jnp.bfloat16)] * len(parts), axis=0)
    out = lax.dot_general(rows_in, tables, (((0,), (0,)), ((), ())), preferred_element_type=f32)
    return out.reshape(8, 64, 128)


def weight_k():
    sub = lax.broadcasted_iota(jnp.int32, (8, 128), 0)
    wk = jnp.zeros((8, 128), f32)
    for k in range(8):
        wk = jnp.where(sub == k, WMAX[k], wk)
    return wk


def coef_kernel(flags, dif, coef):
    pick = pick_table(flags)
    over = pick[0:64, :] + pick[64:128, :]
    wk = weight_k()
    for m in range(3):
        coef[m] = place(thirds(dif[m]), over)
        for i in range(8):
            for j in range(8):
                at = slice(8 * j, 8 * j + 8)
                coef[m, i, at, :] = coef[m, i, at, :] * (wk * (WMAX[i] * WMAX[j] * DT))


def setup_kernel(flags, adj_hbm, vel_hbm, jac_hbm, mass, u, roll_ref, send_e, send_o, y_low, y_high, a, v, di, dj, dk, adj, vel, jac, sems):
    copies = [pltpu.make_async_copy(adj_hbm.at[c], adj.at[c], sems.at[c]) for c in range(3)]
    copies += [pltpu.make_async_copy(vel_hbm.at[c], vel.at[c], sems.at[3 + c]) for c in range(3)]
    copies.append(pltpu.make_async_copy(jac_hbm, jac, sems.at[6]))
    for copy in copies:
        copy.start()
    _, _, _, lane = lanes()
    pick = pick_table(flags)
    over = pick[0:64, :] + pick[64:128, :]
    wk = weight_k()
    for copy in copies[:3]:
        copy.wait()
    a[0] = place(thirds(jnp.concatenate([adj[0], adj[1]], axis=0)), pick)
    a[1] = place(thirds(adj[2]), over)
    kf = roll_factors(DMAT)
    for r, factor in enumerate(kf + roll_factors(DMAT.T)):
        roll_ref[r] = factor

    def planes(n, carry):
        t, j = n // 8, n % 8
        xs = [a[t, i, rows(j), :] for i in range(8)]
        out = along(xs, FWD)
        for i in range(8):
            di[t, i, rows(j), :] = out[i]
            dk[t, i, rows(j), :] = along_k(xs[i], kf)
        return carry

    lax.fori_loop(0, 16, planes, 0)

    def columns(n, carry):
        t, i = n // 8, n % 8
        out = along([a[t, i, 8 * j : 8 * j + 8, :] for j in range(8)], FWD)
        for j in range(8):
            dj[t, i, 8 * j : 8 * j + 8, :] = out[j]
        return carry

    lax.fori_loop(0, 16, columns, 0)
    for copy in copies[3:]:
        copy.wait()
    v[0] = place([jnp.concatenate([vel[0], vel[1]], axis=0)], pick)
    v[1] = place([vel[2]], over)
    mass[...] = place(thirds(jac[...]), over)
    left = lane < 64
    sign = jnp.where(left, 1.0, -1.0)

    def other(x):
        return pltpu.roll(x, 64, 1)

    def cross(i, carry):
        index = jnp.full((8, 128), i, jnp.int32)
        wi = jnp.zeros((8, 128), f32)
        for n in range(8):
            wi = jnp.where(index == n, WMAX[n], wi)
        wi = wk * wi
        for j in range(8):
            at = slice(8 * j, 8 * j + 8)
            swapped = other(dk[0, i, at, :])
            r_a = jnp.where(left, dj[1, i, at, :] - swapped, swapped - di[1, i, at, :])
            mixed = jnp.where(left, dj[0, i, at, :], di[0, i, at, :])
            r_b = sign * (other(mixed) - mixed)
            v_a, v_b = v[0, i, at, :], v[1, i, at, :]
            s_a = sign * (other(v_a) * r_b - v_b * other(r_a))
            prod = v_a * other(r_a)
            s_b = sign * (prod - other(prod))
            m = mass[i, at, :] * (wi * WMAX[j])
            mass[i, at, :] = m
            u[0, i, at, :] = m * (a[0, i, at, :] + DT * s_a)
            u[1, i, at, :] = m * (a[1, i, at, :] + DT * s_b)
        return carry

    lax.fori_loop(0, 8, cross, 0)
    assemble_local(u, flags, send_e, send_o, y_low, y_high)


def mid_kernel(flags, got_e, got_o, y_low, y_high, send_e, send_o):
    X, Y, _, _ = lanes()
    x0, y0 = X == 0, Y == 0
    lows, highs = [], []
    for i in range(8):
        lows.append(y_low[8 * i : 8 * i + 8, :])
        highs.append(y_high[8 * i : 8 * i + 8, :])
    for j, into, pack in ((0, lows, pack_low), (7, highs, pack_high)):
        at = slice(8 * j, 8 * j + 8)
        low, high = received(got_e[at, :], got_o[at, :], is_set(flags, 0), is_set(flags, 2), is_set(flags, 3))
        into[0] = into[0] + pack(*unpack_low(low, x0, 32), y0, 16)
        into[7] = into[7] + pack(*unpack_high(high, x0, 32), y0, 16)
    parity = is_set(flags, 1)
    for i in range(8):
        send_e[8 * i : 8 * i + 8, :] = jnp.where(parity, lows[i], highs[i])
        send_o[8 * i : 8 * i + 8, :] = jnp.where(parity, highs[i], lows[i])


def make_apply(step):
    last = step == STEPS - 1
    n_dots = step + 1 + (step == 0)

    def kernel(flags, u, xe, xo, ye, yo, mass, coef, roll_ref, *refs):
        older = refs[:step]
        if last:
            parts, v, message, y = refs[step:]
        else:
            v, y, send_e, send_o, y_low, y_high, dots = refs[step:]
        X, Y, Z, lane = lanes()
        x0, y0 = X == 0, Y == 0
        scale = 1.0 if step == 0 else SCALE

        def shift(n, carry):
            t, i = n // 8, n % 8
            for j in range(8):
                at = slice(8 * j, 8 * j + 8)
                if step == 0:
                    v[t, i, at, :] = u[t, i, at, :]
                else:
                    v[t, i, at, :] = scale * u[t, i, at, :] - older[-1][t, i, at, :]
            return carry

        lax.fori_loop(0, 16, shift, 0)
        for j in range(8):
            at = slice(8 * j, 8 * j + 8)
            low, high = received(xe[at, :], xo[at, :], is_set(flags, 0), is_set(flags, 2), is_set(flags, 3))
            for i, pair in ((0, unpack_low(low, x0, 32)), (7, unpack_high(high, x0, 32))):
                for t in range(2):
                    v[t, i, at, :] = v[t, i, at, :] + scale * pair[t]
        for i in range(8):
            at = slice(8 * i, 8 * i + 8)
            low, high = received(ye[at, :], yo[at, :], is_set(flags, 1), is_set(flags, 4), is_set(flags, 5))
            for j, pair in ((0, unpack_low(low, y0, 16)), (7, unpack_high(high, y0, 16))):
                for t in range(2):
                    v[t, i, 8 * j : 8 * j + 8, :] = v[t, i, 8 * j : 8 * j + 8, :] + scale * pair[t]

        def planes(n, carry):
            t, j = n // 8, n % 8
            xs = [v[t, i, rows(j), :] for i in range(8)]
            flux = along(xs, FWD)
            out = along([coef[0, i, rows(j), :] * flux[i] for i in range(8)], BWD)
            for i in range(8):
                part = coef[2, i, rows(j), :] * along_k(xs[i], [roll_ref[r] for r in range(8)])
                part = along_k(part, [roll_ref[8 + r] for r in range(8)])
                y[t, i, rows(j), :] = mass[i, rows(j), :] * xs[i] + out[i] + part
            return carry

        lax.fori_loop(0, 16, planes, 0)
        if step == 0:
            wz = jnp.where(((Z > 0) & (lax.broadcasted_iota(jnp.int32, (8, 128), 0) == 0)) | ((Z < 15) & (lax.broadcasted_iota(jnp.int32, (8, 128), 0) == 7)), 0.5, 1.0)
            wy_low = jnp.where((Y == 1) | is_set(flags, 4), 0.5, 1.0)
            wy_high = jnp.where((Y == 0) | is_set(flags, 5), 0.5, 1.0)
            wx_low = jnp.where((X == 1) | is_set(flags, 2), 0.5, 1.0)
            wx_high = jnp.where((X == 0) | is_set(flags, 3), 0.5, 1.0)

        def columns(t):
            def body(i, sums):
                xs = [v[t, i, 8 * j : 8 * j + 8, :] for j in range(8)]
                flux = along(xs, FWD)
                out = along([coef[1, i, 8 * j : 8 * j + 8, :] * flux[j] for j in range(8)], BWD)
                sums = list(sums)
                for j in range(8):
                    at = slice(8 * j, 8 * j + 8)
                    total = y[t, i, at, :] + out[j]
                    if not last:
                        y[t, i, at, :] = total
                    for m in range(step):
                        sums[m] = sums[m] + older[m][t, i, at, :] * total
                    sums[step] = sums[step] + xs[j] * total
                if step == 0:
                    index = jnp.full((8, 128), i, jnp.int32)
                    wx = wz * jnp.where(index == 0, wx_low, jnp.where(index == 7, wx_high, 1.0))
                    square = xs[1] * xs[1]
                    for j in range(2, 7):
                        square = square + xs[j] * xs[j]
                    square = square + wy_low * (xs[0] * xs[0]) + wy_high * (xs[7] * xs[7])
                    sums[1] = sums[1] + wx * square
                return tuple(sums)

            return lax.fori_loop(0, 8, body, tuple(jnp.zeros((8, 128), f32) for _ in range(n_dots)))

        first = columns(0)
        second = columns(1)
        sums = [p + 0.5 * q for p, q in zip(first, second)]
        if not last:
            for m in range(n_dots):
                dots[8 * m : 8 * m + 8, :] = sums[m]
            assemble_local(y, flags, send_e, send_o, y_low, y_high)
            return
        row_of = lax.broadcasted_iota(jnp.int32, (16, 128), 0)
        lane_of = lax.broadcasted_iota(jnp.int32, (16, 128), 1)
        table = jnp.zeros((16, 128), f32)
        every = [parts[8 * m : 8 * m + 8, :] for m in range(7)] + sums
        for m, value in enumerate(every):
            table = jnp.where(row_of == m, jnp.sum(value, axis=0, keepdims=True), table)
        column = jnp.sum(table, axis=1, keepdims=True)
        line = jnp.sum(jnp.where(row_of == lane_of, column, 0.0), axis=0, keepdims=True)
        message[...] = jnp.broadcast_to(line, message.shape)

    return kernel


def store_kernel(flags, v0, v1, v2, v3, stored):
    pick = pick_table(flags).astype(jnp.bfloat16)
    table = jnp.concatenate([pick] * 3, axis=1)
    single = jnp.concatenate([pick[0:64, :]] * 3, axis=1)
    for c, v in enumerate((v0, v1, v2, v3)):
        for t in range(2):
            x = jnp.concatenate(thirds(v[t].reshape(512, 128)), axis=1)
            res = lax.dot_general(table if t == 0 else single, x, (((1,), (1,)), ((), ())), preferred_element_type=f32)
            if t == 0:
                stored[c, 0] = res[0:64, :]
                stored[c, 1] = res[64:128, :]
            else:
                stored[c, 2] = res


def finish_kernel(got, stored, out):
    total = jnp.sum(got[...], axis=0, keepdims=True)
    lane = lax.broadcasted_iota(jnp.int32, (1, 128), 1)

    def entry(m):
        return jnp.sum(jnp.where(lane == m, total, 0.0), axis=1, keepdims=True)

    gram = {}
    order = [(0, 0), None, (0, 1), (1, 1), (0, 2), (1, 2), (2, 2), (0, 3), (1, 3), (2, 3), (3, 3)]
    for m, pair in enumerate(order):
        if pair is None:
            square = entry(m)
        else:
            gram[pair] = entry(m)
    right = [square]
    for j in range(3):
        right.append(SCALE * gram[(0, j)] - right[j])
    lower, inverse, reduced = {}, [], []
    for c in range(4):
        pivot = gram[(c, c)]
        value = right[c]
        for m in range(c):
            pivot = pivot - lower[(c, m)] * lower[(c, m)] * inverse[m]
            value = value - lower[(c, m)] * reduced[m] * inverse[m]
        good = pivot > 1e-6 * gram[(c, c)]
        inverse.append(jnp.where(good, 1.0 / jnp.where(good, pivot, 1.0), 0.0))
        reduced.append(value)
        for r in range(c + 1, 4):
            acc = gram[(c, r)]
            for m in range(c):
                acc = acc - lower[(r, m)] * lower[(c, m)] * inverse[m]
            lower[(r, c)] = acc
    weight = [None] * 4
    for c in reversed(range(4)):
        acc = reduced[c]
        for r in range(c + 1, 4):
            acc = acc - lower[(r, c)] * weight[r]
        weight[c] = acc * inverse[c]
    for n in range(3):
        x = weight[0] * stored[0, n]
        for c in range(1, 4):
            x = x + weight[c] * stored[c, n]
        out[n] = x


def swaps(count, odd):
    pairs = []
    for i in range(count):
        other = i + 1 if i % 2 == odd else i - 1
        pairs.append((i, other if 0 <= other < count else i))
    return pairs


def solution(mesh):
    vmem = pl.BlockSpec(memory_space=pltpu.VMEM)
    params = pltpu.CompilerParams(vmem_limit_bytes=40 * 1024 * 1024)
    sx, sy = mesh.shape["gx"], mesh.shape["gy"]

    def shape(*dims):
        return jax.ShapeDtypeStruct(dims, f32)

    field, face = shape(2, 8, 64, 128), shape(64, 128)

    anywhere = pl.BlockSpec(memory_space=pltpu.HBM)

    def call(kernel, outs, ins, scratch=(), name=None, cost=None):
        return pl.pallas_call(
            kernel,
            out_shape=outs,
            in_specs=ins if isinstance(ins, list) else [vmem] * ins,
            out_specs=[vmem] * len(outs),
            scratch_shapes=scratch,
            compiler_params=params,
            cost_estimate=pl.CostEstimate(flops=0, transcendentals=0, bytes_accessed=cost) if cost else None,
            name=name,
        )

    def held(x):
        return pltpu.with_memory_space_constraint(x, pltpu.HBM)

    def local(adjoint_field, velocity, diffusivity, jacobian, element_slot):
        gx, gy = lax.axis_index("gx"), lax.axis_index("gy")
        flags = jnp.stack([gx % 2, gy % 2, gx > 0, gx < sx - 1, gy > 0, gy < sy - 1, gx, gy]).astype(jnp.int32)
        slot = element_slot.reshape(1, 64)
        slot = jnp.broadcast_to(jnp.concatenate([slot, slot + 64], axis=1), (8, 128))
        flags = jnp.concatenate([jnp.broadcast_to(flags[:, None], (8, 128)), slot], axis=0)
        big = pltpu.VMEM((2, 8, 64, 128), f32)
        scratch = [big] * 5 + [
            pltpu.VMEM((3, 64, 512), f32),
            pltpu.VMEM((3, 64, 512), jnp.bfloat16),
            pltpu.VMEM((64, 512), f32),
            pltpu.SemaphoreType.DMA((7,)),
        ]
        mass, u, table, xe, xo, yl, yh = call(
            setup_kernel,
            [shape(8, 64, 128), field, shape(16, 8, 128), face, face, face, face],
            [vmem, anywhere, anywhere, anywhere],
            scratch,
            "setup",
        )(flags, held(adjoint_field.reshape(3, 64, 512)), held(velocity.reshape(3, 64, 512)), held(jacobian.reshape(64, 512)))
        (coef,) = call(coef_kernel, [shape(3, 8, 64, 128)], 2, name="coef", cost=3 << 20)(flags, diffusivity.reshape(3, 64, 512))
        vs, parts = [], []
        for step in range(STEPS):
            xe = lax.ppermute(xe, "gx", swaps(sx, 0))
            xo = lax.ppermute(xo, "gx", swaps(sx, 1))
            ye, yo = call(mid_kernel, [face, face], 5, name="mid")(flags, xe, xo, yl, yh)
            ye = lax.ppermute(ye, "gy", swaps(sy, 0))
            yo = lax.ppermute(yo, "gy", swaps(sy, 1))
            args = [flags, u, xe, xo, ye, yo, mass, coef, table] + vs
            if step < STEPS - 1:
                n_dots = step + 1 + (step == 0)
                v, u, xe, xo, yl, yh, dots = call(
                    make_apply(step), [field, field, face, face, face, face, shape(8 * n_dots, 128)], len(args), name=f"apply{step}"
                )(*args)
                vs.append(v)
                parts.append(dots)
            else:
                parts = jnp.concatenate(parts, axis=0)
                v, message = call(make_apply(step), [field, shape(sx * sy, 128)], len(args) + 1, [big], "apply3")(*args, parts)
                vs.append(v)
        got = lax.all_to_all(message.reshape(sx * sy, 1, 128), ("gx", "gy"), 0, 0).reshape(sx * sy, 128)
        (stored,) = call(store_kernel, [shape(4, 3, 64, 512)], 5, name="store", cost=6 << 20)(flags, *vs)
        (out,) = call(finish_kernel, [shape(3, 64, 512)], 2, name="finish")(got, stored)
        return out.reshape(3, 1, 1, 64, 512)

    in_specs = (
        P(None, "gx", "gy", None, None),
        P(None, "gx", "gy", None, None),
        P(None, "gx", "gy", None, None),
        P("gx", "gy", None, None),
        P("gx", "gy", None),
    )
    return jax.shard_map(local, mesh=mesh, in_specs=in_specs, out_specs=P(None, "gx", "gy", None, None), check_vma=False)
```

```python
import jax
import jax.numpy as jnp
import numpy as np
from jax import lax
from jax.experimental import pallas as pl
from jax.experimental.pallas import tpu as pltpu
from jax.sharding import PartitionSpec as P


STEPS = 4
DT = 0.25
SCALE = 0.5
f32 = jnp.float32


def legendre_seven(points):
    previous = points * 0.0 + 1.0
    current = points
    for degree in range(1, 7):
        following = ((2 * degree + 1) * points * current - degree * previous) / (degree + 1)
        previous = current
        current = following
    return current


def gll_tables():
    poly_order = 7
    points = np.array(
        [
            -1.0,
            -0.8717401485096066,
            -0.5917001814331423,
            -0.2092992179024789,
            0.2092992179024789,
            0.5917001814331423,
            0.8717401485096066,
            1.0,
        ]
    )
    end_values = legendre_seven(points)
    weights = 2.0 / (poly_order * (poly_order + 1) * end_values**2)
    spread = points[:, None] - points[None, :]
    identity = np.eye(poly_order + 1)
    diff_table = end_values[:, None] / (end_values[None, :] * (spread + identity))
    diff_table = diff_table * (1.0 - identity)
    corners = np.zeros(poly_order + 1)
    corners[0] = -poly_order * (poly_order + 1) / 4.0
    corners[-1] = poly_order * (poly_order + 1) / 4.0
    diff_table = diff_table + identity * corners[None, :]
    return (weights.astype(np.float32), diff_table.astype(np.float32))


WEIGHTS, DMAT = gll_tables()
WMAX = [float(w) for w in WEIGHTS]


def halves(mat):
    mat = mat.astype(np.float64)
    assert np.array_equal(mat[::-1, ::-1], -mat)
    odd = 0.5 * (mat[:4, :4] - mat[:4, 7:3:-1])
    even = 0.5 * (mat[:4, :4] + mat[:4, 7:3:-1])
    return odd, even


FWD = halves(DMAT)
BWD = halves(DMAT.T)


def roll_factors(mat):
    sub = lax.broadcasted_iota(jnp.int32, (8, 128), 0)
    out = []
    for r in range(8):
        factor = jnp.full((8, 128), float(mat[0, -r % 8]), f32)
        for k in range(1, 8):
            factor = jnp.where(sub == k, float(mat[k, (k - r) % 8]), factor)
        out.append(factor)
    return out


def along(xs, tables):
    odd, even = tables
    diff = [xs[b] - xs[7 - b] for b in range(4)]
    both = [xs[b] + xs[7 - b] for b in range(4)]
    out = [None] * 8
    for a in range(4):
        s = float(odd[a, 0]) * diff[0]
        t = float(even[a, 0]) * both[0]
        for b in range(1, 4):
            s = s + float(odd[a, b]) * diff[b]
            t = t + float(even[a, b]) * both[b]
        out[a] = s + t
        out[7 - a] = s - t
    return out


def along_k(x, coef):
    out = coef[0] * x
    for r in range(1, 8):
        out = out + coef[r] * pltpu.roll(x, r, 0)
    return out


def lanes():
    lane = lax.broadcasted_iota(jnp.int32, (8, 128), 1)
    return (lane // 32) % 2, (lane // 16) % 2, lane % 16, lane


def is_set(flags, index):
    return jnp.broadcast_to(flags[index : index + 1, :], (8, 128)) != 0


def rows(j):
    return pl.ds(pl.multiple_of(8 * j, 8), 8)


def pack_low(face0, face1, first, shift):
    return jnp.where(first, face0, pltpu.roll(face1, shift, 1))


def pack_high(face0, face1, first, shift):
    return jnp.where(first, pltpu.roll(face1, 128 - shift, 1), face0)


def unpack_high(got, first, shift):
    zero = jnp.zeros_like(got)
    return jnp.where(first, zero, pltpu.roll(got, shift, 1)), jnp.where(first, zero, got)


def unpack_low(got, first, shift):
    zero = jnp.zeros_like(got)
    return jnp.where(first, pltpu.roll(got, 128 - shift, 1), zero), jnp.where(first, got, zero)


def received(even, odd, parity, has_low, has_high):
    zero = jnp.zeros_like(even)
    low = jnp.where(has_low, jnp.where(parity, even, odd), zero)
    high = jnp.where(has_high, jnp.where(parity, odd, even), zero)
    return low, high


def assemble_local(u, flags, send_e, send_o, y_low, y_high):
    X, Y, Z, _ = lanes()
    x0, y0 = X == 0, Y == 0
    for t in range(2):
        for i in range(8):
            low = u[t, i, pl.ds(0, 8, 8), :]
            high = u[t, i, pl.ds(7, 8, 8), :]
            u[t, i, pl.ds(0, 8, 8), :] = low + jnp.where(Z > 0, pltpu.roll(high, 1, 1), 0.0)
            u[t, i, pl.ds(7, 8, 8), :] = high + jnp.where(Z < 15, pltpu.roll(low, 127, 1), 0.0)
    for t in range(2):
        for i in range(8):
            low = u[t, i, 0:8, :]
            high = u[t, i, 56:64, :]
            u[t, i, 0:8, :] = low + jnp.where(y0, 0.0, pltpu.roll(high, 16, 1))
            u[t, i, 56:64, :] = high + jnp.where(y0, pltpu.roll(low, 112, 1), 0.0)
    parity = is_set(flags, 0)
    for j in range(8):
        at = slice(8 * j, 8 * j + 8)
        lows, highs = [], []
        for t in range(2):
            low = u[t, 0, at, :]
            high = u[t, 7, at, :]
            lows.append(low + jnp.where(x0, 0.0, pltpu.roll(high, 32, 1)))
            highs.append(high + jnp.where(x0, pltpu.roll(low, 96, 1), 0.0))
            u[t, 0, at, :] = lows[t]
            u[t, 7, at, :] = highs[t]
        to_low = pack_low(lows[0], lows[1], x0, 32)
        to_high = pack_high(highs[0], highs[1], x0, 32)
        send_e[at, :] = jnp.where(parity, to_low, to_high)
        send_o[at, :] = jnp.where(parity, to_high, to_low)
    for i in range(8):
        at = slice(8 * i, 8 * i + 8)
        y_low[at, :] = pack_low(u[0, i, 0:8, :], u[1, i, 0:8, :], y0, 16)
        y_high[at, :] = pack_high(u[0, i, 56:64, :], u[1, i, 56:64, :], y0, 16)


def thirds(x):
    high = x.astype(jnp.bfloat16)
    rest = x - high.astype(f32)
    mid = rest.astype(jnp.bfloat16)
    low = (rest - mid.astype(f32)).astype(jnp.bfloat16)
    return [high, mid, low]


def pick_table(flags):
    return (lax.broadcasted_iota(jnp.int32, (128, 128), 0) == flags[8:9, :]).astype(f32).T


def place(parts, table):
    rows_in = jnp.concatenate(parts, axis=0)
    tables = jnp.concatenate([table.astype(jnp.bfloat16)] * len(parts), axis=0)
    out = lax.dot_general(rows_in, tables, (((0,), (0,)), ((), ())), preferred_element_type=f32)
    return out.reshape(8, 64, 128)


def weight_k():
    sub = lax.broadcasted_iota(jnp.int32, (8, 128), 0)
    wk = jnp.zeros((8, 128), f32)
    for k in range(8):
        wk = jnp.where(sub == k, WMAX[k], wk)
    return wk


def coef_kernel(flags, dif, coef):
    pick = pick_table(flags)
    over = pick[0:64, :] + pick[64:128, :]
    wk = weight_k()
    for m in range(3):
        coef[m] = place(thirds(dif[m]), over)
        for i in range(8):
            for j in range(8):
                at = slice(8 * j, 8 * j + 8)
                coef[m, i, at, :] = coef[m, i, at, :] * (wk * (WMAX[i] * WMAX[j] * DT))


def setup_kernel(flags, adj_hbm, vel_hbm, jac_hbm, mass, u, roll_ref, send_e, send_o, y_low, y_high, a, v, di, dj, dk, adj, vel, jac, sems):
    copies = [pltpu.make_async_copy(adj_hbm.at[c], adj.at[c], sems.at[c]) for c in range(3)]
    copies += [pltpu.make_async_copy(vel_hbm.at[c], vel.at[c], sems.at[3 + c]) for c in range(3)]
    copies.append(pltpu.make_async_copy(jac_hbm, jac, sems.at[6]))
    for copy in copies:
        copy.start()
    _, _, _, lane = lanes()
    pick = pick_table(flags)
    over = pick[0:64, :] + pick[64:128, :]
    wk = weight_k()
    for copy in copies[:3]:
        copy.wait()
    a[0] = place(thirds(jnp.concatenate([adj[0], adj[1]], axis=0)), pick)
    a[1] = place(thirds(adj[2]), over)
    kf = roll_factors(DMAT)
    for r, factor in enumerate(kf + roll_factors(DMAT.T)):
        roll_ref[r] = factor

    def planes(n, carry):
        t, j = n // 8, n % 8
        xs = [a[t, i, rows(j), :] for i in range(8)]
        out = along(xs, FWD)
        for i in range(8):
            di[t, i, rows(j), :] = out[i]
            dk[t, i, rows(j), :] = along_k(xs[i], kf)
        return carry

    lax.fori_loop(0, 16, planes, 0)

    def columns(n, carry):
        t, i = n // 8, n % 8
        out = along([a[t, i, 8 * j : 8 * j + 8, :] for j in range(8)], FWD)
        for j in range(8):
            dj[t, i, 8 * j : 8 * j + 8, :] = out[j]
        return carry

    lax.fori_loop(0, 16, columns, 0)
    for copy in copies[3:]:
        copy.wait()
    v[0] = place([jnp.concatenate([vel[0], vel[1]], axis=0)], pick)
    v[1] = place([vel[2]], over)
    mass[...] = place(thirds(jac[...]), over)
    left = lane < 64
    sign = jnp.where(left, 1.0, -1.0)

    def other(x):
        return pltpu.roll(x, 64, 1)

    def cross(i, carry):
        index = jnp.full((8, 128), i, jnp.int32)
        wi = jnp.zeros((8, 128), f32)
        for n in range(8):
            wi = jnp.where(index == n, WMAX[n], wi)
        wi = wk * wi
        for j in range(8):
            at = slice(8 * j, 8 * j + 8)
            swapped = other(dk[0, i, at, :])
            r_a = jnp.where(left, dj[1, i, at, :] - swapped, swapped - di[1, i, at, :])
            mixed = jnp.where(left, dj[0, i, at, :], di[0, i, at, :])
            r_b = sign * (other(mixed) - mixed)
            v_a, v_b = v[0, i, at, :], v[1, i, at, :]
            s_a = sign * (other(v_a) * r_b - v_b * other(r_a))
            prod = v_a * other(r_a)
            s_b = sign * (prod - other(prod))
            m = mass[i, at, :] * (wi * WMAX[j])
            mass[i, at, :] = m
            u[0, i, at, :] = m * (a[0, i, at, :] + DT * s_a)
            u[1, i, at, :] = m * (a[1, i, at, :] + DT * s_b)
        return carry

    lax.fori_loop(0, 8, cross, 0)
    assemble_local(u, flags, send_e, send_o, y_low, y_high)


def mid_kernel(flags, got_e, got_o, y_low, y_high, _, send_e, send_o):
    X, Y, _, _ = lanes()
    x0, y0 = X == 0, Y == 0
    lows, highs = [], []
    for i in range(8):
        lows.append(y_low[8 * i : 8 * i + 8, :])
        highs.append(y_high[8 * i : 8 * i + 8, :])
    for j, into, pack in ((0, lows, pack_low), (7, highs, pack_high)):
        at = slice(8 * j, 8 * j + 8)
        low, high = received(got_e[at, :], got_o[at, :], is_set(flags, 0), is_set(flags, 2), is_set(flags, 3))
        into[0] = into[0] + pack(*unpack_low(low, x0, 32), y0, 16)
        into[7] = into[7] + pack(*unpack_high(high, x0, 32), y0, 16)
    parity = is_set(flags, 1)
    for i in range(8):
        send_e[8 * i : 8 * i + 8, :] = jnp.where(parity, lows[i], highs[i])
        send_o[8 * i : 8 * i + 8, :] = jnp.where(parity, highs[i], lows[i])


def main_kernel(step):
    def kernel(*refs):
        if step == 0:
            u, mass, coef, roll_ref, v, y = refs
        else:
            flags, u, before, mass, coef, roll_ref, v, y, stored = refs
            store(flags, before, stored)

        def planes(n, carry):
            t, j = n // 8, n % 8
            if step == 0:
                xs = [u[t, i, rows(j), :] for i in range(8)]
            else:
                xs = [SCALE * u[t, i, rows(j), :] - before[t, i, rows(j), :] for i in range(8)]
            flux = along(xs, FWD)
            out = along([coef[0, i, rows(j), :] * flux[i] for i in range(8)], BWD)
            for i in range(8):
                v[t, i, rows(j), :] = xs[i]
                part = coef[2, i, rows(j), :] * along_k(xs[i], [roll_ref[r] for r in range(8)])
                part = along_k(part, [roll_ref[8 + r] for r in range(8)])
                y[t, i, rows(j), :] = mass[i, rows(j), :] * xs[i] + out[i] + part
            return carry

        lax.fori_loop(0, 16, planes, 0)

        def columns(n, carry):
            t, i = n // 8, n % 8
            flux = along([v[t, i, 8 * j : 8 * j + 8, :] for j in range(8)], FWD)
            out = along([coef[1, i, 8 * j : 8 * j + 8, :] * flux[j] for j in range(8)], BWD)
            for j in range(8):
                at = slice(8 * j, 8 * j + 8)
                y[t, i, at, :] = y[t, i, at, :] + out[j]
            return carry

        lax.fori_loop(0, 16, columns, 0)

    return kernel


def add_faces(first, axis, got, shift, scale, mass, coef, roll_ref, v, y):
    def at(ref, lead, normal, plane):
        i, j = (normal, plane) if axis == 0 else (plane, normal)
        index = lead + (i, slice(8 * j, 8 * j + 8), slice(None))
        return ref[index], index

    def outer(ref, lead, plane):
        return jnp.where(first, at(ref, lead, 0, plane)[0], at(ref, lead, 7, plane)[0])

    cols = [jnp.where(first, float(DMAT[a, 0]), float(DMAT[a, 7])) for a in range(8)]
    kf = [roll_ref[r] for r in range(8)]
    kb = [roll_ref[8 + r] for r in range(8)]
    for t in range(2):
        face = []
        for low, high in got:
            if t == 0:
                value = jnp.where(first, pltpu.roll(low, 128 - shift, 1), pltpu.roll(high, shift, 1))
            else:
                value = jnp.where(first, low, high)
            face.append(scale * value)
        flux = along(face, FWD)
        inner = along([outer(coef, (1 - axis,), p) * flux[p] for p in range(8)], BWD)
        for p in range(8):
            x = face[p]
            plane = outer(mass, (), p) * x + inner[p]
            plane = plane + along_k(outer(coef, (2,), p) * along_k(x, kf), kb)
            out = along([at(coef, (axis,), a, p)[0] * (cols[a] * x) for a in range(8)], BWD)
            out[0] = out[0] + jnp.where(first, plane, 0.0)
            out[7] = out[7] + jnp.where(first, 0.0, plane)
            for a in range(8):
                value, index = at(y, (t,), a, p)
                y[index] = value + out[a]
            for a, part in ((0, jnp.where(first, x, 0.0)), (7, jnp.where(first, 0.0, x))):
                value, index = at(v, (t,), a, p)
                v[index] = value + part


def x_kernel(step):
    def kernel(flags, xe, xo, mass, coef, roll_ref, v_in, y_in, v, y):
        got = []
        for j in range(8):
            at = slice(8 * j, 8 * j + 8)
            got.append(received(xe[at, :], xo[at, :], is_set(flags, 0), is_set(flags, 2), is_set(flags, 3)))
        add_faces(lanes()[0] == 0, 0, got, 32, SCALE if step else 1.0, mass, coef, roll_ref, v, y)

    return kernel


def y_kernel(step):
    last = step == STEPS - 1
    n_dots = step + 1 + (step == 0)

    def kernel(flags, ye, yo, mass, coef, roll_ref, *refs):
        older = refs[:step]
        if last:
            parts, _, _, v, y, message = refs[step:]
        else:
            _, _, v, y, send_e, send_o, y_low, y_high, dots = refs[step:]
        X, Y, Z, lane = lanes()
        got = []
        for i in range(8):
            at = slice(8 * i, 8 * i + 8)
            got.append(received(ye[at, :], yo[at, :], is_set(flags, 1), is_set(flags, 4), is_set(flags, 5)))
        add_faces(Y == 0, 1, got, 16, SCALE if step else 1.0, mass, coef, roll_ref, v, y)
        if step == 0:
            sub = lax.broadcasted_iota(jnp.int32, (8, 128), 0)
            wz = jnp.where(((Z > 0) & (sub == 0)) | ((Z < 15) & (sub == 7)), 0.5, 1.0)
            wy_low = jnp.where((Y == 1) | is_set(flags, 4), 0.5, 1.0)
            wy_high = jnp.where((Y == 0) | is_set(flags, 5), 0.5, 1.0)
            wx_low = jnp.where((X == 1) | is_set(flags, 2), 0.5, 1.0)
            wx_high = jnp.where((X == 0) | is_set(flags, 3), 0.5, 1.0)

        def products(t):
            def body(i, sums):
                sums = list(sums)
                squares = []
                for j in range(8):
                    at = slice(8 * j, 8 * j + 8)
                    total = y[t, i, at, :]
                    own = v[t, i, at, :]
                    for m in range(step):
                        sums[m] = sums[m] + older[m][t, i, at, :] * total
                    sums[step] = sums[step] + own * total
                    squares.append(own * own)
                if step == 0:
                    index = jnp.full((8, 128), i, jnp.int32)
                    wx = wz * jnp.where(index == 0, wx_low, jnp.where(index == 7, wx_high, 1.0))
                    square = squares[1]
                    for j in range(2, 7):
                        square = square + squares[j]
                    square = square + wy_low * squares[0] + wy_high * squares[7]
                    sums[1] = sums[1] + wx * square
                return tuple(sums)

            return lax.fori_loop(0, 8, body, tuple(jnp.zeros((8, 128), f32) for _ in range(n_dots)))

        sums = [p + 0.5 * q for p, q in zip(products(0), products(1))]
        if not last:
            for m in range(n_dots):
                dots[8 * m : 8 * m + 8, :] = sums[m]
            assemble_local(y, flags, send_e, send_o, y_low, y_high)
            return
        row_of = lax.broadcasted_iota(jnp.int32, (16, 128), 0)
        lane_of = lax.broadcasted_iota(jnp.int32, (16, 128), 1)
        table = jnp.zeros((16, 128), f32)
        every = [parts[8 * m : 8 * m + 8, :] for m in range(7)] + sums
        for m, value in enumerate(every):
            table = jnp.where(row_of == m, jnp.sum(value, axis=0, keepdims=True), table)
        column = jnp.sum(table, axis=1, keepdims=True)
        line = jnp.sum(jnp.where(row_of == lane_of, column, 0.0), axis=0, keepdims=True)
        message[...] = jnp.broadcast_to(line, message.shape)

    return kernel


def store(flags, v, stored):
    pick = pick_table(flags).astype(jnp.bfloat16)
    for t in range(2):
        table = jnp.concatenate([pick if t == 0 else pick[0:64, :]] * 3, axis=1)
        x = jnp.concatenate(thirds(v[t].reshape(512, 128)), axis=1)
        res = lax.dot_general(table, x, (((1,), (1,)), ((), ())), preferred_element_type=f32)
        if t == 0:
            stored[0] = res[0:64, :]
            stored[1] = res[64:128, :]
        else:
            stored[2] = res


def finish_kernel(flags, got, stored0, stored1, stored2, v, out, stored3):
    store(flags, v, stored3)
    stored = (stored0, stored1, stored2, stored3)
    total = jnp.sum(got[...], axis=0, keepdims=True)
    lane = lax.broadcasted_iota(jnp.int32, (1, 128), 1)

    def entry(m):
        return jnp.sum(jnp.where(lane == m, total, 0.0), axis=1, keepdims=True)

    gram = {}
    order = [(0, 0), None, (0, 1), (1, 1), (0, 2), (1, 2), (2, 2), (0, 3), (1, 3), (2, 3), (3, 3)]
    for m, pair in enumerate(order):
        if pair is None:
            square = entry(m)
        else:
            gram[pair] = entry(m)
    right = [square]
    for j in range(3):
        right.append(SCALE * gram[(0, j)] - right[j])
    lower, inverse, reduced = {}, [], []
    for c in range(4):
        pivot = gram[(c, c)]
        value = right[c]
        for m in range(c):
            pivot = pivot - lower[(c, m)] * lower[(c, m)] * inverse[m]
            value = value - lower[(c, m)] * reduced[m] * inverse[m]
        good = pivot > 1e-6 * gram[(c, c)]
        inverse.append(jnp.where(good, 1.0 / jnp.where(good, pivot, 1.0), 0.0))
        reduced.append(value)
        for r in range(c + 1, 4):
            acc = gram[(c, r)]
            for m in range(c):
                acc = acc - lower[(r, m)] * lower[(c, m)] * inverse[m]
            lower[(r, c)] = acc
    weight = [None] * 4
    for c in reversed(range(4)):
        acc = reduced[c]
        for r in range(c + 1, 4):
            acc = acc - lower[(r, c)] * weight[r]
        weight[c] = acc * inverse[c]
    for n in range(3):
        x = weight[0] * stored[0][n]
        for c in range(1, 4):
            x = x + weight[c] * stored[c][n]
        out[n] = x


def swaps(count, odd):
    pairs = []
    for i in range(odd, count, 2):
        pairs += [(i, (i + 1) % count), ((i + 1) % count, i)]
    return pairs


def solution(mesh):
    vmem = pl.BlockSpec(memory_space=pltpu.VMEM)
    params = pltpu.CompilerParams(vmem_limit_bytes=40 * 1024 * 1024)
    sx, sy = mesh.shape["gx"], mesh.shape["gy"]

    def shape(*dims):
        return jax.ShapeDtypeStruct(dims, f32)

    field, face = shape(2, 8, 64, 128), shape(64, 128)

    anywhere = pl.BlockSpec(memory_space=pltpu.HBM)

    def call(kernel, outs, ins, scratch=(), name=None, cost=None, alias=None):
        return pl.pallas_call(
            kernel,
            out_shape=outs,
            in_specs=ins if isinstance(ins, list) else [vmem] * ins,
            out_specs=[vmem] * len(outs),
            scratch_shapes=scratch,
            input_output_aliases=alias or {},
            compiler_params=params,
            cost_estimate=pl.CostEstimate(flops=0, transcendentals=0, bytes_accessed=cost) if cost else None,
            name=name,
        )

    def held(x):
        return pltpu.with_memory_space_constraint(x, pltpu.HBM)

    def local(adjoint_field, velocity, diffusivity, jacobian, element_slot):
        gx, gy = lax.axis_index("gx"), lax.axis_index("gy")
        flags = jnp.stack([gx % 2, gy % 2, gx > 0, gx < sx - 1, gy > 0, gy < sy - 1, gx, gy]).astype(jnp.int32)
        slot = element_slot.reshape(1, 64)
        slot = jnp.broadcast_to(jnp.concatenate([slot, slot + 64], axis=1), (8, 128))
        flags = jnp.concatenate([jnp.broadcast_to(flags[:, None], (8, 128)), slot], axis=0)
        big = pltpu.VMEM((2, 8, 64, 128), f32)
        scratch = [big] * 5 + [
            pltpu.VMEM((3, 64, 512), f32),
            pltpu.VMEM((3, 64, 512), jnp.bfloat16),
            pltpu.VMEM((64, 512), f32),
            pltpu.SemaphoreType.DMA((7,)),
        ]
        mass, u, table, xe, xo, yl, yh = call(
            setup_kernel,
            [shape(8, 64, 128), field, shape(16, 8, 128), face, face, face, face],
            [vmem, anywhere, anywhere, anywhere],
            scratch,
            "setup",
        )(flags, held(adjoint_field.reshape(3, 64, 512)), held(velocity.reshape(3, 64, 512)), held(jacobian.reshape(64, 512)))
        (coef,) = call(coef_kernel, [shape(3, 8, 64, 128)], 2, name="coef", cost=3 << 20)(flags, diffusivity.reshape(3, 64, 512))
        vs, parts, stored = [], [], []
        for step in range(STEPS):
            xe = lax.ppermute(xe, "gx", swaps(sx, 0))
            xo = lax.ppermute(xo, "gx", swaps(sx, 1))
            shared = [mass, coef, table]
            if step == 0:
                v, y = call(main_kernel(step), [field, field], 4, name="main0", cost=8 << 20)(u, *shared)
            else:
                v, y, moved = call(main_kernel(step), [field, field, shape(3, 64, 512)], 6, name=f"main{step}", cost=8 << 20)(flags, u, vs[-1], *shared)
                stored.append(moved)
            ye, yo = call(mid_kernel, [face, face], [vmem] * 5 + [anywhere], name="mid")(flags, xe, xo, yl, yh, y)
            ye = lax.ppermute(ye, "gy", swaps(sy, 0))
            yo = lax.ppermute(yo, "gy", swaps(sy, 1))
            v, y = call(x_kernel(step), [field, field], 8, name=f"xpart{step}", cost=8 << 20, alias={6: 0, 7: 1})(flags, xe, xo, *shared, v, y)
            args = [flags, ye, yo] + shared + vs
            if step < STEPS - 1:
                n_dots = step + 1 + (step == 0)
                n = len(args)
                v, u, xe, xo, yl, yh, dots = call(
                    y_kernel(step), [field, field, face, face, face, face, shape(8 * n_dots, 128)], n + 2, name=f"ypart{step}", alias={n: 0, n + 1: 1}
                )(*args, v, y)
                vs.append(v)
                parts.append(dots)
            else:
                parts = jnp.concatenate(parts, axis=0)
                n = len(args) + 1
                v, _, message = call(y_kernel(step), [field, field, shape(sx * sy, 128)], n + 2, name="ypart3", alias={n: 0, n + 1: 1})(*args, parts, v, y)
        got = lax.all_to_all(message.reshape(sx * sy, 1, 128), ("gx", "gy"), 0, 0).reshape(sx * sy, 128)
        (out,) = call(finish_kernel, [shape(3, 64, 512)], 6, [pltpu.VMEM((3, 64, 512), f32)], name="finish")(flags, got, *stored, v)
        return out.reshape(3, 1, 1, 64, 512)

    in_specs = (
        P(None, "gx", "gy", None, None),
        P(None, "gx", "gy", None, None),
        P(None, "gx", "gy", None, None),
        P("gx", "gy", None, None),
        P("gx", "gy", None),
    )
    return jax.shard_map(local, mesh=mesh, in_specs=in_specs, out_specs=P(None, "gx", "gy", None, None), check_vma=False)
```

```python
import jax
import jax.numpy as jnp
import numpy as np
from jax import lax
from jax.experimental import pallas as pl
from jax.experimental.pallas import tpu as pltpu
from jax.sharding import PartitionSpec as P


STEPS = 4
DT = 0.25
SCALE = 0.5
f32 = jnp.float32


def legendre_seven(points):
    previous = points * 0.0 + 1.0
    current = points
    for degree in range(1, 7):
        following = ((2 * degree + 1) * points * current - degree * previous) / (degree + 1)
        previous = current
        current = following
    return current


def gll_tables():
    poly_order = 7
    points = np.array(
        [
            -1.0,
            -0.8717401485096066,
            -0.5917001814331423,
            -0.2092992179024789,
            0.2092992179024789,
            0.5917001814331423,
            0.8717401485096066,
            1.0,
        ]
    )
    end_values = legendre_seven(points)
    weights = 2.0 / (poly_order * (poly_order + 1) * end_values**2)
    spread = points[:, None] - points[None, :]
    identity = np.eye(poly_order + 1)
    diff_table = end_values[:, None] / (end_values[None, :] * (spread + identity))
    diff_table = diff_table * (1.0 - identity)
    corners = np.zeros(poly_order + 1)
    corners[0] = -poly_order * (poly_order + 1) / 4.0
    corners[-1] = poly_order * (poly_order + 1) / 4.0
    diff_table = diff_table + identity * corners[None, :]
    return (weights.astype(np.float32), diff_table.astype(np.float32))


WEIGHTS, DMAT = gll_tables()
WMAX = [float(w) for w in WEIGHTS]


def halves(mat):
    mat = mat.astype(np.float64)
    assert np.array_equal(mat[::-1, ::-1], -mat)
    odd = 0.5 * (mat[:4, :4] - mat[:4, 7:3:-1])
    even = 0.5 * (mat[:4, :4] + mat[:4, 7:3:-1])
    return odd, even


FWD = halves(DMAT)
BWD = halves(DMAT.T)


def roll_factors(mat):
    sub = lax.broadcasted_iota(jnp.int32, (8, 128), 0)
    out = []
    for r in range(8):
        factor = jnp.full((8, 128), float(mat[0, -r % 8]), f32)
        for k in range(1, 8):
            factor = jnp.where(sub == k, float(mat[k, (k - r) % 8]), factor)
        out.append(factor)
    return out


def along(xs, tables):
    odd, even = tables
    diff = [xs[b] - xs[7 - b] for b in range(4)]
    both = [xs[b] + xs[7 - b] for b in range(4)]
    out = [None] * 8
    for a in range(4):
        s = float(odd[a, 0]) * diff[0]
        t = float(even[a, 0]) * both[0]
        for b in range(1, 4):
            s = s + float(odd[a, b]) * diff[b]
            t = t + float(even[a, b]) * both[b]
        out[a] = s + t
        out[7 - a] = s - t
    return out


def along_k(x, coef):
    out = coef[0] * x
    for r in range(1, 8):
        out = out + coef[r] * pltpu.roll(x, r, 0)
    return out


def lanes():
    lane = lax.broadcasted_iota(jnp.int32, (8, 128), 1)
    return (lane // 32) % 2, (lane // 16) % 2, lane % 16, lane


def is_set(flags, index):
    return jnp.broadcast_to(flags[index : index + 1, :], (8, 128)) != 0


def rows(j):
    return pl.ds(pl.multiple_of(8 * j, 8), 8)


def pack_low(face0, face1, first, shift):
    return jnp.where(first, face0, pltpu.roll(face1, shift, 1))


def pack_high(face0, face1, first, shift):
    return jnp.where(first, pltpu.roll(face1, 128 - shift, 1), face0)


def unpack_high(got, first, shift):
    zero = jnp.zeros_like(got)
    return jnp.where(first, zero, pltpu.roll(got, shift, 1)), jnp.where(first, zero, got)


def unpack_low(got, first, shift):
    zero = jnp.zeros_like(got)
    return jnp.where(first, pltpu.roll(got, 128 - shift, 1), zero), jnp.where(first, got, zero)


def received(even, odd, parity, has_low, has_high):
    zero = jnp.zeros_like(even)
    low = jnp.where(has_low, jnp.where(parity, even, odd), zero)
    high = jnp.where(has_high, jnp.where(parity, odd, even), zero)
    return low, high


def send_x(lows, highs, x0, parity, sends, at):
    to_low = pack_low(lows[0], lows[1], x0, 32)
    to_high = pack_high(highs[0], highs[1], x0, 32)
    sends[0][at, :] = jnp.where(parity, to_low, to_high)
    sends[1][at, :] = jnp.where(parity, to_high, to_low)


def assemble_local(u, flags, sends, y_low, y_high):
    X, Y, Z, _ = lanes()
    x0, y0 = X == 0, Y == 0
    for t in range(2):
        for i in range(8):
            low = u[t, i, pl.ds(0, 8, 8), :]
            high = u[t, i, pl.ds(7, 8, 8), :]
            u[t, i, pl.ds(0, 8, 8), :] = low + jnp.where(Z > 0, pltpu.roll(high, 1, 1), 0.0)
            u[t, i, pl.ds(7, 8, 8), :] = high + jnp.where(Z < 15, pltpu.roll(low, 127, 1), 0.0)
    for t in range(2):
        for i in range(8):
            low = u[t, i, 0:8, :]
            high = u[t, i, 56:64, :]
            u[t, i, 0:8, :] = low + jnp.where(y0, 0.0, pltpu.roll(high, 16, 1))
            u[t, i, 56:64, :] = high + jnp.where(y0, pltpu.roll(low, 112, 1), 0.0)
    parity = is_set(flags, 0)
    for j in range(8):
        at = slice(8 * j, 8 * j + 8)
        lows, highs = [], []
        for t in range(2):
            low = u[t, 0, at, :]
            high = u[t, 7, at, :]
            lows.append(low + jnp.where(x0, 0.0, pltpu.roll(high, 32, 1)))
            highs.append(high + jnp.where(x0, pltpu.roll(low, 96, 1), 0.0))
            u[t, 0, at, :] = lows[t]
            u[t, 7, at, :] = highs[t]
        if sends:
            send_x(lows, highs, x0, parity, sends, at)
    for i in range(8):
        at = slice(8 * i, 8 * i + 8)
        y_low[at, :] = pack_low(u[0, i, 0:8, :], u[1, i, 0:8, :], y0, 16)
        y_high[at, :] = pack_high(u[0, i, 56:64, :], u[1, i, 56:64, :], y0, 16)


def thirds(x):
    high = x.astype(jnp.bfloat16)
    rest = x - high.astype(f32)
    mid = rest.astype(jnp.bfloat16)
    low = (rest - mid.astype(f32)).astype(jnp.bfloat16)
    return [high, mid, low]


def pick_table(flags):
    return (lax.broadcasted_iota(jnp.int32, (128, 128), 0) == flags[8:9, :]).astype(f32).T


def place(parts, table):
    rows_in = jnp.concatenate(parts, axis=0)
    tables = jnp.concatenate([table.astype(jnp.bfloat16)] * len(parts), axis=0)
    out = lax.dot_general(rows_in, tables, (((0,), (0,)), ((), ())), preferred_element_type=f32)
    return out.reshape(8, 64, 128)


def weight_k():
    sub = lax.broadcasted_iota(jnp.int32, (8, 128), 0)
    wk = jnp.zeros((8, 128), f32)
    for k in range(8):
        wk = jnp.where(sub == k, WMAX[k], wk)
    return wk


def coef_kernel(flags, dif, coef):
    pick = pick_table(flags)
    over = pick[0:64, :] + pick[64:128, :]
    wk = weight_k()
    for m in range(3):
        coef[m] = place(thirds(dif[m]), over)
        for i in range(8):
            for j in range(8):
                at = slice(8 * j, 8 * j + 8)
                coef[m, i, at, :] = coef[m, i, at, :] * (wk * (WMAX[i] * WMAX[j] * DT))


def setup_kernel(flags, adj_hbm, vel_hbm, jac_hbm, mass, u, roll_ref, send_e, send_o, y_low, y_high, a, v, di, dj, dk, adj, vel, jac, sems):
    copies = [pltpu.make_async_copy(adj_hbm.at[c], adj.at[c], sems.at[c]) for c in range(3)]
    copies += [pltpu.make_async_copy(vel_hbm.at[c], vel.at[c], sems.at[3 + c]) for c in range(3)]
    copies.append(pltpu.make_async_copy(jac_hbm, jac, sems.at[6]))
    for copy in copies:
        copy.start()
    _, _, _, lane = lanes()
    pick = pick_table(flags)
    over = pick[0:64, :] + pick[64:128, :]
    wk = weight_k()
    for copy in copies[:3]:
        copy.wait()
    a[0] = place(thirds(jnp.concatenate([adj[0], adj[1]], axis=0)), pick)
    a[1] = place(thirds(adj[2]), over)
    kf = roll_factors(DMAT)
    for r, factor in enumerate(kf + roll_factors(DMAT.T)):
        roll_ref[r] = factor

    def planes(n, carry):
        t, j = n // 8, n % 8
        xs = [a[t, i, rows(j), :] for i in range(8)]
        out = along(xs, FWD)
        for i in range(8):
            di[t, i, rows(j), :] = out[i]
            dk[t, i, rows(j), :] = along_k(xs[i], kf)
        return carry

    lax.fori_loop(0, 16, planes, 0)

    def columns(n, carry):
        t, i = n // 8, n % 8
        out = along([a[t, i, 8 * j : 8 * j + 8, :] for j in range(8)], FWD)
        for j in range(8):
            dj[t, i, 8 * j : 8 * j + 8, :] = out[j]
        return carry

    lax.fori_loop(0, 16, columns, 0)
    for copy in copies[3:]:
        copy.wait()
    v[0] = place([jnp.concatenate([vel[0], vel[1]], axis=0)], pick)
    v[1] = place([vel[2]], over)
    mass[...] = place(thirds(jac[...]), over)
    left = lane < 64
    sign = jnp.where(left, 1.0, -1.0)

    def other(x):
        return pltpu.roll(x, 64, 1)

    def cross(i, carry):
        index = jnp.full((8, 128), i, jnp.int32)
        wi = jnp.zeros((8, 128), f32)
        for n in range(8):
            wi = jnp.where(index == n, WMAX[n], wi)
        wi = wk * wi
        for j in range(8):
            at = slice(8 * j, 8 * j + 8)
            swapped = other(dk[0, i, at, :])
            r_a = jnp.where(left, dj[1, i, at, :] - swapped, swapped - di[1, i, at, :])
            mixed = jnp.where(left, dj[0, i, at, :], di[0, i, at, :])
            r_b = sign * (other(mixed) - mixed)
            v_a, v_b = v[0, i, at, :], v[1, i, at, :]
            s_a = sign * (other(v_a) * r_b - v_b * other(r_a))
            prod = v_a * other(r_a)
            s_b = sign * (prod - other(prod))
            m = mass[i, at, :] * (wi * WMAX[j])
            mass[i, at, :] = m
            u[0, i, at, :] = m * (a[0, i, at, :] + DT * s_a)
            u[1, i, at, :] = m * (a[1, i, at, :] + DT * s_b)
        return carry

    lax.fori_loop(0, 8, cross, 0)
    assemble_local(u, flags, (send_e, send_o), y_low, y_high)


def mid_kernel(flags, got_e, got_o, y_low, y_high, _, send_e, send_o):
    X, Y, _, _ = lanes()
    x0, y0 = X == 0, Y == 0
    lows, highs = [], []
    for i in range(8):
        lows.append(y_low[8 * i : 8 * i + 8, :])
        highs.append(y_high[8 * i : 8 * i + 8, :])
    for j, into, pack in ((0, lows, pack_low), (7, highs, pack_high)):
        at = slice(8 * j, 8 * j + 8)
        low, high = received(got_e[at, :], got_o[at, :], is_set(flags, 0), is_set(flags, 2), is_set(flags, 3))
        into[0] = into[0] + pack(*unpack_low(low, x0, 32), y0, 16)
        into[7] = into[7] + pack(*unpack_high(high, x0, 32), y0, 16)
    parity = is_set(flags, 1)
    for i in range(8):
        send_e[8 * i : 8 * i + 8, :] = jnp.where(parity, lows[i], highs[i])
        send_o[8 * i : 8 * i + 8, :] = jnp.where(parity, highs[i], lows[i])


def main_kernel(step):
    def kernel(*refs):
        if step == 0:
            u, mass, coef, roll_ref, v, y = refs
        else:
            flags, u, before, mass, coef, roll_ref, v, y, stored = refs
            store(flags, before, stored)

        def planes(n, carry):
            t, j = n // 8, n % 8
            if step == 0:
                xs = [u[t, i, rows(j), :] for i in range(8)]
            else:
                xs = [SCALE * u[t, i, rows(j), :] - before[t, i, rows(j), :] for i in range(8)]
            flux = along(xs, FWD)
            out = along([coef[0, i, rows(j), :] * flux[i] for i in range(8)], BWD)
            for i in range(8):
                v[t, i, rows(j), :] = xs[i]
                part = coef[2, i, rows(j), :] * along_k(xs[i], [roll_ref[r] for r in range(8)])
                part = along_k(part, [roll_ref[8 + r] for r in range(8)])
                y[t, i, rows(j), :] = mass[i, rows(j), :] * xs[i] + out[i] + part
            return carry

        lax.fori_loop(0, 16, planes, 0)

        def columns(n, carry):
            t, i = n // 8, n % 8
            flux = along([v[t, i, 8 * j : 8 * j + 8, :] for j in range(8)], FWD)
            out = along([coef[1, i, 8 * j : 8 * j + 8, :] * flux[j] for j in range(8)], BWD)
            for j in range(8):
                at = slice(8 * j, 8 * j + 8)
                y[t, i, at, :] = y[t, i, at, :] + out[j]
            return carry

        lax.fori_loop(0, 16, columns, 0)

    return kernel


def plane_at(axis, lead, normal, plane):
    i, j = (normal, plane) if axis == 0 else (plane, normal)
    return lead + (i, slice(8 * j, 8 * j + 8), slice(None))


def outer_faces(first, got, shift, scale, t):
    if t == 0:
        return [scale * jnp.where(first, pltpu.roll(low, 128 - shift, 1), pltpu.roll(high, shift, 1)) for low, high in got]
    return [scale * jnp.where(first, low, high) for low, high in got]


def face_operator(first, axis, face, planes, mass, coef, roll_ref):
    def outer(ref, lead, plane):
        return jnp.where(first, ref[plane_at(axis, lead, 0, plane)], ref[plane_at(axis, lead, 7, plane)])

    cols = [jnp.where(first, float(DMAT[a, 0]), float(DMAT[a, 7])) for a in range(8)]
    kf = [roll_ref[r] for r in range(8)]
    kb = [roll_ref[8 + r] for r in range(8)]
    flux = along(face, FWD)
    inner = along([outer(coef, (1 - axis,), p) * flux[p] for p in range(8)], BWD)
    for p in planes:
        x = face[p]
        plane = outer(mass, (), p) * x + inner[p]
        plane = plane + along_k(outer(coef, (2,), p) * along_k(x, kf), kb)
        out = along([coef[plane_at(axis, (axis,), a, p)] * (cols[a] * x) for a in range(8)], BWD)
        out[0] = out[0] + jnp.where(first, plane, 0.0)
        out[7] = out[7] + jnp.where(first, 0.0, plane)
        yield p, out


def add_values(first, axis, face, t, v):
    for p in range(8):
        for a, part in ((0, jnp.where(first, face[p], 0.0)), (7, jnp.where(first, 0.0, face[p]))):
            index = plane_at(axis, (t,), a, p)
            v[index] = v[index] + part


def got_from(flags, even, odd, axis):
    out = []
    for p in range(8):
        at = slice(8 * p, 8 * p + 8)
        out.append(received(even[at, :], odd[at, :], is_set(flags, axis), is_set(flags, 2 + 2 * axis), is_set(flags, 3 + 2 * axis)))
    return out


def x_kernel(step):
    def kernel(flags, xe, xo, mass, coef, roll_ref, y_in, y):
        first = lanes()[0] == 0
        got = got_from(flags, xe, xo, 0)
        for t in range(2):
            face = outer_faces(first, got, 32, SCALE if step else 1.0, t)
            for p, out in face_operator(first, 0, face, range(8), mass, coef, roll_ref):
                for a in range(8):
                    index = plane_at(0, (t,), a, p)
                    y[index] = y_in[index] + out[a]

    return kernel


def edge_kernel(step):
    def kernel(flags, ye, yo, mass, coef, roll_ref, y_in, send_e, send_o, e):
        X, Y, Z, _ = lanes()
        x0, y0 = X == 0, Y == 0
        got = got_from(flags, ye, yo, 1)
        for t in range(2):
            face = outer_faces(y0, got, 16, SCALE if step else 1.0, t)
            for p, out in face_operator(y0, 1, face, (0, 7), mass, coef, roll_ref):
                for a in range(8):
                    at = slice(8 * a, 8 * a + 8)
                    e[t, p // 7, at, :] = y_in[t, p, at, :] + out[a]
        for t in range(2):
            for q in range(2):
                low = e[t, q, pl.ds(0, 8, 8), :]
                high = e[t, q, pl.ds(7, 8, 8), :]
                e[t, q, pl.ds(0, 8, 8), :] = low + jnp.where(Z > 0, pltpu.roll(high, 1, 1), 0.0)
                e[t, q, pl.ds(7, 8, 8), :] = high + jnp.where(Z < 15, pltpu.roll(low, 127, 1), 0.0)
        ends = {}
        for t in range(2):
            for q in range(2):
                low = e[t, q, 0:8, :]
                high = e[t, q, 56:64, :]
                ends[t, q, 0] = low + jnp.where(y0, 0.0, pltpu.roll(high, 16, 1))
                ends[t, q, 7] = high + jnp.where(y0, pltpu.roll(low, 112, 1), 0.0)
        parity = is_set(flags, 0)
        for j in range(8):
            at = slice(8 * j, 8 * j + 8)
            lows, highs = [], []
            for t in range(2):
                low, high = (ends[t, q, j] if j in (0, 7) else e[t, q, at, :] for q in range(2))
                lows.append(low + jnp.where(x0, 0.0, pltpu.roll(high, 32, 1)))
                highs.append(high + jnp.where(x0, pltpu.roll(low, 96, 1), 0.0))
            send_x(lows, highs, x0, parity, (send_e, send_o), at)

    return kernel


def y_kernel(step):
    last = step == STEPS - 1
    n_dots = step + 1 + (step == 0)

    def kernel(flags, xe, xo, ye, yo, mass, coef, roll_ref, *refs):
        older = refs[:step]
        if last:
            parts, v_in, y_in, v, message, y = refs[step:]
        else:
            v_in, y_in, v, y, y_low, y_high, dots = refs[step:]
        X, Y, Z, lane = lanes()
        scale = SCALE if step else 1.0
        for t in range(2):
            for i in range(8):
                for j in range(8):
                    index = plane_at(0, (t,), i, j)
                    v[index] = v_in[index]
        got_x, got_y = got_from(flags, xe, xo, 0), got_from(flags, ye, yo, 1)
        for t in range(2):
            add_values(X == 0, 0, outer_faces(X == 0, got_x, 32, scale, t), t, v)
            face = outer_faces(Y == 0, got_y, 16, scale, t)
            add_values(Y == 0, 1, face, t, v)
            for p, out in face_operator(Y == 0, 1, face, range(8), mass, coef, roll_ref):
                for a in range(8):
                    index = plane_at(1, (t,), a, p)
                    y[index] = y_in[index] + out[a]
        if step == 0:
            sub = lax.broadcasted_iota(jnp.int32, (8, 128), 0)
            wz = jnp.where(((Z > 0) & (sub == 0)) | ((Z < 15) & (sub == 7)), 0.5, 1.0)
            wy_low = jnp.where((Y == 1) | is_set(flags, 4), 0.5, 1.0)
            wy_high = jnp.where((Y == 0) | is_set(flags, 5), 0.5, 1.0)
            wx_low = jnp.where((X == 1) | is_set(flags, 2), 0.5, 1.0)
            wx_high = jnp.where((X == 0) | is_set(flags, 3), 0.5, 1.0)

        def products(t):
            def body(i, sums):
                sums = list(sums)
                squares = []
                for j in range(8):
                    at = slice(8 * j, 8 * j + 8)
                    total = y[t, i, at, :]
                    own = v[t, i, at, :]
                    for m in range(step):
                        sums[m] = sums[m] + older[m][t, i, at, :] * total
                    sums[step] = sums[step] + own * total
                    squares.append(own * own)
                if step == 0:
                    index = jnp.full((8, 128), i, jnp.int32)
                    wx = wz * jnp.where(index == 0, wx_low, jnp.where(index == 7, wx_high, 1.0))
                    square = squares[1]
                    for j in range(2, 7):
                        square = square + squares[j]
                    square = square + wy_low * squares[0] + wy_high * squares[7]
                    sums[1] = sums[1] + wx * square
                return tuple(sums)

            return lax.fori_loop(0, 8, body, tuple(jnp.zeros((8, 128), f32) for _ in range(n_dots)))

        sums = [p + 0.5 * q for p, q in zip(products(0), products(1))]
        if not last:
            for m in range(n_dots):
                dots[8 * m : 8 * m + 8, :] = sums[m]
            assemble_local(y, flags, None, y_low, y_high)
            return
        row_of = lax.broadcasted_iota(jnp.int32, (16, 128), 0)
        lane_of = lax.broadcasted_iota(jnp.int32, (16, 128), 1)
        table = jnp.zeros((16, 128), f32)
        every = [parts[8 * m : 8 * m + 8, :] for m in range(7)] + sums
        for m, value in enumerate(every):
            table = jnp.where(row_of == m, jnp.sum(value, axis=0, keepdims=True), table)
        column = jnp.sum(table, axis=1, keepdims=True)
        line = jnp.sum(jnp.where(row_of == lane_of, column, 0.0), axis=0, keepdims=True)
        message[...] = jnp.broadcast_to(line, message.shape)

    return kernel


def store(flags, v, stored):
    pick = pick_table(flags).astype(jnp.bfloat16)
    for t in range(2):
        table = jnp.concatenate([pick if t == 0 else pick[0:64, :]] * 3, axis=1)
        x = jnp.concatenate(thirds(v[t].reshape(512, 128)), axis=1)
        res = lax.dot_general(table, x, (((1,), (1,)), ((), ())), preferred_element_type=f32)
        if t == 0:
            stored[0] = res[0:64, :]
            stored[1] = res[64:128, :]
        else:
            stored[2] = res


def finish_kernel(flags, got, stored0, stored1, stored2, v, out, stored3):
    store(flags, v, stored3)
    stored = (stored0, stored1, stored2, stored3)
    total = jnp.sum(got[...], axis=0, keepdims=True)
    lane = lax.broadcasted_iota(jnp.int32, (1, 128), 1)

    def entry(m):
        return jnp.sum(jnp.where(lane == m, total, 0.0), axis=1, keepdims=True)

    gram = {}
    order = [(0, 0), None, (0, 1), (1, 1), (0, 2), (1, 2), (2, 2), (0, 3), (1, 3), (2, 3), (3, 3)]
    for m, pair in enumerate(order):
        if pair is None:
            square = entry(m)
        else:
            gram[pair] = entry(m)
    right = [square]
    for j in range(3):
        right.append(SCALE * gram[(0, j)] - right[j])
    lower, inverse, reduced = {}, [], []
    for c in range(4):
        pivot = gram[(c, c)]
        value = right[c]
        for m in range(c):
            pivot = pivot - lower[(c, m)] * lower[(c, m)] * inverse[m]
            value = value - lower[(c, m)] * reduced[m] * inverse[m]
        good = pivot > 1e-6 * gram[(c, c)]
        inverse.append(jnp.where(good, 1.0 / jnp.where(good, pivot, 1.0), 0.0))
        reduced.append(value)
        for r in range(c + 1, 4):
            acc = gram[(c, r)]
            for m in range(c):
                acc = acc - lower[(r, m)] * lower[(c, m)] * inverse[m]
            lower[(r, c)] = acc
    weight = [None] * 4
    for c in reversed(range(4)):
        acc = reduced[c]
        for r in range(c + 1, 4):
            acc = acc - lower[(r, c)] * weight[r]
        weight[c] = acc * inverse[c]
    for n in range(3):
        x = weight[0] * stored[0][n]
        for c in range(1, 4):
            x = x + weight[c] * stored[c][n]
        out[n] = x


def swaps(sx, sy, along_x, odd):
    pairs = []
    for g in range(sx):
        for h in range(sy):
            at, count = (g, sx) if along_x else (h, sy)
            other = at + 1 if at % 2 == odd else at - 1
            if along_x:
                to = (other, h) if 0 <= other < count else (g, h ^ 1)
            else:
                to = (g, other) if 0 <= other < count else (g ^ 1, h)
            pairs.append((g * sy + h, to[0] * sy + to[1]))
    return pairs


def solution(mesh):
    vmem = pl.BlockSpec(memory_space=pltpu.VMEM)
    params = pltpu.CompilerParams(vmem_limit_bytes=40 * 1024 * 1024)
    sx, sy = mesh.shape["gx"], mesh.shape["gy"]

    def shape(*dims):
        return jax.ShapeDtypeStruct(dims, f32)

    field, face = shape(2, 8, 64, 128), shape(64, 128)

    anywhere = pl.BlockSpec(memory_space=pltpu.HBM)

    def call(kernel, outs, ins, scratch=(), name=None, cost=None):
        return pl.pallas_call(
            kernel,
            out_shape=outs,
            in_specs=ins if isinstance(ins, list) else [vmem] * ins,
            out_specs=[vmem] * len(outs),
            scratch_shapes=scratch,
            compiler_params=params,
            cost_estimate=pl.CostEstimate(flops=0, transcendentals=0, bytes_accessed=cost) if cost else None,
            name=name,
        )

    def held(x):
        return pltpu.with_memory_space_constraint(x, pltpu.HBM)

    def local(adjoint_field, velocity, diffusivity, jacobian, element_slot):
        gx, gy = lax.axis_index("gx"), lax.axis_index("gy")
        flags = jnp.stack([gx % 2, gy % 2, gx > 0, gx < sx - 1, gy > 0, gy < sy - 1, gx, gy]).astype(jnp.int32)
        slot = element_slot.reshape(1, 64)
        slot = jnp.broadcast_to(jnp.concatenate([slot, slot + 64], axis=1), (8, 128))
        flags = jnp.concatenate([jnp.broadcast_to(flags[:, None], (8, 128)), slot], axis=0)
        big = pltpu.VMEM((2, 8, 64, 128), f32)
        scratch = [big] * 5 + [
            pltpu.VMEM((3, 64, 512), f32),
            pltpu.VMEM((3, 64, 512), jnp.bfloat16),
            pltpu.VMEM((64, 512), f32),
            pltpu.SemaphoreType.DMA((7,)),
        ]
        mass, u, table, xe, xo, yl, yh = call(
            setup_kernel,
            [shape(8, 64, 128), field, shape(16, 8, 128), face, face, face, face],
            [vmem, anywhere, anywhere, anywhere],
            scratch,
            "setup",
        )(flags, held(adjoint_field.reshape(3, 64, 512)), held(velocity.reshape(3, 64, 512)), held(jacobian.reshape(64, 512)))
        (coef,) = call(coef_kernel, [shape(3, 8, 64, 128)], 2, name="coef", cost=3 << 20)(flags, diffusivity.reshape(3, 64, 512))
        vs, parts, stored = [], [], []
        for step in range(STEPS):
            xe = lax.ppermute(xe, ("gx", "gy"), swaps(sx, sy, True, 0))
            xo = lax.ppermute(xo, ("gx", "gy"), swaps(sx, sy, True, 1))
            shared = [mass, coef, table]
            if step == 0:
                v, y = call(main_kernel(step), [field, field], 4, name="main0", cost=8 << 20)(u, *shared)
            else:
                v, y, moved = call(main_kernel(step), [field, field, shape(3, 64, 512)], 6, name=f"main{step}", cost=8 << 20)(flags, u, vs[-1], *shared)
                stored.append(moved)
            ye, yo = call(mid_kernel, [face, face], [vmem] * 5 + [anywhere], name="mid")(flags, xe, xo, yl, yh, y)
            ye = lax.ppermute(ye, ("gx", "gy"), swaps(sx, sy, False, 0))
            yo = lax.ppermute(yo, ("gx", "gy"), swaps(sx, sy, False, 1))
            (y,) = call(x_kernel(step), [field], 7, name=f"xpart{step}", cost=8 << 20)(flags, xe, xo, *shared, y)
            args = [flags, xe, xo, ye, yo] + shared + vs
            if step < STEPS - 1:
                xe, xo = call(edge_kernel(step), [face, face], 7, [pltpu.VMEM((2, 2, 64, 128), f32)], f"edge{step}")(flags, ye, yo, *shared, y)
                n_dots = step + 1 + (step == 0)
                v, u, yl, yh, dots = call(
                    y_kernel(step), [field, field, face, face, shape(8 * n_dots, 128)], len(args) + 2, name=f"ypart{step}", cost=8 << 20
                )(*args, v, y)
                vs.append(v)
                parts.append(dots)
            else:
                parts = jnp.concatenate(parts, axis=0)
                v, message = call(y_kernel(step), [field, shape(sx * sy, 128)], len(args) + 3, [big], "ypart3")(*args, parts, v, y)
        got = lax.all_to_all(message.reshape(sx * sy, 1, 128), ("gx", "gy"), 0, 0).reshape(sx * sy, 128)
        (out,) = call(finish_kernel, [shape(3, 64, 512)], 6, [pltpu.VMEM((3, 64, 512), f32)], name="finish")(flags, got, *stored, v)
        return out.reshape(3, 1, 1, 64, 512)

    in_specs = (
        P(None, "gx", "gy", None, None),
        P(None, "gx", "gy", None, None),
        P(None, "gx", "gy", None, None),
        P("gx", "gy", None, None),
        P("gx", "gy", None),
    )
    return jax.shard_map(local, mesh=mesh, in_specs=in_specs, out_specs=P(None, "gx", "gy", None, None), check_vma=False)
```

```python
import jax
import jax.numpy as jnp
import numpy as np
from jax import lax
from jax.experimental import pallas as pl
from jax.experimental.pallas import tpu as pltpu
from jax.sharding import PartitionSpec as P


STEPS = 4
DT = 0.25
SCALE = 0.5
f32 = jnp.float32


def legendre_seven(points):
    previous = points * 0.0 + 1.0
    current = points
    for degree in range(1, 7):
        following = ((2 * degree + 1) * points * current - degree * previous) / (degree + 1)
        previous = current
        current = following
    return current


def gll_tables():
    poly_order = 7
    points = np.array(
        [
            -1.0,
            -0.8717401485096066,
            -0.5917001814331423,
            -0.2092992179024789,
            0.2092992179024789,
            0.5917001814331423,
            0.8717401485096066,
            1.0,
        ]
    )
    end_values = legendre_seven(points)
    weights = 2.0 / (poly_order * (poly_order + 1) * end_values**2)
    spread = points[:, None] - points[None, :]
    identity = np.eye(poly_order + 1)
    diff_table = end_values[:, None] / (end_values[None, :] * (spread + identity))
    diff_table = diff_table * (1.0 - identity)
    corners = np.zeros(poly_order + 1)
    corners[0] = -poly_order * (poly_order + 1) / 4.0
    corners[-1] = poly_order * (poly_order + 1) / 4.0
    diff_table = diff_table + identity * corners[None, :]
    return (weights.astype(np.float32), diff_table.astype(np.float32))


WEIGHTS, DMAT = gll_tables()
WMAX = [float(w) for w in WEIGHTS]


def halves(mat):
    mat = mat.astype(np.float64)
    assert np.array_equal(mat[::-1, ::-1], -mat)
    odd = 0.5 * (mat[:4, :4] - mat[:4, 7:3:-1])
    even = 0.5 * (mat[:4, :4] + mat[:4, 7:3:-1])
    return odd, even


FWD = halves(DMAT)
BWD = halves(DMAT.T)


def roll_factors(mat):
    sub = lax.broadcasted_iota(jnp.int32, (8, 128), 0)
    out = []
    for r in range(8):
        factor = jnp.full((8, 128), float(mat[0, -r % 8]), f32)
        for k in range(1, 8):
            factor = jnp.where(sub == k, float(mat[k, (k - r) % 8]), factor)
        out.append(factor)
    return out


def along(xs, tables):
    odd, even = tables
    diff = [xs[b] - xs[7 - b] for b in range(4)]
    both = [xs[b] + xs[7 - b] for b in range(4)]
    out = [None] * 8
    for a in range(4):
        s = float(odd[a, 0]) * diff[0]
        t = float(even[a, 0]) * both[0]
        for b in range(1, 4):
            s = s + float(odd[a, b]) * diff[b]
            t = t + float(even[a, b]) * both[b]
        out[a] = s + t
        out[7 - a] = s - t
    return out


def along_ends(xs, tables):
    odd, even = tables
    s = float(odd[0, 0]) * (xs[0] - xs[7])
    t = float(even[0, 0]) * (xs[0] + xs[7])
    for b in range(1, 4):
        s = s + float(odd[0, b]) * (xs[b] - xs[7 - b])
        t = t + float(even[0, b]) * (xs[b] + xs[7 - b])
    return s + t, s - t


def along_k(x, coef):
    out = coef[0] * x
    for r in range(1, 8):
        out = out + coef[r] * pltpu.roll(x, r, 0)
    return out


def lanes():
    lane = lax.broadcasted_iota(jnp.int32, (8, 128), 1)
    return (lane // 32) % 2, (lane // 16) % 2, lane % 16, lane


def is_set(flags, index):
    return jnp.broadcast_to(flags[index : index + 1, :], (8, 128)) != 0


def rows(j):
    return pl.ds(pl.multiple_of(8 * j, 8), 8)


def pack_low(face0, face1, first, shift):
    return jnp.where(first, face0, pltpu.roll(face1, shift, 1))


def pack_high(face0, face1, first, shift):
    return jnp.where(first, pltpu.roll(face1, 128 - shift, 1), face0)


def unpack_high(got, first, shift):
    zero = jnp.zeros_like(got)
    return jnp.where(first, zero, pltpu.roll(got, shift, 1)), jnp.where(first, zero, got)


def unpack_low(got, first, shift):
    zero = jnp.zeros_like(got)
    return jnp.where(first, pltpu.roll(got, 128 - shift, 1), zero), jnp.where(first, got, zero)


def received(even, odd, parity, has_low, has_high):
    zero = jnp.zeros_like(even)
    low = jnp.where(has_low, jnp.where(parity, even, odd), zero)
    high = jnp.where(has_high, jnp.where(parity, odd, even), zero)
    return low, high


def send_x(lows, highs, x0, parity, sends, at):
    to_low = pack_low(lows[0], lows[1], x0, 32)
    to_high = pack_high(highs[0], highs[1], x0, 32)
    sends[0][at, :] = jnp.where(parity, to_low, to_high)
    sends[1][at, :] = jnp.where(parity, to_high, to_low)


def assemble_local(u, flags, y_low, y_high):
    X, Y, Z, _ = lanes()
    x0, y0 = X == 0, Y == 0
    for t in range(2):
        for i in range(8):
            low = u[t, i, pl.ds(0, 8, 8), :]
            high = u[t, i, pl.ds(7, 8, 8), :]
            u[t, i, pl.ds(0, 8, 8), :] = low + jnp.where(Z > 0, pltpu.roll(high, 1, 1), 0.0)
            u[t, i, pl.ds(7, 8, 8), :] = high + jnp.where(Z < 15, pltpu.roll(low, 127, 1), 0.0)
    for t in range(2):
        for i in range(8):
            low = u[t, i, 0:8, :]
            high = u[t, i, 56:64, :]
            u[t, i, 0:8, :] = low + jnp.where(y0, 0.0, pltpu.roll(high, 16, 1))
            u[t, i, 56:64, :] = high + jnp.where(y0, pltpu.roll(low, 112, 1), 0.0)
    for j in range(8):
        at = slice(8 * j, 8 * j + 8)
        lows, highs = [], []
        for t in range(2):
            low = u[t, 0, at, :]
            high = u[t, 7, at, :]
            lows.append(low + jnp.where(x0, 0.0, pltpu.roll(high, 32, 1)))
            highs.append(high + jnp.where(x0, pltpu.roll(low, 96, 1), 0.0))
            u[t, 0, at, :] = lows[t]
            u[t, 7, at, :] = highs[t]
    for i in range(8):
        at = slice(8 * i, 8 * i + 8)
        y_low[at, :] = pack_low(u[0, i, 0:8, :], u[1, i, 0:8, :], y0, 16)
        y_high[at, :] = pack_high(u[0, i, 56:64, :], u[1, i, 56:64, :], y0, 16)


def thirds(x):
    high = x.astype(jnp.bfloat16)
    rest = x - high.astype(f32)
    mid = rest.astype(jnp.bfloat16)
    low = (rest - mid.astype(f32)).astype(jnp.bfloat16)
    return [high, mid, low]


def pick_table(flags):
    return (lax.broadcasted_iota(jnp.int32, (128, 128), 0) == flags[8:9, :]).astype(f32).T


def place(parts, table):
    rows_in = jnp.concatenate(parts, axis=0)
    tables = jnp.concatenate([table.astype(jnp.bfloat16)] * len(parts), axis=0)
    out = lax.dot_general(rows_in, tables, (((0,), (0,)), ((), ())), preferred_element_type=f32)
    return out.reshape(8, 64, 128)


def weight_k():
    sub = lax.broadcasted_iota(jnp.int32, (8, 128), 0)
    wk = jnp.zeros((8, 128), f32)
    for k in range(8):
        wk = jnp.where(sub == k, WMAX[k], wk)
    return wk


def coef_kernel(flags, dif, coef):
    pick = pick_table(flags)
    over = pick[0:64, :] + pick[64:128, :]
    wk = weight_k()
    for m in range(3):
        coef[m] = place(thirds(dif[m]), over)
        for i in range(8):
            for j in range(8):
                at = slice(8 * j, 8 * j + 8)
                coef[m, i, at, :] = coef[m, i, at, :] * (wk * (WMAX[i] * WMAX[j] * DT))


def cross_source(lane, dk_a, dj_a, di_a, dj_b, di_b, v_a, v_b, a_a, a_b, m):
    def other(x):
        return pltpu.roll(x, 64, 1)

    left = lane < 64
    sign = jnp.where(left, 1.0, -1.0)
    swapped = other(dk_a)
    r_a = jnp.where(left, dj_b - swapped, swapped - di_b)
    mixed = jnp.where(left, dj_a, di_a)
    r_b = sign * (other(mixed) - mixed)
    turned = other(r_a)
    s_a = sign * (other(v_a) * r_b - v_b * turned)
    prod = v_a * turned
    s_b = sign * (prod - other(prod))
    return m * (a_a + DT * s_a), m * (a_b + DT * s_b)


def send_edges(e, flags, sends):
    X, Y, Z, _ = lanes()
    x0, y0 = X == 0, Y == 0
    for t in range(2):
        for q in range(2):
            low = e[t, q, pl.ds(0, 8, 8), :]
            high = e[t, q, pl.ds(7, 8, 8), :]
            e[t, q, pl.ds(0, 8, 8), :] = low + jnp.where(Z > 0, pltpu.roll(high, 1, 1), 0.0)
            e[t, q, pl.ds(7, 8, 8), :] = high + jnp.where(Z < 15, pltpu.roll(low, 127, 1), 0.0)
    ends = {}
    for t in range(2):
        for q in range(2):
            low = e[t, q, 0:8, :]
            high = e[t, q, 56:64, :]
            ends[t, q, 0] = low + jnp.where(y0, 0.0, pltpu.roll(high, 16, 1))
            ends[t, q, 7] = high + jnp.where(y0, pltpu.roll(low, 112, 1), 0.0)
    parity = is_set(flags, 0)
    for j in range(8):
        at = slice(8 * j, 8 * j + 8)
        lows, highs = [], []
        for t in range(2):
            low, high = (ends[t, q, j] if j in (0, 7) else e[t, q, at, :] for q in range(2))
            lows.append(low + jnp.where(x0, 0.0, pltpu.roll(high, 32, 1)))
            highs.append(high + jnp.where(x0, pltpu.roll(low, 96, 1), 0.0))
        send_x(lows, highs, x0, parity, sends, at)


def make_setup(sx, sy):
    def kernel(slot_hbm, adj_hbm, vel_hbm, jac_hbm, flags, a, v, mass, roll_ref, send_e, send_o, e, slot, adj, vel, jac, sems):
        copies = [pltpu.make_async_copy(slot_hbm, slot, sems.at[7])]
        copies += [pltpu.make_async_copy(adj_hbm.at[c], adj.at[c], sems.at[c]) for c in range(3)]
        copies += [pltpu.make_async_copy(vel_hbm.at[c], vel.at[c], sems.at[3 + c]) for c in range(3)]
        copies.append(pltpu.make_async_copy(jac_hbm, jac, sems.at[6]))
        for copy in copies:
            copy.start()
        gx, gy = lax.axis_index("gx"), lax.axis_index("gy")
        facts = [lax.rem(gx, 2), lax.rem(gy, 2), gx, (sx - 1) - gx, gy, (sy - 1) - gy]
        for n, fact in enumerate(facts):
            flags[n : n + 1, :] = jnp.full((1, 128), fact, jnp.int32)
        flags[6:8, :] = jnp.zeros((2, 128), jnp.int32)
        kf = roll_factors(DMAT)
        for r, factor in enumerate(kf + roll_factors(DMAT.T)):
            roll_ref[r] = factor
        lane = lanes()[3]
        wk = weight_k()
        copies[0].wait()
        flags[8:16, :] = jnp.broadcast_to(jnp.concatenate([slot[...], slot[...] + 64], axis=1), (8, 128))
        pick = pick_table(flags)
        over = pick[0:64, :] + pick[64:128, :]
        for copy in copies[1:4]:
            copy.wait()
        a[0] = place(thirds(jnp.concatenate([adj[0], adj[1]], axis=0)), pick)
        a[1] = place(thirds(adj[2]), over)
        for copy in copies[4:]:
            copy.wait()
        v[0] = place([jnp.concatenate([vel[0], vel[1]], axis=0)], pick)
        v[1] = place([vel[2]], over)
        mass[...] = place(thirds(jac[...]), over)
        ends = {}
        for q, i in enumerate((0, 7)):
            for t in range(2):
                out = along([a[t, i, 8 * j : 8 * j + 8, :] for j in range(8)], FWD)
                for j in range(8):
                    e[t, q, 8 * j : 8 * j + 8, :] = out[j]
        for j in range(8):
            at = slice(8 * j, 8 * j + 8)
            di = [along_ends([a[t, i, at, :] for i in range(8)], FWD) for t in range(2)]
            for q, i in enumerate((0, 7)):
                ends[q] = cross_source(
                    lane, along_k(a[0, i, at, :], kf), e[0, q, at, :], di[0][q], e[1, q, at, :], di[1][q],
                    v[0, i, at, :], v[1, i, at, :], a[0, i, at, :], a[1, i, at, :], mass[i, at, :] * (wk * (WMAX[i] * WMAX[j])),
                )
                for t in range(2):
                    e[t, q, at, :] = ends[q][t]
        send_edges(e, flags, (send_e, send_o))

    return kernel


def source_kernel(flags, a, v, mass_in, roll_ref, mass, u, y_low, y_high, di, dj, dk):
    lane = lanes()[3]
    wk = weight_k()
    kf = [roll_ref[r] for r in range(8)]
    for t in range(2):

        def planes(j, carry, t=t):
            xs = [a[t, i, rows(j), :] for i in range(8)]
            out = along(xs, FWD)
            for i in range(8):
                di[t, i, rows(j), :] = out[i]
                if t == 0:
                    dk[i, rows(j), :] = along_k(xs[i], kf)
            return carry

        lax.fori_loop(0, 8, planes, 0)

    def columns(n, carry):
        t, i = n // 8, n % 8
        out = along([a[t, i, 8 * j : 8 * j + 8, :] for j in range(8)], FWD)
        for j in range(8):
            dj[t, i, 8 * j : 8 * j + 8, :] = out[j]
        return carry

    lax.fori_loop(0, 16, columns, 0)

    def cross(i, carry):
        index = jnp.full((8, 128), i, jnp.int32)
        wi = jnp.zeros((8, 128), f32)
        for n in range(8):
            wi = jnp.where(index == n, WMAX[n], wi)
        for j in range(8):
            at = slice(8 * j, 8 * j + 8)
            m = mass_in[i, at, :] * (wk * (wi * WMAX[j]))
            mass[i, at, :] = m
            u[0, i, at, :], u[1, i, at, :] = cross_source(
                lane, dk[i, at, :], dj[0, i, at, :], di[0, i, at, :], dj[1, i, at, :], di[1, i, at, :],
                v[0, i, at, :], v[1, i, at, :], a[0, i, at, :], a[1, i, at, :], m,
            )
        return carry

    lax.fori_loop(0, 8, cross, 0)
    assemble_local(u, flags, y_low, y_high)


def mid_kernel(flags, got_e, got_o, y_low, y_high, _, send_e, send_o):
    X, Y, _, _ = lanes()
    x0, y0 = X == 0, Y == 0
    lows, highs = [], []
    for i in range(8):
        lows.append(y_low[8 * i : 8 * i + 8, :])
        highs.append(y_high[8 * i : 8 * i + 8, :])
    for j, into, pack in ((0, lows, pack_low), (7, highs, pack_high)):
        at = slice(8 * j, 8 * j + 8)
        low, high = received(got_e[at, :], got_o[at, :], is_set(flags, 0), is_set(flags, 2), is_set(flags, 3))
        into[0] = into[0] + pack(*unpack_low(low, x0, 32), y0, 16)
        into[7] = into[7] + pack(*unpack_high(high, x0, 32), y0, 16)
    parity = is_set(flags, 1)
    for i in range(8):
        send_e[8 * i : 8 * i + 8, :] = jnp.where(parity, lows[i], highs[i])
        send_o[8 * i : 8 * i + 8, :] = jnp.where(parity, highs[i], lows[i])


def main_kernel(step):
    def kernel(*refs):
        if step == 0:
            u, mass, coef, roll_ref, v, y = refs
        else:
            flags, u, before, mass, coef, roll_ref, v, y, stored = refs
            store(flags, before, stored)

        def planes(n, carry):
            t, j = n // 8, n % 8
            if step == 0:
                xs = [u[t, i, rows(j), :] for i in range(8)]
            else:
                xs = [SCALE * u[t, i, rows(j), :] - before[t, i, rows(j), :] for i in range(8)]
            flux = along(xs, FWD)
            out = along([coef[0, i, rows(j), :] * flux[i] for i in range(8)], BWD)
            for i in range(8):
                v[t, i, rows(j), :] = xs[i]
                part = coef[2, i, rows(j), :] * along_k(xs[i], [roll_ref[r] for r in range(8)])
                part = along_k(part, [roll_ref[8 + r] for r in range(8)])
                y[t, i, rows(j), :] = mass[i, rows(j), :] * xs[i] + out[i] + part
            return carry

        lax.fori_loop(0, 16, planes, 0)

        def columns(n, carry):
            t, i = n // 8, n % 8
            flux = along([v[t, i, 8 * j : 8 * j + 8, :] for j in range(8)], FWD)
            out = along([coef[1, i, 8 * j : 8 * j + 8, :] * flux[j] for j in range(8)], BWD)
            for j in range(8):
                at = slice(8 * j, 8 * j + 8)
                y[t, i, at, :] = y[t, i, at, :] + out[j]
            return carry

        lax.fori_loop(0, 16, columns, 0)

    return kernel


def plane_at(axis, lead, normal, plane):
    i, j = (normal, plane) if axis == 0 else (plane, normal)
    return lead + (i, slice(8 * j, 8 * j + 8), slice(None))


def outer_faces(first, got, shift, scale, t):
    if t == 0:
        return [scale * jnp.where(first, pltpu.roll(low, 128 - shift, 1), pltpu.roll(high, shift, 1)) for low, high in got]
    return [scale * jnp.where(first, low, high) for low, high in got]


def face_operator(first, axis, face, planes, mass, coef, roll_ref):
    def outer(ref, lead, plane):
        return jnp.where(first, ref[plane_at(axis, lead, 0, plane)], ref[plane_at(axis, lead, 7, plane)])

    cols = [jnp.where(first, float(DMAT[a, 0]), float(DMAT[a, 7])) for a in range(8)]
    kf = [roll_ref[r] for r in range(8)]
    kb = [roll_ref[8 + r] for r in range(8)]
    flux = along(face, FWD)
    inner = along([outer(coef, (1 - axis,), p) * flux[p] for p in range(8)], BWD)
    for p in planes:
        x = face[p]
        plane = outer(mass, (), p) * x + inner[p]
        plane = plane + along_k(outer(coef, (2,), p) * along_k(x, kf), kb)
        out = along([coef[plane_at(axis, (axis,), a, p)] * (cols[a] * x) for a in range(8)], BWD)
        out[0] = out[0] + jnp.where(first, plane, 0.0)
        out[7] = out[7] + jnp.where(first, 0.0, plane)
        yield p, out


def add_values(first, axis, face, t, v):
    for p in range(8):
        for a, part in ((0, jnp.where(first, face[p], 0.0)), (7, jnp.where(first, 0.0, face[p]))):
            index = plane_at(axis, (t,), a, p)
            v[index] = v[index] + part


def got_from(flags, even, odd, axis):
    out = []
    for p in range(8):
        at = slice(8 * p, 8 * p + 8)
        out.append(received(even[at, :], odd[at, :], is_set(flags, axis), is_set(flags, 2 + 2 * axis), is_set(flags, 3 + 2 * axis)))
    return out


def x_kernel(step):
    def kernel(flags, xe, xo, mass, coef, roll_ref, y_in, y):
        first = lanes()[0] == 0
        got = got_from(flags, xe, xo, 0)
        for t in range(2):
            face = outer_faces(first, got, 32, SCALE if step else 1.0, t)
            for p, out in face_operator(first, 0, face, range(8), mass, coef, roll_ref):
                for a in range(8):
                    index = plane_at(0, (t,), a, p)
                    y[index] = y_in[index] + out[a]

    return kernel


def edge_kernel(step):
    def kernel(flags, ye, yo, mass, coef, roll_ref, y_in, send_e, send_o, e):
        y0 = lanes()[1] == 0
        got = got_from(flags, ye, yo, 1)
        for t in range(2):
            face = outer_faces(y0, got, 16, SCALE if step else 1.0, t)
            for p, out in face_operator(y0, 1, face, (0, 7), mass, coef, roll_ref):
                for a in range(8):
                    at = slice(8 * a, 8 * a + 8)
                    e[t, p // 7, at, :] = y_in[t, p, at, :] + out[a]
        send_edges(e, flags, (send_e, send_o))

    return kernel


def y_kernel(step):
    last = step == STEPS - 1
    n_dots = step + 1 + (step == 0)

    def kernel(flags, xe, xo, ye, yo, mass, coef, roll_ref, *refs):
        older = refs[:step]
        if last:
            parts, v_in, y_in, v, message, y = refs[step:]
        else:
            v_in, y_in, v, y, y_low, y_high, dots = refs[step:]
        X, Y, Z, lane = lanes()
        scale = SCALE if step else 1.0
        for t in range(2):
            for i in range(8):
                for j in range(8):
                    index = plane_at(0, (t,), i, j)
                    v[index] = v_in[index]
        got_x, got_y = got_from(flags, xe, xo, 0), got_from(flags, ye, yo, 1)
        for t in range(2):
            add_values(X == 0, 0, outer_faces(X == 0, got_x, 32, scale, t), t, v)
            face = outer_faces(Y == 0, got_y, 16, scale, t)
            add_values(Y == 0, 1, face, t, v)
            for p, out in face_operator(Y == 0, 1, face, range(8), mass, coef, roll_ref):
                for a in range(8):
                    index = plane_at(1, (t,), a, p)
                    y[index] = y_in[index] + out[a]
        if step == 0:
            sub = lax.broadcasted_iota(jnp.int32, (8, 128), 0)
            wz = jnp.where(((Z > 0) & (sub == 0)) | ((Z < 15) & (sub == 7)), 0.5, 1.0)
            wy_low = jnp.where((Y == 1) | is_set(flags, 4), 0.5, 1.0)
            wy_high = jnp.where((Y == 0) | is_set(flags, 5), 0.5, 1.0)
            wx_low = jnp.where((X == 1) | is_set(flags, 2), 0.5, 1.0)
            wx_high = jnp.where((X == 0) | is_set(flags, 3), 0.5, 1.0)

        def products(t):
            def body(i, sums):
                sums = list(sums)
                squares = []
                for j in range(8):
                    at = slice(8 * j, 8 * j + 8)
                    total = y[t, i, at, :]
                    own = v[t, i, at, :]
                    for m in range(step):
                        sums[m] = sums[m] + older[m][t, i, at, :] * total
                    sums[step] = sums[step] + own * total
                    squares.append(own * own)
                if step == 0:
                    index = jnp.full((8, 128), i, jnp.int32)
                    wx = wz * jnp.where(index == 0, wx_low, jnp.where(index == 7, wx_high, 1.0))
                    square = squares[1]
                    for j in range(2, 7):
                        square = square + squares[j]
                    square = square + wy_low * squares[0] + wy_high * squares[7]
                    sums[1] = sums[1] + wx * square
                return tuple(sums)

            return lax.fori_loop(0, 8, body, tuple(jnp.zeros((8, 128), f32) for _ in range(n_dots)))

        sums = [p + 0.5 * q for p, q in zip(products(0), products(1))]
        if not last:
            for m in range(n_dots):
                dots[8 * m : 8 * m + 8, :] = sums[m]
            assemble_local(y, flags, y_low, y_high)
            return
        row_of = lax.broadcasted_iota(jnp.int32, (16, 128), 0)
        lane_of = lax.broadcasted_iota(jnp.int32, (16, 128), 1)
        table = jnp.zeros((16, 128), f32)
        every = [parts[8 * m : 8 * m + 8, :] for m in range(7)] + sums
        for m, value in enumerate(every):
            table = jnp.where(row_of == m, jnp.sum(value, axis=0, keepdims=True), table)
        column = jnp.sum(table, axis=1, keepdims=True)
        line = jnp.sum(jnp.where(row_of == lane_of, column, 0.0), axis=0, keepdims=True)
        message[...] = jnp.broadcast_to(line, message.shape)

    return kernel


def store(flags, v, stored):
    pick = pick_table(flags).astype(jnp.bfloat16)
    for t in range(2):
        table = jnp.concatenate([pick if t == 0 else pick[0:64, :]] * 3, axis=1)
        x = jnp.concatenate(thirds(v[t].reshape(512, 128)), axis=1)
        res = lax.dot_general(table, x, (((1,), (1,)), ((), ())), preferred_element_type=f32)
        if t == 0:
            stored[0] = res[0:64, :]
            stored[1] = res[64:128, :]
        else:
            stored[2] = res


def finish_kernel(flags, got, stored0, stored1, stored2, v, out, stored3):
    store(flags, v, stored3)
    stored = (stored0, stored1, stored2, stored3)
    total = jnp.sum(got[...], axis=0, keepdims=True)
    lane = lax.broadcasted_iota(jnp.int32, (1, 128), 1)

    def entry(m):
        return jnp.sum(jnp.where(lane == m, total, 0.0), axis=1, keepdims=True)

    gram = {}
    order = [(0, 0), None, (0, 1), (1, 1), (0, 2), (1, 2), (2, 2), (0, 3), (1, 3), (2, 3), (3, 3)]
    for m, pair in enumerate(order):
        if pair is None:
            square = entry(m)
        else:
            gram[pair] = entry(m)
    right = [square]
    for j in range(3):
        right.append(SCALE * gram[(0, j)] - right[j])
    lower, inverse, reduced = {}, [], []
    for c in range(4):
        pivot = gram[(c, c)]
        value = right[c]
        for m in range(c):
            pivot = pivot - lower[(c, m)] * lower[(c, m)] * inverse[m]
            value = value - lower[(c, m)] * reduced[m] * inverse[m]
        good = pivot > 1e-6 * gram[(c, c)]
        inverse.append(jnp.where(good, 1.0 / jnp.where(good, pivot, 1.0), 0.0))
        reduced.append(value)
        for r in range(c + 1, 4):
            acc = gram[(c, r)]
            for m in range(c):
                acc = acc - lower[(r, m)] * lower[(c, m)] * inverse[m]
            lower[(r, c)] = acc
    weight = [None] * 4
    for c in reversed(range(4)):
        acc = reduced[c]
        for r in range(c + 1, 4):
            acc = acc - lower[(r, c)] * weight[r]
        weight[c] = acc * inverse[c]
    for n in range(3):
        x = weight[0] * stored[0][n]
        for c in range(1, 4):
            x = x + weight[c] * stored[c][n]
        out[n] = x


def swaps(sx, sy, along_x, odd):
    pairs = []
    for g in range(sx):
        for h in range(sy):
            at, count = (g, sx) if along_x else (h, sy)
            other = at + 1 if at % 2 == odd else at - 1
            if along_x:
                to = (other, h) if 0 <= other < count else (g, h ^ 1)
            else:
                to = (g, other) if 0 <= other < count else (g ^ 1, h)
            pairs.append((g * sy + h, to[0] * sy + to[1]))
    return pairs


def solution(mesh):
    vmem = pl.BlockSpec(memory_space=pltpu.VMEM)
    params = pltpu.CompilerParams(vmem_limit_bytes=40 * 1024 * 1024)
    sx, sy = mesh.shape["gx"], mesh.shape["gy"]

    def shape(*dims):
        return jax.ShapeDtypeStruct(dims, f32)

    field, face = shape(2, 8, 64, 128), shape(64, 128)

    anywhere = pl.BlockSpec(memory_space=pltpu.HBM)

    def call(kernel, outs, ins, scratch=(), name=None, cost=None):
        return pl.pallas_call(
            kernel,
            out_shape=outs,
            in_specs=ins if isinstance(ins, list) else [vmem] * ins,
            out_specs=[vmem] * len(outs),
            scratch_shapes=scratch,
            compiler_params=params,
            cost_estimate=pl.CostEstimate(flops=0, transcendentals=0, bytes_accessed=cost) if cost else None,
            name=name,
        )

    def held(x):
        return pltpu.with_memory_space_constraint(x, pltpu.HBM)

    def local(adjoint_field, velocity, diffusivity, jacobian, element_slot):
        big = pltpu.VMEM((2, 8, 64, 128), f32)
        flags, a, v, mass, table, xe, xo = call(
            make_setup(sx, sy),
            [jax.ShapeDtypeStruct((16, 128), jnp.int32), field, field, shape(8, 64, 128), shape(16, 8, 128), face, face],
            [anywhere] * 4,
            [
                pltpu.VMEM((2, 2, 64, 128), f32),
                pltpu.VMEM((1, 64), jnp.int32),
                pltpu.VMEM((3, 64, 512), f32),
                pltpu.VMEM((3, 64, 512), jnp.bfloat16),
                pltpu.VMEM((64, 512), f32),
                pltpu.SemaphoreType.DMA((8,)),
            ],
            "setup",
        )(held(element_slot.reshape(1, 64)), held(adjoint_field.reshape(3, 64, 512)), held(velocity.reshape(3, 64, 512)), held(jacobian.reshape(64, 512)))
        mass, u, yl, yh = call(
            source_kernel, [shape(8, 64, 128), field, face, face], 5, [big, big, pltpu.VMEM((8, 64, 128), f32)], "source", cost=8 << 20
        )(flags, a, v, mass, table)
        (coef,) = call(coef_kernel, [shape(3, 8, 64, 128)], 2, name="coef", cost=3 << 20)(flags, diffusivity.reshape(3, 64, 512))
        vs, parts, stored = [], [], []
        for step in range(STEPS):
            xe = lax.ppermute(xe, ("gx", "gy"), swaps(sx, sy, True, 0))
            xo = lax.ppermute(xo, ("gx", "gy"), swaps(sx, sy, True, 1))
            shared = [mass, coef, table]
            if step == 0:
                v, y = call(main_kernel(step), [field, field], 4, name="main0", cost=8 << 20)(u, *shared)
            else:
                v, y, moved = call(main_kernel(step), [field, field, shape(3, 64, 512)], 6, name=f"main{step}", cost=8 << 20)(flags, u, vs[-1], *shared)
                stored.append(moved)
            ye, yo = call(mid_kernel, [face, face], [vmem] * 5 + [anywhere], name="mid")(flags, xe, xo, yl, yh, y if step else coef)
            ye = lax.ppermute(ye, ("gx", "gy"), swaps(sx, sy, False, 0))
            yo = lax.ppermute(yo, ("gx", "gy"), swaps(sx, sy, False, 1))
            (y,) = call(x_kernel(step), [field], 7, name=f"xpart{step}", cost=8 << 20)(flags, xe, xo, *shared, y)
            args = [flags, xe, xo, ye, yo] + shared + vs
            if step < STEPS - 1:
                xe, xo = call(edge_kernel(step), [face, face], 7, [pltpu.VMEM((2, 2, 64, 128), f32)], f"edge{step}")(flags, ye, yo, *shared, y)
                n_dots = step + 1 + (step == 0)
                v, u, yl, yh, dots = call(
                    y_kernel(step), [field, field, face, face, shape(8 * n_dots, 128)], len(args) + 2, name=f"ypart{step}", cost=8 << 20
                )(*args, v, y)
                vs.append(v)
                parts.append(dots)
            else:
                parts = jnp.concatenate(parts, axis=0)
                v, message = call(y_kernel(step), [field, shape(sx * sy, 128)], len(args) + 3, [big], "ypart3")(*args, parts, v, y)
        got = lax.all_to_all(message.reshape(sx * sy, 1, 128), ("gx", "gy"), 0, 0).reshape(sx * sy, 128)
        (out,) = call(finish_kernel, [shape(3, 64, 512)], 6, [pltpu.VMEM((3, 64, 512), f32)], name="finish")(flags, got, *stored, v)
        return out.reshape(3, 1, 1, 64, 512)

    in_specs = (
        P(None, "gx", "gy", None, None),
        P(None, "gx", "gy", None, None),
        P(None, "gx", "gy", None, None),
        P("gx", "gy", None, None),
        P("gx", "gy", None),
    )
    return jax.shard_map(local, mesh=mesh, in_specs=in_specs, out_specs=P(None, "gx", "gy", None, None), check_vma=False)
```

```python
import jax
import jax.numpy as jnp
import numpy as np
from jax import lax
from jax.experimental import pallas as pl
from jax.experimental.pallas import tpu as pltpu
from jax.sharding import PartitionSpec as P


STEPS = 4
DT = 0.25
SCALE = 0.5
f32 = jnp.float32


def legendre_seven(points):
    previous = points * 0.0 + 1.0
    current = points
    for degree in range(1, 7):
        following = ((2 * degree + 1) * points * current - degree * previous) / (degree + 1)
        previous = current
        current = following
    return current


def gll_tables():
    poly_order = 7
    points = np.array(
        [
            -1.0,
            -0.8717401485096066,
            -0.5917001814331423,
            -0.2092992179024789,
            0.2092992179024789,
            0.5917001814331423,
            0.8717401485096066,
            1.0,
        ]
    )
    end_values = legendre_seven(points)
    weights = 2.0 / (poly_order * (poly_order + 1) * end_values**2)
    spread = points[:, None] - points[None, :]
    identity = np.eye(poly_order + 1)
    diff_table = end_values[:, None] / (end_values[None, :] * (spread + identity))
    diff_table = diff_table * (1.0 - identity)
    corners = np.zeros(poly_order + 1)
    corners[0] = -poly_order * (poly_order + 1) / 4.0
    corners[-1] = poly_order * (poly_order + 1) / 4.0
    diff_table = diff_table + identity * corners[None, :]
    return (weights.astype(np.float32), diff_table.astype(np.float32))


WEIGHTS, DMAT = gll_tables()
WMAX = [float(w) for w in WEIGHTS]


def halves(mat):
    mat = mat.astype(np.float64)
    assert np.array_equal(mat[::-1, ::-1], -mat)
    odd = 0.5 * (mat[:4, :4] - mat[:4, 7:3:-1])
    even = 0.5 * (mat[:4, :4] + mat[:4, 7:3:-1])
    return odd, even


FWD = halves(DMAT)
BWD = halves(DMAT.T)


def roll_factors(mat):
    sub = lax.broadcasted_iota(jnp.int32, (8, 128), 0)
    out = []
    for r in range(8):
        factor = jnp.full((8, 128), float(mat[0, -r % 8]), f32)
        for k in range(1, 8):
            factor = jnp.where(sub == k, float(mat[k, (k - r) % 8]), factor)
        out.append(factor)
    return out


def along(xs, tables):
    odd, even = tables
    diff = [xs[b] - xs[7 - b] for b in range(4)]
    both = [xs[b] + xs[7 - b] for b in range(4)]
    out = [None] * 8
    for a in range(4):
        s = float(odd[a, 0]) * diff[0]
        t = float(even[a, 0]) * both[0]
        for b in range(1, 4):
            s = s + float(odd[a, b]) * diff[b]
            t = t + float(even[a, b]) * both[b]
        out[a] = s + t
        out[7 - a] = s - t
    return out


def along_ends(xs, tables):
    odd, even = tables
    s = float(odd[0, 0]) * (xs[0] - xs[7])
    t = float(even[0, 0]) * (xs[0] + xs[7])
    for b in range(1, 4):
        s = s + float(odd[0, b]) * (xs[b] - xs[7 - b])
        t = t + float(even[0, b]) * (xs[b] + xs[7 - b])
    return s + t, s - t


def along_k(x, coef):
    out = coef[0] * x
    for r in range(1, 8):
        out = out + coef[r] * pltpu.roll(x, r, 0)
    return out


def lanes():
    lane = lax.broadcasted_iota(jnp.int32, (8, 128), 1)
    return (lane // 32) % 2, (lane // 16) % 2, lane % 16, lane


def is_set(flags, index):
    return jnp.broadcast_to(flags[index : index + 1, :], (8, 128)) != 0


def rows(j):
    return pl.ds(pl.multiple_of(8 * j, 8), 8)


def pack_low(face0, face1, first, shift):
    return jnp.where(first, face0, pltpu.roll(face1, shift, 1))


def pack_high(face0, face1, first, shift):
    return jnp.where(first, pltpu.roll(face1, 128 - shift, 1), face0)


def unpack_high(got, first, shift):
    zero = jnp.zeros_like(got)
    return jnp.where(first, zero, pltpu.roll(got, shift, 1)), jnp.where(first, zero, got)


def unpack_low(got, first, shift):
    zero = jnp.zeros_like(got)
    return jnp.where(first, pltpu.roll(got, 128 - shift, 1), zero), jnp.where(first, got, zero)


def received(even, odd, parity, has_low, has_high):
    zero = jnp.zeros_like(even)
    low = jnp.where(has_low, jnp.where(parity, even, odd), zero)
    high = jnp.where(has_high, jnp.where(parity, odd, even), zero)
    return low, high


def send_x(lows, highs, x0, parity, sends, at):
    to_low = pack_low(lows[0], lows[1], x0, 32)
    to_high = pack_high(highs[0], highs[1], x0, 32)
    sends[0][at, :] = jnp.where(parity, to_low, to_high)
    sends[1][at, :] = jnp.where(parity, to_high, to_low)


def assemble_local(u, flags, y_low, y_high):
    X, Y, Z, _ = lanes()
    x0, y0 = X == 0, Y == 0
    for t in range(2):
        for i in range(8):
            low = u[t, i, pl.ds(0, 8, 8), :]
            high = u[t, i, pl.ds(7, 8, 8), :]
            u[t, i, pl.ds(0, 8, 8), :] = low + jnp.where(Z > 0, pltpu.roll(high, 1, 1), 0.0)
            u[t, i, pl.ds(7, 8, 8), :] = high + jnp.where(Z < 15, pltpu.roll(low, 127, 1), 0.0)
    for t in range(2):
        for i in range(8):
            low = u[t, i, 0:8, :]
            high = u[t, i, 56:64, :]
            u[t, i, 0:8, :] = low + jnp.where(y0, 0.0, pltpu.roll(high, 16, 1))
            u[t, i, 56:64, :] = high + jnp.where(y0, pltpu.roll(low, 112, 1), 0.0)
    for j in range(8):
        at = slice(8 * j, 8 * j + 8)
        lows, highs = [], []
        for t in range(2):
            low = u[t, 0, at, :]
            high = u[t, 7, at, :]
            lows.append(low + jnp.where(x0, 0.0, pltpu.roll(high, 32, 1)))
            highs.append(high + jnp.where(x0, pltpu.roll(low, 96, 1), 0.0))
            u[t, 0, at, :] = lows[t]
            u[t, 7, at, :] = highs[t]
    for i in range(8):
        at = slice(8 * i, 8 * i + 8)
        y_low[at, :] = pack_low(u[0, i, 0:8, :], u[1, i, 0:8, :], y0, 16)
        y_high[at, :] = pack_high(u[0, i, 56:64, :], u[1, i, 56:64, :], y0, 16)


def thirds(x):
    high = x.astype(jnp.bfloat16)
    rest = x - high.astype(f32)
    mid = rest.astype(jnp.bfloat16)
    low = (rest - mid.astype(f32)).astype(jnp.bfloat16)
    return [high, mid, low]


def pick_table(flags):
    return (lax.broadcasted_iota(jnp.int32, (128, 128), 0) == flags[8:9, :]).astype(f32).T


def place(parts, table):
    rows_in = jnp.concatenate(parts, axis=0)
    tables = jnp.concatenate([table.astype(jnp.bfloat16)] * len(parts), axis=0)
    out = lax.dot_general(rows_in, tables, (((0,), (0,)), ((), ())), preferred_element_type=f32)
    return out.reshape(8, 64, 128)


def weight_k():
    sub = lax.broadcasted_iota(jnp.int32, (8, 128), 0)
    wk = jnp.zeros((8, 128), f32)
    for k in range(8):
        wk = jnp.where(sub == k, WMAX[k], wk)
    return wk


def coef_kernel(flags, dif, coef):
    pick = pick_table(flags)
    over = pick[0:64, :] + pick[64:128, :]
    wk = weight_k()
    for m in range(3):
        coef[m] = place(thirds(dif[m]), over)
        for i in range(8):
            for j in range(8):
                at = slice(8 * j, 8 * j + 8)
                coef[m, i, at, :] = coef[m, i, at, :] * (wk * (WMAX[i] * WMAX[j] * DT))


def cross_source(lane, dk_a, dj_a, di_a, dj_b, di_b, v_a, v_b, a_a, a_b, m):
    def other(x):
        return pltpu.roll(x, 64, 1)

    left = lane < 64
    sign = jnp.where(left, 1.0, -1.0)
    swapped = other(dk_a)
    r_a = jnp.where(left, dj_b - swapped, swapped - di_b)
    mixed = jnp.where(left, dj_a, di_a)
    r_b = sign * (other(mixed) - mixed)
    turned = other(r_a)
    s_a = sign * (other(v_a) * r_b - v_b * turned)
    prod = v_a * turned
    s_b = sign * (prod - other(prod))
    return m * (a_a + DT * s_a), m * (a_b + DT * s_b)


def send_edges(e, flags, sends):
    X, Y, Z, _ = lanes()
    x0, y0 = X == 0, Y == 0
    for t in range(2):
        for q in range(2):
            low = e[t, q, pl.ds(0, 8, 8), :]
            high = e[t, q, pl.ds(7, 8, 8), :]
            e[t, q, pl.ds(0, 8, 8), :] = low + jnp.where(Z > 0, pltpu.roll(high, 1, 1), 0.0)
            e[t, q, pl.ds(7, 8, 8), :] = high + jnp.where(Z < 15, pltpu.roll(low, 127, 1), 0.0)
    ends = {}
    for t in range(2):
        for q in range(2):
            low = e[t, q, 0:8, :]
            high = e[t, q, 56:64, :]
            ends[t, q, 0] = low + jnp.where(y0, 0.0, pltpu.roll(high, 16, 1))
            ends[t, q, 7] = high + jnp.where(y0, pltpu.roll(low, 112, 1), 0.0)
    parity = is_set(flags, 0)
    for j in range(8):
        at = slice(8 * j, 8 * j + 8)
        lows, highs = [], []
        for t in range(2):
            low, high = (ends[t, q, j] if j in (0, 7) else e[t, q, at, :] for q in range(2))
            lows.append(low + jnp.where(x0, 0.0, pltpu.roll(high, 32, 1)))
            highs.append(high + jnp.where(x0, pltpu.roll(low, 96, 1), 0.0))
        send_x(lows, highs, x0, parity, sends, at)


def make_setup(sx, sy):
    def kernel(slot_hbm, adj_hbm, vel_hbm, jac_hbm, flags, a, v, mass, roll_ref, send_e, send_o, e, slot, adj, vel, jac, sems):
        copies = [pltpu.make_async_copy(slot_hbm, slot, sems.at[7])]
        copies += [pltpu.make_async_copy(adj_hbm.at[c], adj.at[c], sems.at[c]) for c in range(3)]
        copies += [pltpu.make_async_copy(vel_hbm.at[c], vel.at[c], sems.at[3 + c]) for c in range(3)]
        copies.append(pltpu.make_async_copy(jac_hbm, jac, sems.at[6]))
        for copy in copies:
            copy.start()
        gx, gy = lax.axis_index("gx"), lax.axis_index("gy")
        facts = [lax.rem(gx, 2), lax.rem(gy, 2), gx, (sx - 1) - gx, gy, (sy - 1) - gy]
        for n, fact in enumerate(facts):
            flags[n : n + 1, :] = jnp.full((1, 128), fact, jnp.int32)
        flags[6:8, :] = jnp.zeros((2, 128), jnp.int32)
        kf = roll_factors(DMAT)
        for r, factor in enumerate(kf + roll_factors(DMAT.T)):
            roll_ref[r] = factor
        lane = lanes()[3]
        wk = weight_k()
        copies[0].wait()
        flags[8:16, :] = jnp.broadcast_to(jnp.concatenate([slot[...], slot[...] + 64], axis=1), (8, 128))
        pick = pick_table(flags)
        over = pick[0:64, :] + pick[64:128, :]
        for copy in copies[1:4]:
            copy.wait()
        a[0] = place(thirds(jnp.concatenate([adj[0], adj[1]], axis=0)), pick)
        a[1] = place(thirds(adj[2]), over)
        for copy in copies[4:]:
            copy.wait()
        v[0] = place([jnp.concatenate([vel[0], vel[1]], axis=0)], pick)
        v[1] = place([vel[2]], over)
        mass[...] = place(thirds(jac[...]), over)
        ends = {}
        for q, i in enumerate((0, 7)):
            for t in range(2):
                out = along([a[t, i, 8 * j : 8 * j + 8, :] for j in range(8)], FWD)
                for j in range(8):
                    e[t, q, 8 * j : 8 * j + 8, :] = out[j]
        for j in range(8):
            at = slice(8 * j, 8 * j + 8)
            di = [along_ends([a[t, i, at, :] for i in range(8)], FWD) for t in range(2)]
            for q, i in enumerate((0, 7)):
                ends[q] = cross_source(
                    lane, along_k(a[0, i, at, :], kf), e[0, q, at, :], di[0][q], e[1, q, at, :], di[1][q],
                    v[0, i, at, :], v[1, i, at, :], a[0, i, at, :], a[1, i, at, :], mass[i, at, :] * (wk * (WMAX[i] * WMAX[j])),
                )
                for t in range(2):
                    e[t, q, at, :] = ends[q][t]
        send_edges(e, flags, (send_e, send_o))

    return kernel


def source_kernel(flags, a, v, mass_in, roll_ref, mass, u, y_low, y_high, di, dj, dk):
    lane = lanes()[3]
    wk = weight_k()
    kf = [roll_ref[r] for r in range(8)]
    for t in range(2):

        def planes(j, carry, t=t):
            xs = [a[t, i, rows(j), :] for i in range(8)]
            out = along(xs, FWD)
            for i in range(8):
                di[t, i, rows(j), :] = out[i]
                if t == 0:
                    dk[i, rows(j), :] = along_k(xs[i], kf)
            return carry

        lax.fori_loop(0, 8, planes, 0)

    def columns(n, carry):
        t, i = n // 8, n % 8
        out = along([a[t, i, 8 * j : 8 * j + 8, :] for j in range(8)], FWD)
        for j in range(8):
            dj[t, i, 8 * j : 8 * j + 8, :] = out[j]
        return carry

    lax.fori_loop(0, 16, columns, 0)

    def cross(i, carry):
        index = jnp.full((8, 128), i, jnp.int32)
        wi = jnp.zeros((8, 128), f32)
        for n in range(8):
            wi = jnp.where(index == n, WMAX[n], wi)
        for j in range(8):
            at = slice(8 * j, 8 * j + 8)
            m = mass_in[i, at, :] * (wk * (wi * WMAX[j]))
            mass[i, at, :] = m
            u[0, i, at, :], u[1, i, at, :] = cross_source(
                lane, dk[i, at, :], dj[0, i, at, :], di[0, i, at, :], dj[1, i, at, :], di[1, i, at, :],
                v[0, i, at, :], v[1, i, at, :], a[0, i, at, :], a[1, i, at, :], m,
            )
        return carry

    lax.fori_loop(0, 8, cross, 0)
    assemble_local(u, flags, y_low, y_high)


def mid_kernel(flags, got_e, got_o, y_low, y_high, _, send_e, send_o):
    X, Y, _, _ = lanes()
    x0, y0 = X == 0, Y == 0
    lows, highs = [], []
    for i in range(8):
        lows.append(y_low[8 * i : 8 * i + 8, :])
        highs.append(y_high[8 * i : 8 * i + 8, :])
    for j, into, pack in ((0, lows, pack_low), (7, highs, pack_high)):
        at = slice(8 * j, 8 * j + 8)
        low, high = received(got_e[at, :], got_o[at, :], is_set(flags, 0), is_set(flags, 2), is_set(flags, 3))
        into[0] = into[0] + pack(*unpack_low(low, x0, 32), y0, 16)
        into[7] = into[7] + pack(*unpack_high(high, x0, 32), y0, 16)
    parity = is_set(flags, 1)
    for i in range(8):
        send_e[8 * i : 8 * i + 8, :] = jnp.where(parity, lows[i], highs[i])
        send_o[8 * i : 8 * i + 8, :] = jnp.where(parity, highs[i], lows[i])


def main_kernel(step):
    def kernel(*refs):
        if step == 0:
            u, mass, coef, roll_ref, v, y = refs
        else:
            flags, u, before, mass, coef, roll_ref, v, y, stored = refs
            store(flags, before, stored)

        def planes(n, carry):
            t, j = n // 8, n % 8
            if step == 0:
                xs = [u[t, i, rows(j), :] for i in range(8)]
            else:
                xs = [SCALE * u[t, i, rows(j), :] - before[t, i, rows(j), :] for i in range(8)]
            flux = along(xs, FWD)
            out = along([coef[0, i, rows(j), :] * flux[i] for i in range(8)], BWD)
            for i in range(8):
                v[t, i, rows(j), :] = xs[i]
                part = coef[2, i, rows(j), :] * along_k(xs[i], [roll_ref[r] for r in range(8)])
                part = along_k(part, [roll_ref[8 + r] for r in range(8)])
                y[t, i, rows(j), :] = mass[i, rows(j), :] * xs[i] + out[i] + part
            return carry

        lax.fori_loop(0, 16, planes, 0)

        def columns(n, carry):
            t, i = n // 8, n % 8
            flux = along([v[t, i, 8 * j : 8 * j + 8, :] for j in range(8)], FWD)
            out = along([coef[1, i, 8 * j : 8 * j + 8, :] * flux[j] for j in range(8)], BWD)
            for j in range(8):
                at = slice(8 * j, 8 * j + 8)
                y[t, i, at, :] = y[t, i, at, :] + out[j]
            return carry

        lax.fori_loop(0, 16, columns, 0)

    return kernel


def plane_at(axis, lead, normal, plane):
    i, j = (normal, plane) if axis == 0 else (plane, normal)
    return lead + (i, slice(8 * j, 8 * j + 8), slice(None))


def outer_faces(first, got, shift, scale, t):
    if t == 0:
        return [scale * jnp.where(first, pltpu.roll(low, 128 - shift, 1), pltpu.roll(high, shift, 1)) for low, high in got]
    return [scale * jnp.where(first, low, high) for low, high in got]


def face_operator(first, axis, face, planes, mass, coef, roll_ref):
    def outer(ref, lead, plane):
        return jnp.where(first, ref[plane_at(axis, lead, 0, plane)], ref[plane_at(axis, lead, 7, plane)])

    cols = [jnp.where(first, float(DMAT[a, 0]), float(DMAT[a, 7])) for a in range(8)]
    kf = [roll_ref[r] for r in range(8)]
    kb = [roll_ref[8 + r] for r in range(8)]
    flux = along(face, FWD)
    inner = along([outer(coef, (1 - axis,), p) * flux[p] for p in range(8)], BWD)
    for p in planes:
        x = face[p]
        plane = outer(mass, (), p) * x + inner[p]
        plane = plane + along_k(outer(coef, (2,), p) * along_k(x, kf), kb)
        out = along([coef[plane_at(axis, (axis,), a, p)] * (cols[a] * x) for a in range(8)], BWD)
        out[0] = out[0] + jnp.where(first, plane, 0.0)
        out[7] = out[7] + jnp.where(first, 0.0, plane)
        yield p, out


def add_values(first, axis, face, t, v):
    for p in range(8):
        for a, part in ((0, jnp.where(first, face[p], 0.0)), (7, jnp.where(first, 0.0, face[p]))):
            index = plane_at(axis, (t,), a, p)
            v[index] = v[index] + part


def got_from(flags, even, odd, axis):
    out = []
    for p in range(8):
        at = slice(8 * p, 8 * p + 8)
        out.append(received(even[at, :], odd[at, :], is_set(flags, axis), is_set(flags, 2 + 2 * axis), is_set(flags, 3 + 2 * axis)))
    return out


def x_kernel(step):
    last = step == STEPS - 1

    def kernel(flags, xe, xo, mass, coef, roll_ref, y_in, *refs):
        y = refs[-1]
        first = lanes()[0] == 0
        got = got_from(flags, xe, xo, 0)
        for t in range(2):
            face = outer_faces(first, got, 32, SCALE if step else 1.0, t)
            for p, out in face_operator(first, 0, face, range(8), mass, coef, roll_ref):
                for a in range(8):
                    index = plane_at(0, (t,), a, p)
                    y[index] = y_in[index] + out[a]
        if not last:
            return
        v_in, older, v, dots = refs[0], refs[1 : 1 + step], refs[-3], refs[-2]
        for t in range(2):
            for i in range(8):
                for j in range(8):
                    index = plane_at(0, (t,), i, j)
                    v[index] = v_in[index]
            add_values(first, 0, outer_faces(first, got, 32, SCALE, t), t, v)

        def products(t):
            def body(i, sums):
                sums = list(sums)
                for j in range(8):
                    at = slice(8 * j, 8 * j + 8)
                    total = y[t, i, at, :]
                    for m in range(step):
                        sums[m] = sums[m] + older[m][t, i, at, :] * total
                    sums[step] = sums[step] + v[t, i, at, :] * total
                return tuple(sums)

            return lax.fori_loop(0, 8, body, tuple(jnp.zeros((8, 128), f32) for _ in range(step + 1)))

        for m, (p, q) in enumerate(zip(products(0), products(1))):
            dots[8 * m : 8 * m + 8, :] = p + 0.5 * q

    return kernel


def last_kernel(flags, ye, yo, mass, coef, roll_ref, f0, f1, f2, early, dots_in, v_in, y_in, v, message):
    first = lanes()[1] == 0
    got = got_from(flags, ye, yo, 1)
    kf = [roll_ref[r] for r in range(8)]
    kb = [roll_ref[8 + r] for r in range(8)]
    squares = [jnp.where(first, float(DMAT[a, 0]) ** 2, float(DMAT[a, 7]) ** 2) for a in range(8)]

    def outer(ref, lead, plane):
        return jnp.where(first, ref[plane_at(1, lead, 0, plane)], ref[plane_at(1, lead, 7, plane)])

    sums = [dots_in[8 * m : 8 * m + 8, :] for m in range(4)]
    for t in range(2):
        for i in range(8):
            for j in range(8):
                index = plane_at(0, (t,), i, j)
                v[index] = v_in[index]
        face = outer_faces(first, got, 16, SCALE, t)
        add_values(first, 1, face, t, v)
        flux = along(face, FWD)
        inner = along([outer(coef, (0,), p) * flux[p] for p in range(8)], BWD)
        part = [None] * 4
        for p in range(8):
            x = face[p]
            normal = outer(mass, (), p)
            for a in range(8):
                normal = normal + squares[a] * coef[plane_at(1, (1,), a, p)]
            own = normal * x + inner[p] + along_k(outer(coef, (2,), p) * along_k(x, kf), kb)
            own = own + 2.0 * outer(y_in, (t,), p)
            for m, value in enumerate([ref[t, 8 * p : 8 * p + 8, :] for ref in (f0, f1, f2)] + [own]):
                part[m] = x * value if part[m] is None else part[m] + x * value
        sums = [s + (1.0 if t == 0 else 0.5) * q for s, q in zip(sums, part)]
    row_of = lax.broadcasted_iota(jnp.int32, (16, 128), 0)
    lane_of = lax.broadcasted_iota(jnp.int32, (16, 128), 1)
    table = jnp.zeros((16, 128), f32)
    every = [early[8 * m : 8 * m + 8, :] for m in range(7)] + sums
    for m, value in enumerate(every):
        table = jnp.where(row_of == m, jnp.sum(value, axis=0, keepdims=True), table)
    column = jnp.sum(table, axis=1, keepdims=True)
    line = jnp.sum(jnp.where(row_of == lane_of, column, 0.0), axis=0, keepdims=True)
    message[...] = jnp.broadcast_to(line, message.shape)


def edge_kernel(step):
    def kernel(flags, ye, yo, mass, coef, roll_ref, y_in, send_e, send_o, e):
        y0 = lanes()[1] == 0
        got = got_from(flags, ye, yo, 1)
        for t in range(2):
            face = outer_faces(y0, got, 16, SCALE if step else 1.0, t)
            for p, out in face_operator(y0, 1, face, (0, 7), mass, coef, roll_ref):
                for a in range(8):
                    at = slice(8 * a, 8 * a + 8)
                    e[t, p // 7, at, :] = y_in[t, p, at, :] + out[a]
        send_edges(e, flags, (send_e, send_o))

    return kernel


def y_kernel(step):
    n_dots = step + 1 + (step == 0)

    def kernel(flags, xe, xo, ye, yo, mass, coef, roll_ref, *refs):
        older = refs[:step]
        v_in, y_in, v, y, y_low, y_high, dots, outer_y = refs[step:]
        X, Y, Z, lane = lanes()
        scale = SCALE if step else 1.0
        for t in range(2):
            for i in range(8):
                for j in range(8):
                    index = plane_at(0, (t,), i, j)
                    v[index] = v_in[index]
        got_x, got_y = got_from(flags, xe, xo, 0), got_from(flags, ye, yo, 1)
        for t in range(2):
            add_values(X == 0, 0, outer_faces(X == 0, got_x, 32, scale, t), t, v)
            face = outer_faces(Y == 0, got_y, 16, scale, t)
            add_values(Y == 0, 1, face, t, v)
            for p, out in face_operator(Y == 0, 1, face, range(8), mass, coef, roll_ref):
                for a in range(8):
                    index = plane_at(1, (t,), a, p)
                    y[index] = y_in[index] + out[a]
        if step == 0:
            sub = lax.broadcasted_iota(jnp.int32, (8, 128), 0)
            wz = jnp.where(((Z > 0) & (sub == 0)) | ((Z < 15) & (sub == 7)), 0.5, 1.0)
            wy_low = jnp.where((Y == 1) | is_set(flags, 4), 0.5, 1.0)
            wy_high = jnp.where((Y == 0) | is_set(flags, 5), 0.5, 1.0)
            wx_low = jnp.where((X == 1) | is_set(flags, 2), 0.5, 1.0)
            wx_high = jnp.where((X == 0) | is_set(flags, 3), 0.5, 1.0)

        def products(t):
            def body(i, sums):
                sums = list(sums)
                squares = []
                for j in range(8):
                    at = slice(8 * j, 8 * j + 8)
                    total = y[t, i, at, :]
                    own = v[t, i, at, :]
                    for m in range(step):
                        sums[m] = sums[m] + older[m][t, i, at, :] * total
                    sums[step] = sums[step] + own * total
                    squares.append(own * own)
                if step == 0:
                    index = jnp.full((8, 128), i, jnp.int32)
                    wx = wz * jnp.where(index == 0, wx_low, jnp.where(index == 7, wx_high, 1.0))
                    square = squares[1]
                    for j in range(2, 7):
                        square = square + squares[j]
                    square = square + wy_low * squares[0] + wy_high * squares[7]
                    sums[1] = sums[1] + wx * square
                return tuple(sums)

            return lax.fori_loop(0, 8, body, tuple(jnp.zeros((8, 128), f32) for _ in range(n_dots)))

        sums = [p + 0.5 * q for p, q in zip(products(0), products(1))]
        for m in range(n_dots):
            dots[8 * m : 8 * m + 8, :] = sums[m]
        for t in range(2):
            for i in range(8):
                outer_y[t, 8 * i : 8 * i + 8, :] = jnp.where(Y == 0, y[t, i, 0:8, :], y[t, i, 56:64, :])
        assemble_local(y, flags, y_low, y_high)

    return kernel


def store(flags, v, stored):
    pick = pick_table(flags).astype(jnp.bfloat16)
    for t in range(2):
        table = jnp.concatenate([pick if t == 0 else pick[0:64, :]] * 3, axis=1)
        x = jnp.concatenate(thirds(v[t].reshape(512, 128)), axis=1)
        res = lax.dot_general(table, x, (((1,), (1,)), ((), ())), preferred_element_type=f32)
        if t == 0:
            stored[0] = res[0:64, :]
            stored[1] = res[64:128, :]
        else:
            stored[2] = res


def finish_kernel(flags, got, stored0, stored1, stored2, v, out_hbm, stored3, out, sems):
    store(flags, v, stored3)
    stored = (stored0, stored1, stored2, stored3)
    total = jnp.sum(got[...], axis=0, keepdims=True)
    lane = lax.broadcasted_iota(jnp.int32, (1, 128), 1)

    def entry(m):
        return jnp.sum(jnp.where(lane == m, total, 0.0), axis=1, keepdims=True)

    gram = {}
    order = [(0, 0), None, (0, 1), (1, 1), (0, 2), (1, 2), (2, 2), (0, 3), (1, 3), (2, 3), (3, 3)]
    for m, pair in enumerate(order):
        if pair is None:
            square = entry(m)
        else:
            gram[pair] = entry(m)
    right = [square]
    for j in range(3):
        right.append(SCALE * gram[(0, j)] - right[j])
    lower, inverse, reduced = {}, [], []
    for c in range(4):
        pivot = gram[(c, c)]
        value = right[c]
        for m in range(c):
            pivot = pivot - lower[(c, m)] * lower[(c, m)] * inverse[m]
            value = value - lower[(c, m)] * reduced[m] * inverse[m]
        good = pivot > 1e-6 * gram[(c, c)]
        inverse.append(jnp.where(good, 1.0 / jnp.where(good, pivot, 1.0), 0.0))
        reduced.append(value)
        for r in range(c + 1, 4):
            acc = gram[(c, r)]
            for m in range(c):
                acc = acc - lower[(r, m)] * lower[(c, m)] * inverse[m]
            lower[(r, c)] = acc
    weight = [None] * 4
    for c in reversed(range(4)):
        acc = reduced[c]
        for r in range(c + 1, 4):
            acc = acc - lower[(r, c)] * weight[r]
        weight[c] = acc * inverse[c]
    copies = []
    for n in range(3):
        for half in range(2):
            at = slice(32 * half, 32 * half + 32)
            x = weight[0] * stored[0][n, at, :]
            for c in range(1, 4):
                x = x + weight[c] * stored[c][n, at, :]
            out[n, at, :] = x
            copies.append(pltpu.make_async_copy(out.at[n, pl.ds(32 * half, 32)], out_hbm.at[n, pl.ds(32 * half, 32)], sems.at[2 * n + half]))
            copies[-1].start()
    for copy in copies:
        copy.wait()


def swaps(sx, sy, along_x, odd):
    pairs = []
    for g in range(sx):
        for h in range(sy):
            at, count = (g, sx) if along_x else (h, sy)
            other = at + 1 if at % 2 == odd else at - 1
            if along_x:
                to = (other, h) if 0 <= other < count else (g, h ^ 1)
            else:
                to = (g, other) if 0 <= other < count else (g ^ 1, h)
            pairs.append((g * sy + h, to[0] * sy + to[1]))
    return pairs


def solution(mesh):
    vmem = pl.BlockSpec(memory_space=pltpu.VMEM)
    params = pltpu.CompilerParams(vmem_limit_bytes=40 * 1024 * 1024)
    sx, sy = mesh.shape["gx"], mesh.shape["gy"]

    def shape(*dims):
        return jax.ShapeDtypeStruct(dims, f32)

    field, face = shape(2, 8, 64, 128), shape(64, 128)

    anywhere = pl.BlockSpec(memory_space=pltpu.HBM)

    def call(kernel, outs, ins, scratch=(), name=None, cost=None):
        return pl.pallas_call(
            kernel,
            out_shape=outs,
            in_specs=ins if isinstance(ins, list) else [vmem] * ins,
            out_specs=[vmem] * len(outs),
            scratch_shapes=scratch,
            compiler_params=params,
            cost_estimate=pl.CostEstimate(flops=0, transcendentals=0, bytes_accessed=cost) if cost else None,
            name=name,
        )

    def held(x):
        return pltpu.with_memory_space_constraint(x, pltpu.HBM)

    def local(adjoint_field, velocity, diffusivity, jacobian, element_slot):
        big = pltpu.VMEM((2, 8, 64, 128), f32)
        flags, a, v, mass, table, xe, xo = call(
            make_setup(sx, sy),
            [jax.ShapeDtypeStruct((16, 128), jnp.int32), field, field, shape(8, 64, 128), shape(16, 8, 128), face, face],
            [anywhere] * 4,
            [
                pltpu.VMEM((2, 2, 64, 128), f32),
                pltpu.VMEM((1, 64), jnp.int32),
                pltpu.VMEM((3, 64, 512), f32),
                pltpu.VMEM((3, 64, 512), jnp.bfloat16),
                pltpu.VMEM((64, 512), f32),
                pltpu.SemaphoreType.DMA((8,)),
            ],
            "setup",
        )(held(element_slot.reshape(1, 64)), held(adjoint_field.reshape(3, 64, 512)), held(velocity.reshape(3, 64, 512)), held(jacobian.reshape(64, 512)))
        mass, u, yl, yh = call(
            source_kernel, [shape(8, 64, 128), field, face, face], 5, [big, big, pltpu.VMEM((8, 64, 128), f32)], "source", cost=8 << 20
        )(flags, a, v, mass, table)
        (coef,) = call(coef_kernel, [shape(3, 8, 64, 128)], 2, name="coef", cost=3 << 20)(flags, diffusivity.reshape(3, 64, 512))
        vs, parts, stored, faces = [], [], [], []
        for step in range(STEPS):
            xe = lax.ppermute(xe, ("gx", "gy"), swaps(sx, sy, True, 0))
            xo = lax.ppermute(xo, ("gx", "gy"), swaps(sx, sy, True, 1))
            shared = [mass, coef, table]
            if step == 0:
                v, y = call(main_kernel(step), [field, field], 4, name="main0", cost=8 << 20)(u, *shared)
            else:
                v, y, moved = call(main_kernel(step), [field, field, shape(3, 64, 512)], 6, name=f"main{step}", cost=8 << 20)(flags, u, vs[-1], *shared)
                stored.append(moved)
            ye, yo = call(mid_kernel, [face, face], [vmem] * 5 + [anywhere], name="mid")(flags, xe, xo, yl, yh, u)
            ye = lax.ppermute(ye, ("gx", "gy"), swaps(sx, sy, False, 0))
            yo = lax.ppermute(yo, ("gx", "gy"), swaps(sx, sy, False, 1))
            if step < STEPS - 1:
                (y,) = call(x_kernel(step), [field], 7, name=f"xpart{step}", cost=8 << 20)(flags, xe, xo, *shared, y)
                args = [flags, xe, xo, ye, yo] + shared + vs
                xe, xo = call(edge_kernel(step), [face, face], 7, [pltpu.VMEM((2, 2, 64, 128), f32)], f"edge{step}")(flags, ye, yo, *shared, y)
                n_dots = step + 1 + (step == 0)
                v, u, yl, yh, dots, outer_y = call(
                    y_kernel(step),
                    [field, field, face, face, shape(8 * n_dots, 128), shape(2, 64, 128)],
                    len(args) + 2,
                    name=f"ypart{step}",
                    cost=8 << 20,
                )(*args, v, y)
                vs.append(v)
                parts.append(dots)
                faces.append(outer_y)
            else:
                early = jnp.concatenate(parts, axis=0)
                v, dots, y = call(x_kernel(step), [field, shape(32, 128), field], 11, name=f"xpart{step}", cost=8 << 20)(flags, xe, xo, *shared, y, v, *vs)
                v, message = call(last_kernel, [field, shape(sx * sy, 128)], 13, name="last")(flags, ye, yo, *shared, *faces, early, dots, v, y)
        got = lax.all_to_all(message.reshape(sx * sy, 1, 128), ("gx", "gy"), 0, 0).reshape(sx * sy, 128)
        (out,) = pl.pallas_call(
            finish_kernel,
            out_shape=[shape(3, 64, 512)],
            in_specs=[vmem] * 6,
            out_specs=[anywhere],
            scratch_shapes=[pltpu.VMEM((3, 64, 512), f32), pltpu.VMEM((3, 64, 512), f32), pltpu.SemaphoreType.DMA((6,))],
            compiler_params=params,
            name="finish",
        )(flags, got, *stored, v)
        return out.reshape(3, 1, 1, 64, 512)

    in_specs = (
        P(None, "gx", "gy", None, None),
        P(None, "gx", "gy", None, None),
        P(None, "gx", "gy", None, None),
        P("gx", "gy", None, None),
        P("gx", "gy", None),
    )
    return jax.shard_map(local, mesh=mesh, in_specs=in_specs, out_specs=P(None, "gx", "gy", None, None), check_vma=False)
```

```python
import jax
import jax.numpy as jnp
import numpy as np
from jax import lax
from jax.experimental import pallas as pl
from jax.experimental.pallas import tpu as pltpu
from jax.sharding import PartitionSpec as P


STEPS = 4
DT = 0.25
SCALE = 0.5
f32 = jnp.float32


def legendre_seven(points):
    previous = points * 0.0 + 1.0
    current = points
    for degree in range(1, 7):
        following = ((2 * degree + 1) * points * current - degree * previous) / (degree + 1)
        previous = current
        current = following
    return current


def gll_tables():
    poly_order = 7
    points = np.array(
        [
            -1.0,
            -0.8717401485096066,
            -0.5917001814331423,
            -0.2092992179024789,
            0.2092992179024789,
            0.5917001814331423,
            0.8717401485096066,
            1.0,
        ]
    )
    end_values = legendre_seven(points)
    weights = 2.0 / (poly_order * (poly_order + 1) * end_values**2)
    spread = points[:, None] - points[None, :]
    identity = np.eye(poly_order + 1)
    diff_table = end_values[:, None] / (end_values[None, :] * (spread + identity))
    diff_table = diff_table * (1.0 - identity)
    corners = np.zeros(poly_order + 1)
    corners[0] = -poly_order * (poly_order + 1) / 4.0
    corners[-1] = poly_order * (poly_order + 1) / 4.0
    diff_table = diff_table + identity * corners[None, :]
    return (weights.astype(np.float32), diff_table.astype(np.float32))


WEIGHTS, DMAT = gll_tables()
WMAX = [float(w) for w in WEIGHTS]


def halves(mat):
    mat = mat.astype(np.float64)
    assert np.array_equal(mat[::-1, ::-1], -mat)
    odd = 0.5 * (mat[:4, :4] - mat[:4, 7:3:-1])
    even = 0.5 * (mat[:4, :4] + mat[:4, 7:3:-1])
    return odd, even


FWD = halves(DMAT)
BWD = halves(DMAT.T)


def roll_factors(mat):
    sub = lax.broadcasted_iota(jnp.int32, (8, 128), 0)
    out = []
    for r in range(8):
        factor = jnp.full((8, 128), float(mat[0, -r % 8]), f32)
        for k in range(1, 8):
            factor = jnp.where(sub == k, float(mat[k, (k - r) % 8]), factor)
        out.append(factor)
    return out


def along(xs, tables):
    odd, even = tables
    diff = [xs[b] - xs[7 - b] for b in range(4)]
    both = [xs[b] + xs[7 - b] for b in range(4)]
    out = [None] * 8
    for a in range(4):
        s = float(odd[a, 0]) * diff[0]
        t = float(even[a, 0]) * both[0]
        for b in range(1, 4):
            s = s + float(odd[a, b]) * diff[b]
            t = t + float(even[a, b]) * both[b]
        out[a] = s + t
        out[7 - a] = s - t
    return out


def along_ends(xs, tables):
    odd, even = tables
    s = float(odd[0, 0]) * (xs[0] - xs[7])
    t = float(even[0, 0]) * (xs[0] + xs[7])
    for b in range(1, 4):
        s = s + float(odd[0, b]) * (xs[b] - xs[7 - b])
        t = t + float(even[0, b]) * (xs[b] + xs[7 - b])
    return s + t, s - t


def along_k(x, coef):
    out = coef[0] * x
    for r in range(1, 8):
        out = out + coef[r] * pltpu.roll(x, r, 0)
    return out


def lanes():
    lane = lax.broadcasted_iota(jnp.int32, (8, 128), 1)
    return (lane // 32) % 2, (lane // 16) % 2, lane % 16, lane


def is_set(flags, index):
    return jnp.broadcast_to(flags[index : index + 1, :], (8, 128)) != 0


def rows(j):
    return pl.ds(pl.multiple_of(8 * j, 8), 8)


def pack_low(face0, face1, first, shift):
    return jnp.where(first, face0, pltpu.roll(face1, shift, 1))


def pack_high(face0, face1, first, shift):
    return jnp.where(first, pltpu.roll(face1, 128 - shift, 1), face0)


def unpack_high(got, first, shift):
    zero = jnp.zeros_like(got)
    return jnp.where(first, zero, pltpu.roll(got, shift, 1)), jnp.where(first, zero, got)


def unpack_low(got, first, shift):
    zero = jnp.zeros_like(got)
    return jnp.where(first, pltpu.roll(got, 128 - shift, 1), zero), jnp.where(first, got, zero)


def received(even, odd, parity, has_low, has_high):
    zero = jnp.zeros_like(even)
    low = jnp.where(has_low, jnp.where(parity, even, odd), zero)
    high = jnp.where(has_high, jnp.where(parity, odd, even), zero)
    return low, high


def send_x(lows, highs, x0, parity, sends, at):
    to_low = pack_low(lows[0], lows[1], x0, 32)
    to_high = pack_high(highs[0], highs[1], x0, 32)
    sends[0][at, :] = jnp.where(parity, to_low, to_high)
    sends[1][at, :] = jnp.where(parity, to_high, to_low)


def assemble_local(u, flags, y_low, y_high):
    X, Y, Z, _ = lanes()
    x0, y0 = X == 0, Y == 0
    for t in range(2):
        for i in range(8):
            low = u[t, i, pl.ds(0, 8, 8), :]
            high = u[t, i, pl.ds(7, 8, 8), :]
            u[t, i, pl.ds(0, 8, 8), :] = low + jnp.where(Z > 0, pltpu.roll(high, 1, 1), 0.0)
            u[t, i, pl.ds(7, 8, 8), :] = high + jnp.where(Z < 15, pltpu.roll(low, 127, 1), 0.0)
    for t in range(2):
        for i in range(8):
            low = u[t, i, 0:8, :]
            high = u[t, i, 56:64, :]
            u[t, i, 0:8, :] = low + jnp.where(y0, 0.0, pltpu.roll(high, 16, 1))
            u[t, i, 56:64, :] = high + jnp.where(y0, pltpu.roll(low, 112, 1), 0.0)
    for j in range(8):
        at = slice(8 * j, 8 * j + 8)
        lows, highs = [], []
        for t in range(2):
            low = u[t, 0, at, :]
            high = u[t, 7, at, :]
            lows.append(low + jnp.where(x0, 0.0, pltpu.roll(high, 32, 1)))
            highs.append(high + jnp.where(x0, pltpu.roll(low, 96, 1), 0.0))
            u[t, 0, at, :] = lows[t]
            u[t, 7, at, :] = highs[t]
    for i in range(8):
        at = slice(8 * i, 8 * i + 8)
        y_low[at, :] = pack_low(u[0, i, 0:8, :], u[1, i, 0:8, :], y0, 16)
        y_high[at, :] = pack_high(u[0, i, 56:64, :], u[1, i, 56:64, :], y0, 16)


def thirds(x):
    high = x.astype(jnp.bfloat16)
    rest = x - high.astype(f32)
    mid = rest.astype(jnp.bfloat16)
    low = (rest - mid.astype(f32)).astype(jnp.bfloat16)
    return [high, mid, low]


def pick_table(flags):
    return (lax.broadcasted_iota(jnp.int32, (128, 128), 0) == flags[8:9, :]).astype(f32).T


def place(parts, table):
    rows_in = jnp.concatenate(parts, axis=0)
    tables = jnp.concatenate([table.astype(jnp.bfloat16)] * len(parts), axis=0)
    out = lax.dot_general(rows_in, tables, (((0,), (0,)), ((), ())), preferred_element_type=f32)
    return out.reshape(8, 64, 128)


def weight_k():
    sub = lax.broadcasted_iota(jnp.int32, (8, 128), 0)
    wk = jnp.zeros((8, 128), f32)
    for k in range(8):
        wk = jnp.where(sub == k, WMAX[k], wk)
    return wk


def coef_kernel(flags, dif, coef):
    pick = pick_table(flags)
    over = pick[0:64, :] + pick[64:128, :]
    wk = weight_k()
    for m in range(3):
        coef[m] = place(thirds(dif[m]), over)
        for i in range(8):
            for j in range(8):
                at = slice(8 * j, 8 * j + 8)
                coef[m, i, at, :] = coef[m, i, at, :] * (wk * (WMAX[i] * WMAX[j] * DT))


def cross_source(lane, dk_a, dj_a, di_a, dj_b, di_b, v_a, v_b, a_a, a_b, m):
    def other(x):
        return pltpu.roll(x, 64, 1)

    left = lane < 64
    sign = jnp.where(left, 1.0, -1.0)
    swapped = other(dk_a)
    r_a = jnp.where(left, dj_b - swapped, swapped - di_b)
    mixed = jnp.where(left, dj_a, di_a)
    r_b = sign * (other(mixed) - mixed)
    turned = other(r_a)
    s_a = sign * (other(v_a) * r_b - v_b * turned)
    prod = v_a * turned
    s_b = sign * (prod - other(prod))
    return m * (a_a + DT * s_a), m * (a_b + DT * s_b)


def send_edges(e, flags, sends):
    X, Y, Z, _ = lanes()
    x0, y0 = X == 0, Y == 0
    for t in range(2):
        for q in range(2):
            low = e[t, q, pl.ds(0, 8, 8), :]
            high = e[t, q, pl.ds(7, 8, 8), :]
            e[t, q, pl.ds(0, 8, 8), :] = low + jnp.where(Z > 0, pltpu.roll(high, 1, 1), 0.0)
            e[t, q, pl.ds(7, 8, 8), :] = high + jnp.where(Z < 15, pltpu.roll(low, 127, 1), 0.0)
    ends = {}
    for t in range(2):
        for q in range(2):
            low = e[t, q, 0:8, :]
            high = e[t, q, 56:64, :]
            ends[t, q, 0] = low + jnp.where(y0, 0.0, pltpu.roll(high, 16, 1))
            ends[t, q, 7] = high + jnp.where(y0, pltpu.roll(low, 112, 1), 0.0)
    parity = is_set(flags, 0)
    for j in range(8):
        at = slice(8 * j, 8 * j + 8)
        lows, highs = [], []
        for t in range(2):
            low, high = (ends[t, q, j] if j in (0, 7) else e[t, q, at, :] for q in range(2))
            lows.append(low + jnp.where(x0, 0.0, pltpu.roll(high, 32, 1)))
            highs.append(high + jnp.where(x0, pltpu.roll(low, 96, 1), 0.0))
        send_x(lows, highs, x0, parity, sends, at)


def make_setup(sx, sy):
    def kernel(slot_hbm, adj_hbm, vel_hbm, jac_hbm, flags, a, v, mass, roll_ref, send_e, send_o, e, slot, adj, vel, jac, sems):
        copies = [pltpu.make_async_copy(slot_hbm, slot, sems.at[7])]
        copies += [
            pltpu.make_async_copy(adj_hbm.at[c, pl.ds(32 * h, 32)], adj.at[c, pl.ds(32 * h, 32)], sems.at[8 * h + c]) for c in range(3) for h in range(2)
        ]
        copies += [pltpu.make_async_copy(vel_hbm.at[c], vel.at[c], sems.at[3 + c]) for c in range(3)]
        copies.append(pltpu.make_async_copy(jac_hbm, jac, sems.at[6]))
        for copy in copies:
            copy.start()
        gx, gy = lax.axis_index("gx"), lax.axis_index("gy")
        facts = [lax.rem(gx, 2), lax.rem(gy, 2), gx, (sx - 1) - gx, gy, (sy - 1) - gy]
        for n, fact in enumerate(facts):
            flags[n : n + 1, :] = jnp.full((1, 128), fact, jnp.int32)
        flags[6:8, :] = jnp.zeros((2, 128), jnp.int32)
        kf = roll_factors(DMAT)
        for r, factor in enumerate(kf + roll_factors(DMAT.T)):
            roll_ref[r] = factor
        lane = lanes()[3]
        wk = weight_k()
        copies[0].wait()
        flags[8:16, :] = jnp.broadcast_to(jnp.concatenate([slot[...], slot[...] + 64], axis=1), (8, 128))
        pick = pick_table(flags)
        over = pick[0:64, :] + pick[64:128, :]
        for copy in copies[1:7]:
            copy.wait()
        a[0] = place(thirds(jnp.concatenate([adj[0], adj[1]], axis=0)), pick)
        a[1] = place(thirds(adj[2]), over)
        for copy in copies[7:]:
            copy.wait()
        v[0] = place([jnp.concatenate([vel[0], vel[1]], axis=0)], pick)
        v[1] = place([vel[2]], over)
        mass[...] = place(thirds(jac[...]), over)
        ends = {}
        for q, i in enumerate((0, 7)):
            for t in range(2):
                out = along([a[t, i, 8 * j : 8 * j + 8, :] for j in range(8)], FWD)
                for j in range(8):
                    e[t, q, 8 * j : 8 * j + 8, :] = out[j]
        for j in range(8):
            at = slice(8 * j, 8 * j + 8)
            di = [along_ends([a[t, i, at, :] for i in range(8)], FWD) for t in range(2)]
            for q, i in enumerate((0, 7)):
                ends[q] = cross_source(
                    lane, along_k(a[0, i, at, :], kf), e[0, q, at, :], di[0][q], e[1, q, at, :], di[1][q],
                    v[0, i, at, :], v[1, i, at, :], a[0, i, at, :], a[1, i, at, :], mass[i, at, :] * (wk * (WMAX[i] * WMAX[j])),
                )
                for t in range(2):
                    e[t, q, at, :] = ends[q][t]
        send_edges(e, flags, (send_e, send_o))

    return kernel


def source_kernel(flags, a, v, mass_in, roll_ref, mass, u, y_low, y_high, di, dj, dk):
    lane = lanes()[3]
    wk = weight_k()
    kf = [roll_ref[r] for r in range(8)]
    for t in range(2):

        def planes(j, carry, t=t):
            xs = [a[t, i, rows(j), :] for i in range(8)]
            out = along(xs, FWD)
            for i in range(8):
                di[t, i, rows(j), :] = out[i]
                if t == 0:
                    dk[i, rows(j), :] = along_k(xs[i], kf)
            return carry

        lax.fori_loop(0, 8, planes, 0)

    def columns(n, carry):
        t, i = n // 8, n % 8
        out = along([a[t, i, 8 * j : 8 * j + 8, :] for j in range(8)], FWD)
        for j in range(8):
            dj[t, i, 8 * j : 8 * j + 8, :] = out[j]
        return carry

    lax.fori_loop(0, 16, columns, 0)

    def cross(i, carry):
        index = jnp.full((8, 128), i, jnp.int32)
        wi = jnp.zeros((8, 128), f32)
        for n in range(8):
            wi = jnp.where(index == n, WMAX[n], wi)
        for j in range(8):
            at = slice(8 * j, 8 * j + 8)
            m = mass_in[i, at, :] * (wk * (wi * WMAX[j]))
            mass[i, at, :] = m
            u[0, i, at, :], u[1, i, at, :] = cross_source(
                lane, dk[i, at, :], dj[0, i, at, :], di[0, i, at, :], dj[1, i, at, :], di[1, i, at, :],
                v[0, i, at, :], v[1, i, at, :], a[0, i, at, :], a[1, i, at, :], m,
            )
        return carry

    lax.fori_loop(0, 8, cross, 0)
    assemble_local(u, flags, y_low, y_high)


def mid_kernel(flags, got_e, got_o, y_low, y_high, _, send_e, send_o):
    X, Y, _, _ = lanes()
    x0, y0 = X == 0, Y == 0
    lows, highs = [], []
    for i in range(8):
        lows.append(y_low[8 * i : 8 * i + 8, :])
        highs.append(y_high[8 * i : 8 * i + 8, :])
    for j, into, pack in ((0, lows, pack_low), (7, highs, pack_high)):
        at = slice(8 * j, 8 * j + 8)
        low, high = received(got_e[at, :], got_o[at, :], is_set(flags, 0), is_set(flags, 2), is_set(flags, 3))
        into[0] = into[0] + pack(*unpack_low(low, x0, 32), y0, 16)
        into[7] = into[7] + pack(*unpack_high(high, x0, 32), y0, 16)
    parity = is_set(flags, 1)
    for i in range(8):
        send_e[8 * i : 8 * i + 8, :] = jnp.where(parity, lows[i], highs[i])
        send_o[8 * i : 8 * i + 8, :] = jnp.where(parity, highs[i], lows[i])


def main_kernel(step):
    def kernel(*refs):
        if step == 0:
            u, mass, coef, roll_ref, v, y = refs
        else:
            flags, u, before, mass, coef, roll_ref, v, y, stored = refs
            store(flags, before, stored)

        def planes(n, carry):
            t, j = n // 8, n % 8
            if step == 0:
                xs = [u[t, i, rows(j), :] for i in range(8)]
            else:
                xs = [SCALE * u[t, i, rows(j), :] - before[t, i, rows(j), :] for i in range(8)]
            flux = along(xs, FWD)
            out = along([coef[0, i, rows(j), :] * flux[i] for i in range(8)], BWD)
            for i in range(8):
                v[t, i, rows(j), :] = xs[i]
                part = coef[2, i, rows(j), :] * along_k(xs[i], [roll_ref[r] for r in range(8)])
                part = along_k(part, [roll_ref[8 + r] for r in range(8)])
                y[t, i, rows(j), :] = mass[i, rows(j), :] * xs[i] + out[i] + part
            return carry

        lax.fori_loop(0, 16, planes, 0)

        def columns(n, carry):
            t, i = n // 8, n % 8
            flux = along([v[t, i, 8 * j : 8 * j + 8, :] for j in range(8)], FWD)
            out = along([coef[1, i, 8 * j : 8 * j + 8, :] * flux[j] for j in range(8)], BWD)
            for j in range(8):
                at = slice(8 * j, 8 * j + 8)
                y[t, i, at, :] = y[t, i, at, :] + out[j]
            return carry

        lax.fori_loop(0, 16, columns, 0)

    return kernel


def plane_at(axis, lead, normal, plane):
    i, j = (normal, plane) if axis == 0 else (plane, normal)
    return lead + (i, slice(8 * j, 8 * j + 8), slice(None))


def outer_faces(first, got, shift, scale, t):
    if t == 0:
        return [scale * jnp.where(first, pltpu.roll(low, 128 - shift, 1), pltpu.roll(high, shift, 1)) for low, high in got]
    return [scale * jnp.where(first, low, high) for low, high in got]


def face_operator(first, axis, face, planes, mass, coef, roll_ref):
    def outer(ref, lead, plane):
        return jnp.where(first, ref[plane_at(axis, lead, 0, plane)], ref[plane_at(axis, lead, 7, plane)])

    cols = [jnp.where(first, float(DMAT[a, 0]), float(DMAT[a, 7])) for a in range(8)]
    kf = [roll_ref[r] for r in range(8)]
    kb = [roll_ref[8 + r] for r in range(8)]
    flux = along(face, FWD)
    inner = along([outer(coef, (1 - axis,), p) * flux[p] for p in range(8)], BWD)
    for p in planes:
        x = face[p]
        plane = outer(mass, (), p) * x + inner[p]
        plane = plane + along_k(outer(coef, (2,), p) * along_k(x, kf), kb)
        out = along([coef[plane_at(axis, (axis,), a, p)] * (cols[a] * x) for a in range(8)], BWD)
        out[0] = out[0] + jnp.where(first, plane, 0.0)
        out[7] = out[7] + jnp.where(first, 0.0, plane)
        yield p, out


def add_values(first, axis, face, t, v):
    for p in range(8):
        for a, part in ((0, jnp.where(first, face[p], 0.0)), (7, jnp.where(first, 0.0, face[p]))):
            index = plane_at(axis, (t,), a, p)
            v[index] = v[index] + part


def got_from(flags, even, odd, axis):
    out = []
    for p in range(8):
        at = slice(8 * p, 8 * p + 8)
        out.append(received(even[at, :], odd[at, :], is_set(flags, axis), is_set(flags, 2 + 2 * axis), is_set(flags, 3 + 2 * axis)))
    return out


def x_kernel(step):
    last = step == STEPS - 1

    def kernel(flags, xe, xo, mass, coef, roll_ref, y_in, *refs):
        y = refs[-1]
        first = lanes()[0] == 0
        got = got_from(flags, xe, xo, 0)
        for t in range(2):
            face = outer_faces(first, got, 32, SCALE if step else 1.0, t)
            for p, out in face_operator(first, 0, face, range(8), mass, coef, roll_ref):
                for a in range(8):
                    index = plane_at(0, (t,), a, p)
                    y[index] = y_in[index] + out[a]
        if not last:
            return
        v_in, older, v, dots = refs[0], refs[1 : 1 + step], refs[-3], refs[-2]
        for t in range(2):
            for i in range(8):
                for j in range(8):
                    index = plane_at(0, (t,), i, j)
                    v[index] = v_in[index]
            add_values(first, 0, outer_faces(first, got, 32, SCALE, t), t, v)

        def products(t):
            def body(i, sums):
                sums = list(sums)
                for j in range(8):
                    at = slice(8 * j, 8 * j + 8)
                    total = y[t, i, at, :]
                    for m in range(step):
                        sums[m] = sums[m] + older[m][t, i, at, :] * total
                    sums[step] = sums[step] + v[t, i, at, :] * total
                return tuple(sums)

            return lax.fori_loop(0, 8, body, tuple(jnp.zeros((8, 128), f32) for _ in range(step + 1)))

        for m, (p, q) in enumerate(zip(products(0), products(1))):
            dots[8 * m : 8 * m + 8, :] = p + 0.5 * q

    return kernel


def last_kernel(flags, ye, yo, mass, coef, roll_ref, f0, f1, f2, early, dots_in, v_in, y_in, v, message):
    first = lanes()[1] == 0
    got = got_from(flags, ye, yo, 1)
    kf = [roll_ref[r] for r in range(8)]
    kb = [roll_ref[8 + r] for r in range(8)]
    squares = [jnp.where(first, float(DMAT[a, 0]) ** 2, float(DMAT[a, 7]) ** 2) for a in range(8)]

    def outer(ref, lead, plane):
        return jnp.where(first, ref[plane_at(1, lead, 0, plane)], ref[plane_at(1, lead, 7, plane)])

    sums = [dots_in[8 * m : 8 * m + 8, :] for m in range(4)]
    for t in range(2):
        for i in range(8):
            for j in range(8):
                index = plane_at(0, (t,), i, j)
                v[index] = v_in[index]
        face = outer_faces(first, got, 16, SCALE, t)
        add_values(first, 1, face, t, v)
        flux = along(face, FWD)
        inner = along([outer(coef, (0,), p) * flux[p] for p in range(8)], BWD)
        part = [None] * 4
        for p in range(8):
            x = face[p]
            normal = outer(mass, (), p)
            for a in range(8):
                normal = normal + squares[a] * coef[plane_at(1, (1,), a, p)]
            own = normal * x + inner[p] + along_k(outer(coef, (2,), p) * along_k(x, kf), kb)
            own = own + 2.0 * outer(y_in, (t,), p)
            for m, value in enumerate([ref[t, 8 * p : 8 * p + 8, :] for ref in (f0, f1, f2)] + [own]):
                part[m] = x * value if part[m] is None else part[m] + x * value
        sums = [s + (1.0 if t == 0 else 0.5) * q for s, q in zip(sums, part)]
    row_of = lax.broadcasted_iota(jnp.int32, (16, 128), 0)
    lane_of = lax.broadcasted_iota(jnp.int32, (16, 128), 1)
    table = jnp.zeros((16, 128), f32)
    every = [early[8 * m : 8 * m + 8, :] for m in range(7)] + sums
    for m, value in enumerate(every):
        table = jnp.where(row_of == m, jnp.sum(value, axis=0, keepdims=True), table)
    column = jnp.sum(table, axis=1, keepdims=True)
    line = jnp.sum(jnp.where(row_of == lane_of, column, 0.0), axis=0, keepdims=True)
    message[...] = jnp.broadcast_to(line, message.shape)


def edge_kernel(step):
    def kernel(flags, ye, yo, mass, coef, roll_ref, y_in, send_e, send_o, e):
        y0 = lanes()[1] == 0
        got = got_from(flags, ye, yo, 1)
        for t in range(2):
            face = outer_faces(y0, got, 16, SCALE if step else 1.0, t)
            for p, out in face_operator(y0, 1, face, (0, 7), mass, coef, roll_ref):
                for a in range(8):
                    at = slice(8 * a, 8 * a + 8)
                    e[t, p // 7, at, :] = y_in[t, p, at, :] + out[a]
        send_edges(e, flags, (send_e, send_o))

    return kernel


def y_kernel(step):
    n_dots = step + 1 + (step == 0)

    def kernel(flags, xe, xo, ye, yo, mass, coef, roll_ref, *refs):
        older = refs[:step]
        v_in, y_in, v, y, y_low, y_high, dots, outer_y = refs[step:]
        X, Y, Z, lane = lanes()
        scale = SCALE if step else 1.0
        for t in range(2):
            for i in range(8):
                for j in range(8):
                    index = plane_at(0, (t,), i, j)
                    v[index] = v_in[index]
        got_x, got_y = got_from(flags, xe, xo, 0), got_from(flags, ye, yo, 1)
        for t in range(2):
            add_values(X == 0, 0, outer_faces(X == 0, got_x, 32, scale, t), t, v)
            face = outer_faces(Y == 0, got_y, 16, scale, t)
            add_values(Y == 0, 1, face, t, v)
            for p, out in face_operator(Y == 0, 1, face, range(8), mass, coef, roll_ref):
                for a in range(8):
                    index = plane_at(1, (t,), a, p)
                    y[index] = y_in[index] + out[a]
        if step == 0:
            sub = lax.broadcasted_iota(jnp.int32, (8, 128), 0)
            wz = jnp.where(((Z > 0) & (sub == 0)) | ((Z < 15) & (sub == 7)), 0.5, 1.0)
            wy_low = jnp.where((Y == 1) | is_set(flags, 4), 0.5, 1.0)
            wy_high = jnp.where((Y == 0) | is_set(flags, 5), 0.5, 1.0)
            wx_low = jnp.where((X == 1) | is_set(flags, 2), 0.5, 1.0)
            wx_high = jnp.where((X == 0) | is_set(flags, 3), 0.5, 1.0)

        def products(t):
            def body(i, sums):
                sums = list(sums)
                squares = []
                for j in range(8):
                    at = slice(8 * j, 8 * j + 8)
                    total = y[t, i, at, :]
                    own = v[t, i, at, :]
                    for m in range(step):
                        sums[m] = sums[m] + older[m][t, i, at, :] * total
                    sums[step] = sums[step] + own * total
                    squares.append(own * own)
                if step == 0:
                    index = jnp.full((8, 128), i, jnp.int32)
                    wx = wz * jnp.where(index == 0, wx_low, jnp.where(index == 7, wx_high, 1.0))
                    square = squares[1]
                    for j in range(2, 7):
                        square = square + squares[j]
                    square = square + wy_low * squares[0] + wy_high * squares[7]
                    sums[1] = sums[1] + wx * square
                return tuple(sums)

            return lax.fori_loop(0, 8, body, tuple(jnp.zeros((8, 128), f32) for _ in range(n_dots)))

        sums = [p + 0.5 * q for p, q in zip(products(0), products(1))]
        for m in range(n_dots):
            dots[8 * m : 8 * m + 8, :] = sums[m]
        for t in range(2):
            for i in range(8):
                outer_y[t, 8 * i : 8 * i + 8, :] = jnp.where(Y == 0, y[t, i, 0:8, :], y[t, i, 56:64, :])
        assemble_local(y, flags, y_low, y_high)

    return kernel


def store(flags, v, stored):
    pick = pick_table(flags).astype(jnp.bfloat16)
    for t in range(2):
        table = jnp.concatenate([pick if t == 0 else pick[0:64, :]] * 3, axis=1)
        x = jnp.concatenate(thirds(v[t].reshape(512, 128)), axis=1)
        res = lax.dot_general(table, x, (((1,), (1,)), ((), ())), preferred_element_type=f32)
        if t == 0:
            stored[0] = res[0:64, :]
            stored[1] = res[64:128, :]
        else:
            stored[2] = res


def finish_kernel(flags, got, stored0, stored1, stored2, v, out_hbm, stored3, out, sems):
    store(flags, v, stored3)
    stored = (stored0, stored1, stored2, stored3)
    total = jnp.sum(got[...], axis=0, keepdims=True)
    lane = lax.broadcasted_iota(jnp.int32, (1, 128), 1)

    def entry(m):
        return jnp.sum(jnp.where(lane == m, total, 0.0), axis=1, keepdims=True)

    gram = {}
    order = [(0, 0), None, (0, 1), (1, 1), (0, 2), (1, 2), (2, 2), (0, 3), (1, 3), (2, 3), (3, 3)]
    for m, pair in enumerate(order):
        if pair is None:
            square = entry(m)
        else:
            gram[pair] = entry(m)
    right = [square]
    for j in range(3):
        right.append(SCALE * gram[(0, j)] - right[j])
    lower, inverse, reduced = {}, [], []
    for c in range(4):
        pivot = gram[(c, c)]
        value = right[c]
        for m in range(c):
            pivot = pivot - lower[(c, m)] * lower[(c, m)] * inverse[m]
            value = value - lower[(c, m)] * reduced[m] * inverse[m]
        good = pivot > 1e-6 * gram[(c, c)]
        inverse.append(jnp.where(good, 1.0 / jnp.where(good, pivot, 1.0), 0.0))
        reduced.append(value)
        for r in range(c + 1, 4):
            acc = gram[(c, r)]
            for m in range(c):
                acc = acc - lower[(r, m)] * lower[(c, m)] * inverse[m]
            lower[(r, c)] = acc
    weight = [None] * 4
    for c in reversed(range(4)):
        acc = reduced[c]
        for r in range(c + 1, 4):
            acc = acc - lower[(r, c)] * weight[r]
        weight[c] = acc * inverse[c]
    copies = []
    for n in range(3):
        for half in range(2):
            at = slice(32 * half, 32 * half + 32)
            x = weight[0] * stored[0][n, at, :]
            for c in range(1, 4):
                x = x + weight[c] * stored[c][n, at, :]
            out[n, at, :] = x
            copies.append(pltpu.make_async_copy(out.at[n, pl.ds(32 * half, 32)], out_hbm.at[n, pl.ds(32 * half, 32)], sems.at[2 * n + half]))
            copies[-1].start()
    for copy in copies:
        copy.wait()


def swaps(sx, sy, along_x, odd):
    pairs = []
    for g in range(sx):
        for h in range(sy):
            at, count = (g, sx) if along_x else (h, sy)
            other = at + 1 if at % 2 == odd else at - 1
            if along_x:
                to = (other, h) if 0 <= other < count else (g, h ^ 1)
            else:
                to = (g, other) if 0 <= other < count else (g ^ 1, h)
            pairs.append((g * sy + h, to[0] * sy + to[1]))
    return pairs


def solution(mesh):
    vmem = pl.BlockSpec(memory_space=pltpu.VMEM)
    params = pltpu.CompilerParams(vmem_limit_bytes=40 * 1024 * 1024)
    sx, sy = mesh.shape["gx"], mesh.shape["gy"]

    def shape(*dims):
        return jax.ShapeDtypeStruct(dims, f32)

    field, face = shape(2, 8, 64, 128), shape(64, 128)

    anywhere = pl.BlockSpec(memory_space=pltpu.HBM)

    def call(kernel, outs, ins, scratch=(), name=None, cost=None):
        return pl.pallas_call(
            kernel,
            out_shape=outs,
            in_specs=ins if isinstance(ins, list) else [vmem] * ins,
            out_specs=[vmem] * len(outs),
            scratch_shapes=scratch,
            compiler_params=params,
            cost_estimate=pl.CostEstimate(flops=0, transcendentals=0, bytes_accessed=cost) if cost else None,
            name=name,
        )

    def held(x):
        return pltpu.with_memory_space_constraint(x, pltpu.HBM)

    def local(adjoint_field, velocity, diffusivity, jacobian, element_slot):
        big = pltpu.VMEM((2, 8, 64, 128), f32)
        flags, a, v, mass, table, xe, xo = call(
            make_setup(sx, sy),
            [jax.ShapeDtypeStruct((16, 128), jnp.int32), field, field, shape(8, 64, 128), shape(16, 8, 128), face, face],
            [anywhere] * 4,
            [
                pltpu.VMEM((2, 2, 64, 128), f32),
                pltpu.VMEM((1, 64), jnp.int32),
                pltpu.VMEM((3, 64, 512), f32),
                pltpu.VMEM((3, 64, 512), jnp.bfloat16),
                pltpu.VMEM((64, 512), f32),
                pltpu.SemaphoreType.DMA((11,)),
            ],
            "setup",
        )(held(element_slot.reshape(1, 64)), held(adjoint_field.reshape(3, 64, 512)), held(velocity.reshape(3, 64, 512)), held(jacobian.reshape(64, 512)))
        mass, u, yl, yh = call(
            source_kernel, [shape(8, 64, 128), field, face, face], 5, [big, big, pltpu.VMEM((8, 64, 128), f32)], "source", cost=8 << 20
        )(flags, a, v, mass, table)
        (coef,) = call(coef_kernel, [shape(3, 8, 64, 128)], 2, name="coef", cost=3 << 20)(flags, diffusivity.reshape(3, 64, 512))
        vs, parts, stored, faces = [], [], [], []
        for step in range(STEPS):
            xe = lax.ppermute(xe, ("gx", "gy"), swaps(sx, sy, True, 0))
            xo = lax.ppermute(xo, ("gx", "gy"), swaps(sx, sy, True, 1))
            shared = [mass, coef, table]
            if step == 0:
                v, y = call(main_kernel(step), [field, field], 4, name="main0", cost=8 << 20)(u, *shared)
            else:
                v, y, moved = call(main_kernel(step), [field, field, shape(3, 64, 512)], 6, name=f"main{step}", cost=8 << 20)(flags, u, vs[-1], *shared)
                stored.append(moved)
            ye, yo = call(mid_kernel, [face, face], [vmem] * 5 + [anywhere], name="mid")(flags, xe, xo, yl, yh, u)
            ye = lax.ppermute(ye, ("gx", "gy"), swaps(sx, sy, False, 0))
            yo = lax.ppermute(yo, ("gx", "gy"), swaps(sx, sy, False, 1))
            if step < STEPS - 1:
                (y,) = call(x_kernel(step), [field], 7, name=f"xpart{step}", cost=8 << 20)(flags, xe, xo, *shared, y)
                args = [flags, xe, xo, ye, yo] + shared + vs
                xe, xo = call(edge_kernel(step), [face, face], 7, [pltpu.VMEM((2, 2, 64, 128), f32)], f"edge{step}")(flags, ye, yo, *shared, y)
                n_dots = step + 1 + (step == 0)
                v, u, yl, yh, dots, outer_y = call(
                    y_kernel(step),
                    [field, field, face, face, shape(8 * n_dots, 128), shape(2, 64, 128)],
                    len(args) + 2,
                    name=f"ypart{step}",
                    cost=8 << 20,
                )(*args, v, y)
                vs.append(v)
                parts.append(dots)
                faces.append(outer_y)
            else:
                early = jnp.concatenate(parts, axis=0)
                v, dots, y = call(x_kernel(step), [field, shape(32, 128), field], 11, name=f"xpart{step}", cost=8 << 20)(flags, xe, xo, *shared, y, v, *vs)
                v, message = call(last_kernel, [field, shape(sx * sy, 128)], 13, name="last")(flags, ye, yo, *shared, *faces, early, dots, v, y)
        got = lax.all_to_all(message.reshape(sx * sy, 1, 128), ("gx", "gy"), 0, 0).reshape(sx * sy, 128)
        (out,) = pl.pallas_call(
            finish_kernel,
            out_shape=[shape(3, 64, 512)],
            in_specs=[vmem] * 6,
            out_specs=[anywhere],
            scratch_shapes=[pltpu.VMEM((3, 64, 512), f32), pltpu.VMEM((3, 64, 512), f32), pltpu.SemaphoreType.DMA((6,))],
            compiler_params=params,
            name="finish",
        )(flags, got, *stored, v)
        return out.reshape(3, 1, 1, 64, 512)

    in_specs = (
        P(None, "gx", "gy", None, None),
        P(None, "gx", "gy", None, None),
        P(None, "gx", "gy", None, None),
        P("gx", "gy", None, None),
        P("gx", "gy", None),
    )
    return jax.shard_map(local, mesh=mesh, in_specs=in_specs, out_specs=P(None, "gx", "gy", None, None), check_vma=False)
```
